32 devices in a mesh: dp: 4 (over z), seq: 8 (over y, x, core).
Axes of the slice: x: 2, y: 2, z: 4, core: 2. Of those that a mesh axis runs over, the one named last changes fastest.
Arguments:
- tiles: bfloat16 [4, 1536, 768], P('dp', 'seq'), may hold values from -40 to 40
- cotangent: bfloat16 [4, 1536, 768], P('dp', 'seq'), may hold values from -0.078125 to 0.078125
- segment_of: int32 [4, 1536, 1], P('dp', 'seq'), may hold values from 0 to 15; in each aligned block of 192 rows (0 to 191, 192 to 383, ..., all dimensions but the last counted through in order) at most 20 rows name the same one
- tissue_count: int32 [4], P('dp'), may hold values from 768 to 1536
- w_query: bfloat16 [768, 768], P('seq'), may hold values from -0.21875 to 0.21875
- w_key: bfloat16 [768, 768], P('seq'), may hold values from -0.21875 to 0.21875
- w_value: bfloat16 [768, 768], P('seq'), may hold values from -0.21875 to 0.21875
- w_out: bfloat16 [768, 768], P('seq'), may hold values from -2.390625 to 2.390625
Outputs:
- layer_out: bfloat16 [4, 1536, 768], P('dp', 'seq')
- grad_value: float32 [768, 768], P('seq')
The draws below stay inside these ranges and needn't reach their ends.
Inputs may be any that keep to these rules, and one draw needn't show every extreme that they name: `segment_of`: within one slide, the 192 tiles of one block name one group at most 20 times; some group is named exactly 20 times.
All inputs are finite; a program needn't handle non-finite values.
Results may differ from the reference program's by a relative error of at most 0.014.
Values may be sent and summed in bfloat16 or wider, within the bound.
No kernel may reach another device: no remote copies, remote signals or barrier semaphores. Data moves between devices by JAX's collectives and lax.ppermute only.
A program may use at most 64 MiB of HBM per device.

```python
import math
import jax
import jax.numpy as jnp
import numpy as np
from jax import lax

D = 768
HEADS = 12
HEAD_DIM = 64
TOK_DEV = 192
SLIDES = 4
TILES = 1536
SEGMENTS = 16
SEG_CAP = 20
SEG_SLOTS = 160
N_SEQ = 8


def draw_tiles(key, part):
    first_key = jax.random.fold_in(jax.random.fold_in(key, 17), 0)
    shape = (SLIDES, TILES, D)
    values = jnp.clip(jax.random.normal(first_key, shape, jnp.float32), -6.0, 6.0)
    return values.astype(jnp.bfloat16)


def set_ends(entries, rng, low, high):
    shape = entries.shape
    place = [jax.random.randint(jax.random.fold_in(rng, axis), (), 0, shape[axis]) for axis in range(len(shape))]
    entries = entries.at[tuple(place)].set(low)
    longest = shape.index(max(shape))
    place[longest] = (place[longest] + 1) % shape[longest]
    return entries.at[tuple(place)].set(high)


def levels(rng, extent, pieces, least, largest):
    gain, own = 1.0, jax.random.fold_in(rng, 6)
    for dim, shards_of in pieces:
        steps = jnp.exp(jax.random.uniform(jax.random.fold_in(own, dim), (shards_of,), jnp.float32, least / len(pieces), largest / len(pieces)))
        gain = gain * jnp.repeat(steps, extent[dim] // shards_of).reshape([-1 if axis == dim else 1 for axis in range(len(extent))])
    return gain


def assign_block(rng, own, number, rows, count, top, bound, slope):
    ranking = jax.random.permutation(rng, count)
    crowded, usual = shares(count, rows * top, bound, slope, True), shares(count, rows * top, bound, slope, False)
    places = jnp.arange(count)

    def named(tallies, turn):
        used = int((tallies > 0).sum())
        fixed = max(1, used // 4)
        shifted = fixed + (places - fixed + turn * (used - fixed)) % max(1, count - fixed)
        return jnp.zeros((count,), jnp.int32).at[ranking[jnp.where(places < fixed, places, shifted)]].set(jnp.asarray(tallies, jnp.int32))

    tallies = jnp.where(number % 4 == 0, named(crowded, number // 4), named(usual, number - number // 4 - 1))
    mixed = jax.random.permutation(jax.random.fold_in(own, 3), count)
    donor, receiver = mixed[0:count // 2 * 2:2], mixed[1:count // 2 * 2:2]
    slack = jnp.minimum(tallies[donor] - 1, bound - tallies[receiver]) // 2
    slack = jnp.where((donor == ranking[0]) | (receiver == ranking[0]) | (tallies[receiver] == 0), 0, jnp.maximum(slack, 0))
    shifted = jax.random.randint(jax.random.fold_in(own, 4), (count // 2,), 0, 1 << 20) % (slack + 1)
    tallies = tallies.at[donor].add(-shifted).at[receiver].add(shifted)
    items = jnp.searchsorted(jnp.cumsum(tallies), jnp.arange(rows * top), side="right").astype(jnp.int32)
    listing = items.reshape(top, rows).T
    listing = listing[jax.random.permutation(jax.random.fold_in(own, 1), rows)]
    turn = jax.random.randint(jax.random.fold_in(own, 2), (rows, 1), 0, top)
    return jnp.take_along_axis(listing, (jnp.arange(top)[None, :] + turn) % top, axis=1)


def shares(number_of, total, bound, skew, full):
    weights = [(1 << 20) // math.isqrt(rank ** skew) + 1 for rank in range(1, number_of + 1)]
    largest = bound if full else min(bound, max(-(-total // number_of), total * weights[0] // sum(weights)))
    least = 1 if total - largest >= number_of - 1 else 0
    holding, surplus = [largest] + [least] * (number_of - 1), total - largest - least * (number_of - 1)
    while surplus > 0:
        free = [i for i in range(1, number_of) if holding[i] < largest] or [i for i in range(1, number_of) if holding[i] < bound]
        whole, remaining = sum([weights[i] for i in free]), surplus
        for i in free:
            more = min(bound - holding[i], max(1, remaining * weights[i] // whole), surplus)
            holding[i] = holding[i] + more
            surplus = surplus - more
    return np.array(holding)


def scatter_about(rng, shape, deviation, most, pieces=(), kind=jnp.bfloat16):
    values = deviation * jax.random.normal(rng, shape, jnp.float32)
    if pieces:
        values = values * levels(rng, shape, pieces, -0.22, 0.18)
    return jnp.clip(values, -most, most).astype(kind)


def setup_inputs(seed: int = 0) -> dict:
    arg_keys = jax.random.split(jax.random.key(seed), 9)
    tiles = draw_tiles(jax.random.fold_in(arg_keys[8], 71), 0)
    cotangent = scatter_about(arg_keys[1], (SLIDES, TILES, D), (SLIDES * TILES) ** -0.5, 0.078125, ((0, 4), (1, 8)))
    segment_of_keys = jax.random.split(jax.random.fold_in(arg_keys[2], 1), SLIDES * TILES // TOK_DEV)
    segment_of_turns = jax.random.permutation(jax.random.fold_in(arg_keys[2], 3), SLIDES * TILES // TOK_DEV)
    segment_of = jax.vmap(lambda own, number: assign_block(jax.random.fold_in(arg_keys[2], 2), own, number, TOK_DEV, SEGMENTS, 1, SEG_CAP, 2))(segment_of_keys, segment_of_turns).reshape((SLIDES, TILES, 1))
    tissue_count = set_ends(jax.random.randint(arg_keys[3], (SLIDES,), TILES // 2, TILES + 1), jax.random.fold_in(arg_keys[3], 1), TILES // 2, TILES).astype(jnp.int32)
    w_query = scatter_about(arg_keys[4], (D, D), D ** -0.5, 0.21875, ((0, 8),))
    w_key = scatter_about(arg_keys[5], (D, D), D ** -0.5, 0.21875, ((0, 8),))
    w_value = scatter_about(arg_keys[6], (D, D), D ** -0.5, 0.21875, ((0, 8),))
    w_out = scatter_about(arg_keys[7], (D, D), 0.4, 2.390625, ((0, 8),))
    return dict(tiles=tiles, cotangent=cotangent, segment_of=segment_of, tissue_count=tissue_count, w_query=w_query, w_key=w_key, w_value=w_value, w_out=w_out)


NEG_BIG = -1.0e30


def pad_one(block):
    return jnp.concatenate([block, jnp.zeros((1,) + block.shape[1:], block.dtype)], axis=0)


def reference(tiles, cotangent, segment_of, tissue_count, w_query, w_key, w_value, w_out):
    scale = HEAD_DIM ** -0.5
    eye_local = jnp.eye(TOK_DEV, dtype=bool)
    eye_slots = jnp.eye(SEG_SLOTS, dtype=bool)

    def one_slide(item):
        inputs, cot_rows, segment_rows, count = item
        position = jnp.arange(TILES, dtype=jnp.int32)
        inside = position < count
        masked_cot = cot_rows * inside[:, None].astype(jnp.bfloat16)
        query_rows = jnp.dot(inputs, w_query, preferred_element_type=jnp.float32).astype(jnp.bfloat16)
        key_rows = jnp.dot(inputs, w_key, preferred_element_type=jnp.float32).astype(jnp.bfloat16)
        value_rows = jnp.dot(inputs, w_value, preferred_element_type=jnp.float32).astype(jnp.bfloat16)
        dout_rows = jnp.dot(masked_cot, w_out.T, preferred_element_type=jnp.float32).astype(jnp.bfloat16)

        def split_blocks(block):
            return block.reshape(N_SEQ, TOK_DEV, HEADS, HEAD_DIM)

        inside_blocks = inside.reshape(N_SEQ, TOK_DEV)

        def local_scores(query_block, key_block, inside_block):
            scores = jnp.einsum("qhc,khc->hqk", query_block.astype(jnp.float32), key_block.astype(jnp.float32)) * scale
            visible = inside_block[None, :] | eye_local
            return jnp.where(visible[None], scores, NEG_BIG)

        def local_stats(part):
            scores = local_scores(part[0], part[1], part[2])
            top = jnp.max(scores, axis=2)
            total = jnp.sum(jnp.exp(scores - top[:, :, None]), axis=2)
            return top, total

        local_max, local_sum = lax.map(local_stats, (split_blocks(query_rows), split_blocks(key_rows), inside_blocks))
        near_max = local_max.transpose(0, 2, 1).reshape(TILES, HEADS)
        near_sum = local_sum.transpose(0, 2, 1).reshape(TILES, HEADS)

        block_of = position // TOK_DEV
        member = (segment_rows.reshape(N_SEQ, TOK_DEV)[:, :, None] == jnp.arange(SEGMENTS, dtype=jnp.int32)[None, None, :]).astype(jnp.int32)
        rank = (jnp.sum(jnp.cumsum(member, axis=1) * member, axis=2) - 1).reshape(TILES).astype(jnp.int32)
        slot_index = (segment_rows * SEG_SLOTS + block_of * SEG_CAP + rank).astype(jnp.int32)
        source_row = jnp.full((SEGMENTS * SEG_SLOTS,), TILES, jnp.int32).at[slot_index].set(position)
        source_row = source_row.reshape(SEGMENTS, SEG_SLOTS)
        state_rows = jnp.where(inside, 2, 1).astype(jnp.int32)
        tables = (pad_one(query_rows), pad_one(key_rows), pad_one(value_rows), pad_one(dout_rows),
                  pad_one(near_max), pad_one(near_sum), pad_one(state_rows))

        def one_segment(members):
            picked = [jnp.take(table, members, axis=0) for table in tables]
            query_seg = picked[0].reshape(SEG_SLOTS, HEADS, HEAD_DIM).astype(jnp.float32)
            key_seg = picked[1].reshape(SEG_SLOTS, HEADS, HEAD_DIM).astype(jnp.float32)
            value_seg = picked[2].reshape(SEG_SLOTS, HEADS, HEAD_DIM).astype(jnp.float32)
            dout_seg = picked[3].reshape(SEG_SLOTS, HEADS, HEAD_DIM).astype(jnp.float32)
            seg_near_max = picked[4].T
            seg_near_sum = picked[5].T
            seen = (picked[6] == 2)[None, :] | eye_slots
            scores = jnp.einsum("qhc,khc->hqk", query_seg, key_seg) * scale
            scores = jnp.where(seen[None], scores, NEG_BIG)
            far_max = jnp.max(scores, axis=2)
            far_sum = jnp.sum(jnp.exp(scores - far_max[:, :, None]), axis=2)
            top = jnp.maximum(far_max, seg_near_max)
            log_total = top + jnp.log(seg_near_sum * jnp.exp(seg_near_max - top) + far_sum * jnp.exp(far_max - top))
            weights = jnp.exp(scores - log_total[:, :, None]).astype(jnp.bfloat16).astype(jnp.float32)
            far_out = jnp.einsum("hqk,khc->qhc", weights, value_seg).astype(jnp.bfloat16).reshape(SEG_SLOTS, D)
            far_grad = jnp.einsum("hqk,qhc->khc", weights, dout_seg).astype(jnp.bfloat16).reshape(SEG_SLOTS, D)
            return far_out, far_grad, log_total.T

        far_out, far_grad, log_total = lax.map(one_segment, source_row)
        far_out = jnp.take(far_out.reshape(SEGMENTS * SEG_SLOTS, D), slot_index, axis=0)
        far_grad = jnp.take(far_grad.reshape(SEGMENTS * SEG_SLOTS, D), slot_index, axis=0)
        lse_rows = jnp.take(log_total.reshape(SEGMENTS * SEG_SLOTS, HEADS), slot_index, axis=0)

        def local_apply(part):
            query_block, key_block, value_block, dout_block, inside_block, lse_block = part
            scores = local_scores(query_block, key_block, inside_block)
            weights = jnp.exp(scores - lse_block.T[:, :, None]).astype(jnp.bfloat16).astype(jnp.float32)
            near_out = jnp.einsum("hqk,khc->qhc", weights, value_block.astype(jnp.float32))
            near_grad = jnp.einsum("hqk,qhc->khc", weights, dout_block.astype(jnp.float32))
            return near_out.reshape(TOK_DEV, D), near_grad.reshape(TOK_DEV, D)

        near_out, near_grad = lax.map(local_apply, (split_blocks(query_rows), split_blocks(key_rows), split_blocks(value_rows),
                                                    split_blocks(dout_rows), inside_blocks, lse_rows.reshape(N_SEQ, TOK_DEV, HEADS)))
        attention = (near_out.reshape(TILES, D) + far_out.astype(jnp.float32)).astype(jnp.bfloat16)
        layer_rows = jnp.dot(attention, w_out, preferred_element_type=jnp.float32).astype(jnp.bfloat16)
        near_grad = near_grad.reshape(TILES, D).astype(jnp.bfloat16)
        grad_term = jnp.dot(inputs.T, near_grad, preferred_element_type=jnp.float32)
        grad_term = grad_term + jnp.dot(inputs.T, far_grad, preferred_element_type=jnp.float32)
        return layer_rows, grad_term

    layer_out, grad_terms = lax.map(one_slide, (tiles, cotangent, segment_of[:, :, 0], tissue_count))
    return layer_out, jnp.sum(grad_terms, axis=0)
```

```python
import functools
import math

import jax
import jax.numpy as jnp
from jax import lax
from jax.experimental import pallas as pl
from jax.experimental.pallas import tpu as pltpu
from jax.sharding import PartitionSpec as P

HEADS = 12
NEG_BIG = -1e30
LOG2E = 1.4426950408889634


VM = pl.BlockSpec(memory_space=pltpu.VMEM)
SM = pl.BlockSpec(memory_space=pltpu.SMEM)


def dot_last(a, b):
    return lax.dot_general(a, b, (((1,), (1,)), ((), ())), preferred_element_type=jnp.float32)


def dot(a, b):
    return lax.dot_general(a, b, (((1,), (0,)), ((), ())), preferred_element_type=jnp.float32)


def pack_kernel(hg, tg, wr, cw, wq, wk, wv, seg, *outs):
    group = lax.axis_index("seq") // tg
    for k in range(hg):
        for part in range(hg):

            @pl.when((group ^ k) == part)
            def _():
                cols = slice(part * cw, (part + 1) * cw)
                outs[k][0, :wr] = wq[:, cols]
                outs[k][1, :wr] = wk[:, cols]
                outs[k][2, :wr] = wv[:, cols]

        for i in range(3):
            outs[k][i, wr:] = jnp.broadcast_to(seg[...], (8, cw)).astype(jnp.bfloat16)


def dout_kernel(hg, tg, cw, count, cot, wout, *outs):
    own = lax.axis_index("seq")
    group = own // tg
    rows = cot.shape[0]
    position = own * rows + lax.broadcasted_iota(jnp.int32, cot.shape, 0)
    masked = jnp.where(position < count[0], cot[...].astype(jnp.float32), 0.0).astype(jnp.bfloat16)
    for k in range(hg):
        start = pl.multiple_of((group ^ k) * cw, cw)
        outs[k][...] = dot_last(masked, wout[pl.ds(start, cw), :]).astype(jnp.bfloat16)


def proj_kernel(hg, tg, cw, wout, *refs):
    group = lax.axis_index("seq") // tg
    out = refs[hg]
    total = None
    for k in range(hg):
        start = pl.multiple_of((group ^ k) * cw, cw)
        term = dot(refs[k][...], wout[pl.ds(start, cw), :])
        total = term if total is None else total + term
    out[0] = total.astype(jnp.bfloat16)


def main_kernel(hg, tg, rows, width, cw, wr, head_dim, by_dp, *refs):
    n = hg * tg
    weights, seg_row, seg_col, count = refs[:4]
    tiles = refs[4 : 4 + n]
    douts = refs[4 + n : 4 + n + hg]
    o_out = refs[4 + n + hg : 4 + n + 2 * hg]
    g_out = refs[4 + n + 2 * hg : 4 + n + 2 * hg + tg]
    q_s, k_s, v_s, t_s, bias_s, p_s, d_s, o_s, gt_s, grad_s = refs[4 + n + 2 * hg + tg :]
    own = lax.axis_index("seq")
    group = own // tg
    member = own % tg
    keys = n * rows
    heads = cw // head_dim
    for tau in range(tg):
        for k in range(hg):
            r = tau * hg + k
            block = tiles[r][...]
            at = slice(r * rows, (r + 1) * rows)
            t_s[at, :] = block
            if tau == 0:
                q_s[at, :] = dot(block, weights[0]).astype(jnp.bfloat16)
                d_s[at, :] = douts[k][...]
            k_s[at, :] = dot(block, weights[1]).astype(jnp.bfloat16)
            v_s[at, :] = dot(block, weights[2]).astype(jnp.bfloat16)
    gt_s[...] = jnp.zeros_like(gt_s)
    scale = head_dim ** (-0.5) * LOG2E
    lane_head = lax.broadcasted_iota(jnp.int32, (rows, cw), 1) // head_dim
    label = seg_row[...]

    def chunk(k, carry):
        start = pl.multiple_of(k * rows, rows)
        column = lax.broadcasted_iota(jnp.int32, (1, keys), 1)
        in_block = (column >= start) & (column < start + rows) & (label >= 0)
        same_value = jnp.where(in_block, 1.0, 0.0)
        other_value = jnp.where(in_block, 0.0, NEG_BIG)
        segment = seg_col[pl.ds(start, rows), :]
        bias = jnp.where(segment == label, same_value, other_value)
        row_at = start + lax.broadcasted_iota(jnp.int32, (rows, keys), 0)
        col_at = lax.broadcasted_iota(jnp.int32, (rows, keys), 1)
        bias_s[...] = jnp.where(row_at == col_at, 1.0, bias)
        q = q_s[pl.ds(start, rows), :]
        scaled = jnp.zeros((rows, cw), jnp.float32)
        for h in range(heads):
            qh = jnp.where(lane_head == h, q, jnp.zeros_like(q))
            s = dot_last(qh, k_s[...]) * scale + bias_s[...]
            top = jnp.max(s, axis=1, keepdims=True)
            p = jnp.exp2(s - top)
            total = jnp.sum(p, axis=1, keepdims=True)
            p_s[h] = p.astype(jnp.bfloat16)
            inverse = 1.0 / total
            scaled = jnp.where(lane_head == h, inverse, scaled)
        acc = jnp.zeros((rows, cw), jnp.float32)
        for h in range(heads):
            acc = jnp.where(lane_head == h, dot(p_s[h], v_s[...]), acc)
        o_s[pl.ds(start, rows), :] = (acc * scaled).astype(jnp.bfloat16)
        d = (d_s[pl.ds(start, rows), :].astype(jnp.float32) * scaled).T.astype(jnp.bfloat16)
        for h in range(heads):
            at = slice(h * head_dim, (h + 1) * head_dim)
            gt_s[at, :] += dot(d[at, :], p_s[h])
        return carry

    lax.fori_loop(0, hg, chunk, 0)
    for k in range(hg):
        o_out[k][...] = o_s[k * rows : (k + 1) * rows, :]
    grad_s[...] = dot(gt_s[...].astype(jnp.bfloat16), t_s[...]).T
    first = lax.axis_index("dp") if by_dp else 0
    for tau in range(tg):
        for m in range(hg):
            to = ((group ^ m ^ first) * tg + (member ^ tau)) * wr
            to = pl.multiple_of(to, wr)
            g_out[tau][m] = grad_s[pl.ds(to, wr), :].astype(jnp.bfloat16)


def local(tiles, cotangent, segment_of, tissue_count, w_query, w_key, w_value, w_out):
    rows, width = tiles.shape[1:]
    wr = w_query.shape[0]
    n = lax.axis_size("seq")
    dp = lax.axis_size("dp")
    hg = math.gcd(HEADS, n)
    tg = n // hg
    cw = width // hg
    head_dim = width // HEADS
    by_dp = dp == hg
    own = lax.axis_index("seq")
    group = own // tg
    bf16 = jnp.bfloat16

    def hop(x, step):
        return lax.ppermute(x, "seq", [(s, s ^ step) for s in range(n)])

    def over_groups(pieces):
        return [pieces[0]] + [hop(pieces[k], k * tg) for k in range(1, hg)]

    def over_members(pieces):
        return [pieces] + [[hop(x, tau) for x in pieces] for tau in range(1, tg)]

    def absolute(table):
        flat = [table[r % tg][r // tg] for r in range(n)]
        stacked = jnp.stack(flat)
        return jnp.concatenate(
            [lax.dynamic_slice_in_dim(stacked, own ^ s, 1, 0) for s in range(n)], axis=0
        )

    seg_line = segment_of.reshape(1, rows)
    packed = pl.pallas_call(
        functools.partial(pack_kernel, hg, tg, wr, cw),
        out_shape=[jax.ShapeDtypeStruct((3, wr + 8, cw), bf16)] * hg,
        in_specs=[VM] * 4,
        out_specs=[VM] * hg,
    )(w_query, w_key, w_value, seg_line)
    wout_table = over_members(over_groups([w_out] * hg))
    weight_table = over_members(over_groups(packed))
    tile_table = over_members(over_groups([tiles[0]] * hg))

    wout = absolute(wout_table).reshape(width, width)
    douts = pl.pallas_call(
        functools.partial(dout_kernel, hg, tg, cw),
        out_shape=[jax.ShapeDtypeStruct((rows, cw), bf16)] * hg,
        in_specs=[SM, VM, VM],
        out_specs=[VM] * hg,
    )(tissue_count, cotangent[0], wout)
    douts = over_groups(douts)

    stacked = absolute(weight_table)
    weights = stacked[:, :, :wr].transpose(1, 0, 2, 3).reshape(3, width, cw)
    segs = jnp.concatenate(
        [weight_table[tau][k][0, wr : wr + 1] for tau in range(tg) for k in range(hg)], axis=0
    ).astype(jnp.int32)
    blocks = jnp.array([[k * tg + tau] for tau in range(tg) for k in range(hg)], jnp.int32) ^ own
    position = blocks * rows + jnp.arange(rows, dtype=jnp.int32)[None, :]
    labels = jnp.where(position < tissue_count[0], segs, -1).reshape(1, n * rows)
    seg_col = segs[:hg].reshape(hg * rows, 1)

    keys = n * rows
    results = pl.pallas_call(
        functools.partial(main_kernel, hg, tg, rows, width, cw, wr, head_dim, by_dp),
        out_shape=[jax.ShapeDtypeStruct((rows, cw), bf16)] * hg
        + [jax.ShapeDtypeStruct((hg, wr, cw), bf16)] * tg,
        in_specs=[VM, VM, VM, SM] + [VM] * (n + hg),
        out_specs=[VM] * (hg + tg),
        scratch_shapes=[
            pltpu.VMEM((hg * rows, cw), bf16),
            pltpu.VMEM((keys, cw), bf16),
            pltpu.VMEM((keys, cw), bf16),
            pltpu.VMEM((keys, width), bf16),
            pltpu.VMEM((rows, keys), jnp.float32),
            pltpu.VMEM((cw // head_dim, rows, keys), bf16),
            pltpu.VMEM((hg * rows, cw), bf16),
            pltpu.VMEM((hg * rows, cw), bf16),
            pltpu.VMEM((cw, keys), jnp.float32),
            pltpu.VMEM((width, cw), jnp.float32),
        ],
        compiler_params=pltpu.CompilerParams(vmem_limit_bytes=60 * 1024 * 1024),
    )(
        weights,
        labels,
        seg_col,
        tissue_count,
        *[x for line in tile_table for x in line],
        *douts,
    )
    attention = over_groups(results[:hg])
    grads = results[hg:]
    summed = grads[0].astype(jnp.float32)
    for tau in range(1, tg):
        summed = summed + hop(grads[tau], tau).astype(jnp.float32)
    summed = summed.astype(bf16)

    layer_rows = pl.pallas_call(
        functools.partial(proj_kernel, hg, tg, cw),
        out_shape=jax.ShapeDtypeStruct((1, rows, width), bf16),
        in_specs=[VM] * (1 + hg),
        out_specs=VM,
    )(wout, *attention)

    if by_dp:
        own_dp = lax.axis_index("dp")
        mine = summed[0].astype(jnp.float32)
        for m in range(1, hg):
            got = lax.ppermute(summed[m], "dp", [(z, z ^ m) for z in range(dp)])
            mine = mine + got.astype(jnp.float32)
        mine = mine.astype(bf16)
        parts = []
        for m in range(dp):
            pairs = [
                (z * n + s, (z ^ m) * n + (s ^ (z * tg))) for z in range(dp) for s in range(n)
            ]
            parts.append(lax.ppermute(mine, ("dp", "seq"), pairs))
        index = group ^ own_dp
    else:
        total = lax.psum(summed, "dp")
        parts = over_groups([total[k] for k in range(hg)])
        index = group
    columns = []
    for p in range(hg):
        piece = parts[0]
        for m in range(1, hg):
            piece = jnp.where((index ^ p) == m, parts[m], piece)
        columns.append(piece)
    return (layer_rows, jnp.concatenate(columns, axis=1).astype(jnp.float32))


def solution(mesh):
    placed = (
        P("dp", "seq", None),
        P("dp", "seq", None),
        P("dp", "seq", None),
        P("dp"),
        P("seq", None),
        P("seq", None),
        P("seq", None),
        P("seq", None),
    )
    return jax.shard_map(
        local,
        mesh=mesh,
        in_specs=placed,
        out_specs=(P("dp", "seq", None), P("seq", None)),
        check_vma=False,
    )
```

```python
import functools
import math

import jax
import jax.numpy as jnp
from jax import lax
from jax.experimental import pallas as pl
from jax.experimental.pallas import tpu as pltpu
from jax.sharding import PartitionSpec as P

HEADS = 12
NEG_BIG = -1e30
LOG2E = 1.4426950408889634


VM = pl.BlockSpec(memory_space=pltpu.VMEM)
ANY = pl.BlockSpec(memory_space=pl.ANY)
SM = pl.BlockSpec(memory_space=pltpu.SMEM)


def dot_last(a, b):
    return lax.dot_general(a, b, (((1,), (1,)), ((), ())), preferred_element_type=jnp.float32)


def dot(a, b):
    return lax.dot_general(a, b, (((1,), (0,)), ((), ())), preferred_element_type=jnp.float32)


def pack_kernel(hg, tg, wr, cw, wq, wk, wv, seg, *outs):
    group = lax.axis_index("seq") // tg
    for k in range(hg):
        for part in range(hg):

            @pl.when((group ^ k) == part)
            def _():
                cols = slice(part * cw, (part + 1) * cw)
                outs[k][0, :wr] = wq[:, cols]
                outs[k][1, :wr] = wk[:, cols]
                outs[k][2, :wr] = wv[:, cols]

        for i in range(3):
            outs[k][i, wr:] = jnp.broadcast_to(seg[...], (8, cw)).astype(jnp.bfloat16)


def dout_kernel(hg, tg, wr, cw, count, cot, *refs):
    n = hg * tg
    pieces, outs, wout = refs[:n], refs[n : n + hg], refs[n + hg]
    own = lax.axis_index("seq")
    member = own % tg
    rows = cot.shape[0]
    position = own * rows + lax.broadcasted_iota(jnp.int32, cot.shape, 0)
    masked = jnp.where(position < count[0], cot[...].astype(jnp.float32), 0.0).astype(jnp.bfloat16)
    for k in range(hg):
        for tau in range(tg):
            to = pl.multiple_of((member ^ tau) * wr, wr)
            wout[k, pl.ds(to, wr), :] = pieces[tau * hg + k][...].astype(wout.dtype)
        block = wout[k].astype(jnp.bfloat16)
        outs[k][...] = dot_last(masked, block).astype(jnp.bfloat16)


def proj_kernel(hg, wout, *refs):
    out = refs[hg]
    total = None
    for k in range(hg):
        term = dot(refs[k][...], wout[k].astype(jnp.bfloat16))
        total = term if total is None else total + term
    out[0] = total.astype(jnp.bfloat16)


def main_kernel(hg, tg, parts, rows, wr, head_dim, by_dp, count, *refs):
    n = hg * tg
    refs = list(refs)
    tiles = [[refs.pop(0) for _ in range(parts)] for _ in range(n)]
    packed = [refs.pop(0) for _ in range(n)]
    douts = [refs.pop(0) for _ in range(hg)]
    o_out = [refs.pop(0) for _ in range(hg)]
    g_out = [refs.pop(0) for _ in range(tg)]
    w_s, seg_s, col_s, q_s, k_s, v_s, t_s, bias_s, p_s, d_s, o_s, gt_s, grad_s, sems = refs
    cw = q_s.shape[1]
    own = lax.axis_index("seq")
    group = own // tg
    member = own % tg
    keys = n * rows
    heads = cw // head_dim
    copies = []
    for r in range(n):
        size = rows // parts
        copies.append(
            [
                pltpu.make_async_copy(
                    tiles[r][i],
                    t_s.at[pl.ds(r * rows + i * size, size), :],
                    sems.at[r * parts + i],
                )
                for i in range(parts)
            ]
        )
        for copy in copies[r]:
            copy.start()
    for tau in range(tg):
        for k in range(hg):
            r = tau * hg + k
            source = (group ^ k) * tg + (member ^ tau)
            to = pl.multiple_of(source * wr, wr)
            for i in range(3):
                w_s[i, pl.ds(to, wr), :] = packed[r][i, :wr].astype(w_s.dtype)
            line = packed[r][0, wr : wr + 8, :].astype(jnp.float32)[:1]
            at = source * rows + lax.broadcasted_iota(jnp.int32, (1, rows), 1)
            columns = slice(r * rows, (r + 1) * rows)
            seg_s[0:1, columns] = line
            seg_s[1:2, columns] = jnp.where(at < count[0], line, -1.0)
    for r in range(n):
        for copy in copies[r]:
            copy.wait()
        at = slice(r * rows, (r + 1) * rows)
        block = t_s[at, :]
        if r < hg:
            q_s[at, :] = dot(block, w_s[0].astype(jnp.bfloat16)).astype(jnp.bfloat16)
            d_s[at, :] = douts[r][...]
        k_s[at, :] = dot(block, w_s[1].astype(jnp.bfloat16)).astype(jnp.bfloat16)
        v_s[at, :] = dot(block, w_s[2].astype(jnp.bfloat16)).astype(jnp.bfloat16)
    gt_s[...] = jnp.zeros_like(gt_s)
    scale = head_dim ** (-0.5) * LOG2E
    lane_head = lax.broadcasted_iota(jnp.int32, (rows, cw), 1) // head_dim
    label = seg_s[1:2, :]
    square_row = lax.broadcasted_iota(jnp.int32, (rows, rows), 0)
    square_col = lax.broadcasted_iota(jnp.int32, (rows, rows), 1)

    for k in range(hg):
        at = slice(k * rows, (k + 1) * rows)
        line = jnp.where(square_row == square_col, seg_s[0:1, at], 0.0)
        col_s[:, k : k + 1] = jnp.sum(line, axis=1, keepdims=True)

    def chunk(k, carry):
        start = pl.multiple_of(k * rows, rows)
        column = lax.broadcasted_iota(jnp.int32, (1, keys), 1)
        in_block = (column >= start) & (column < start + rows) & (label >= 0.0)
        same_value = jnp.where(in_block, 1.0, 0.0)
        other_value = jnp.where(in_block, 0.0, NEG_BIG)
        chosen = lax.broadcasted_iota(jnp.int32, (rows, 128), 1) == k
        segment = jnp.sum(
            jnp.where(chosen, col_s[...], 0.0), axis=1, keepdims=True
        )
        bias = jnp.where(segment == label, same_value, other_value)
        row_at = start + lax.broadcasted_iota(jnp.int32, (rows, keys), 0)
        col_at = lax.broadcasted_iota(jnp.int32, (rows, keys), 1)
        bias_s[...] = jnp.where(row_at == col_at, 1.0, bias)
        q = q_s[pl.ds(start, rows), :]
        scaled = jnp.zeros((rows, cw), jnp.float32)
        for h in range(heads):
            qh = jnp.where(lane_head == h, q, jnp.zeros_like(q))
            s = dot_last(qh, k_s[...]) * scale + bias_s[...]
            top = jnp.max(s, axis=1, keepdims=True)
            p = jnp.exp2(s - top)
            total = jnp.sum(p, axis=1, keepdims=True)
            p_s[h] = p.astype(jnp.bfloat16)
            inverse = 1.0 / total
            scaled = jnp.where(lane_head == h, inverse, scaled)
        acc = jnp.zeros((rows, cw), jnp.float32)
        for h in range(heads):
            acc = jnp.where(lane_head == h, dot(p_s[h], v_s[...]), acc)
        o_s[pl.ds(start, rows), :] = (acc * scaled).astype(jnp.bfloat16)
        d = (d_s[pl.ds(start, rows), :].astype(jnp.float32) * scaled).T.astype(jnp.bfloat16)
        for h in range(heads):
            at = slice(h * head_dim, (h + 1) * head_dim)
            gt_s[at, :] += dot(d[at, :], p_s[h])
        return carry

    lax.fori_loop(0, hg, chunk, 0)
    for k in range(hg):
        o_out[k][...] = o_s[k * rows : (k + 1) * rows, :]
    grad_s[...] = dot(gt_s[...].astype(jnp.bfloat16), t_s[...]).T
    first = lax.axis_index("dp") if by_dp else 0
    for tau in range(tg):
        for m in range(hg):
            to = ((group ^ m ^ first) * tg + (member ^ tau)) * wr
            to = pl.multiple_of(to, wr)
            g_out[tau][m] = grad_s[pl.ds(to, wr), :].astype(jnp.bfloat16)


def local(tiles, cotangent, segment_of, tissue_count, w_query, w_key, w_value, w_out):
    rows, width = tiles.shape[1:]
    wr = w_query.shape[0]
    n = lax.axis_size("seq")
    dp = lax.axis_size("dp")
    hg = math.gcd(HEADS, n)
    tg = n // hg
    cw = width // hg
    head_dim = width // HEADS
    by_dp = dp == hg
    own = lax.axis_index("seq")
    group = own // tg
    bf16 = jnp.bfloat16

    def hop(x, step):
        return lax.ppermute(x, "seq", [(s, s ^ step) for s in range(n)])

    def over_groups(pieces):
        return [pieces[0]] + [hop(pieces[k], k * tg) for k in range(1, hg)]

    def over_members(pieces):
        return [pieces] + [[hop(x, tau) for x in pieces] for tau in range(1, tg)]

    def flat(table):
        return [table[tau][k] for tau in range(tg) for k in range(hg)]

    wide = bf16 if wr % 16 == 0 else jnp.float32
    parts = 2 if hg == 4 and rows % 32 == 0 else 1
    segment_line = segment_of.reshape(1, rows)
    wout_table = over_members(over_groups([w_out] * hg))
    packed = pl.pallas_call(
        functools.partial(pack_kernel, hg, tg, wr, cw),
        out_shape=[jax.ShapeDtypeStruct((3, wr + 8, cw), bf16)] * hg,
        in_specs=[VM] * 4,
        out_specs=[VM] * hg,
    )(w_query, w_key, w_value, segment_line)
    weight_table = over_members(over_groups(packed))
    if parts == 2:
        half = rows // 2
        upper, lower = tiles[0, :half], tiles[0, half:]
        first = [hop(x, tg) for x in (upper, lower)]
        second = [hop(x, 2 * tg) for x in (upper, lower)]
        third = [hop(first[0], 2 * tg), hop(second[1], tg)]
        tile_pieces = [[upper, lower], first, second, third]
    else:
        tile_pieces = [[x] for x in over_groups([tiles[0]] * hg)]
    tile_pieces = tile_pieces + [
        [hop(x, tau) for x in piece] for tau in range(1, tg) for piece in tile_pieces
    ]

    *douts, wout = pl.pallas_call(
        functools.partial(dout_kernel, hg, tg, wr, cw),
        out_shape=[jax.ShapeDtypeStruct((rows, cw), bf16)] * hg
        + [jax.ShapeDtypeStruct((hg, cw, width), wide)],
        in_specs=[SM] + [VM] * (1 + n),
        out_specs=[VM] * (hg + 1),
    )(tissue_count, cotangent[0], *flat(wout_table))
    douts = over_groups(douts)

    keys = n * rows
    results = pl.pallas_call(
        functools.partial(main_kernel, hg, tg, parts, rows, wr, head_dim, by_dp),
        out_shape=[jax.ShapeDtypeStruct((rows, cw), bf16)] * hg
        + [jax.ShapeDtypeStruct((hg, wr, cw), bf16)] * tg,
        in_specs=[SM] + [ANY] * (n * parts) + [VM] * (n + hg),
        out_specs=[VM] * (hg + tg),
        scratch_shapes=[
            pltpu.VMEM((3, width, cw), wide),
            pltpu.VMEM((8, keys), jnp.float32),
            pltpu.VMEM((rows, 128), jnp.float32),
            pltpu.VMEM((hg * rows, cw), bf16),
            pltpu.VMEM((keys, cw), bf16),
            pltpu.VMEM((keys, cw), bf16),
            pltpu.VMEM((keys, width), bf16),
            pltpu.VMEM((rows, keys), jnp.float32),
            pltpu.VMEM((cw // head_dim, rows, keys), bf16),
            pltpu.VMEM((hg * rows, cw), bf16),
            pltpu.VMEM((hg * rows, cw), bf16),
            pltpu.VMEM((cw, keys), jnp.float32),
            pltpu.VMEM((width, cw), jnp.float32),
            pltpu.SemaphoreType.DMA((n * parts,)),
        ],
        compiler_params=pltpu.CompilerParams(vmem_limit_bytes=60 * 1024 * 1024),
    )(
        tissue_count,
        *[x for piece in tile_pieces for x in piece],
        *flat(weight_table),
        *douts,
    )
    attention = over_groups(results[:hg])
    grads = results[hg:]
    summed = grads[0].astype(jnp.float32)
    for tau in range(1, tg):
        summed = summed + hop(grads[tau], tau).astype(jnp.float32)
    summed = summed.astype(bf16)

    layer_rows = pl.pallas_call(
        functools.partial(proj_kernel, hg),
        out_shape=jax.ShapeDtypeStruct((1, rows, width), bf16),
        in_specs=[VM] * (1 + hg),
        out_specs=VM,
    )(wout, *attention)

    if by_dp:
        own_dp = lax.axis_index("dp")
        mine = summed[0].astype(jnp.float32)
        for m in range(1, hg):
            got = lax.ppermute(summed[m], "dp", [(z, z ^ m) for z in range(dp)])
            mine = mine + got.astype(jnp.float32)
        mine = mine.astype(bf16)
        parts = []
        for m in range(dp):
            pairs = [
                (z * n + s, (z ^ m) * n + (s ^ (z * tg))) for z in range(dp) for s in range(n)
            ]
            parts.append(lax.ppermute(mine, ("dp", "seq"), pairs))
        index = group ^ own_dp
    else:
        total = lax.psum(summed, "dp")
        parts = over_groups([total[k] for k in range(hg)])
        index = group
    columns = []
    for p in range(hg):
        piece = parts[0]
        for m in range(1, hg):
            piece = jnp.where((index ^ p) == m, parts[m], piece)
        columns.append(piece)
    return (layer_rows, jnp.concatenate(columns, axis=1).astype(jnp.float32))


def solution(mesh):
    placed = (
        P("dp", "seq", None),
        P("dp", "seq", None),
        P("dp", "seq", None),
        P("dp"),
        P("seq", None),
        P("seq", None),
        P("seq", None),
        P("seq", None),
    )
    return jax.shard_map(
        local,
        mesh=mesh,
        in_specs=placed,
        out_specs=(P("dp", "seq", None), P("seq", None)),
        check_vma=False,
    )
```

```python
import functools
import math

import jax
import jax.numpy as jnp
from jax import lax
from jax.experimental import pallas as pl
from jax.experimental.pallas import tpu as pltpu
from jax.sharding import PartitionSpec as P


HEADS = 12
NEG_BIG = -1e30
LOG2E = 1.4426950408889634


VM = pl.BlockSpec(memory_space=pltpu.VMEM)
ANY = pl.BlockSpec(memory_space=pl.ANY)
SM = pl.BlockSpec(memory_space=pltpu.SMEM)


def dot_last(a, b):
    return lax.dot_general(a, b, (((1,), (1,)), ((), ())), preferred_element_type=jnp.float32)


def dot(a, b):
    return lax.dot_general(a, b, (((1,), (0,)), ((), ())), preferred_element_type=jnp.float32)


def pack_kernel(hg, tg, wr, cw, wq, wk, wv, seg, *outs):
    group = lax.axis_index("seq") // tg
    for k in range(hg):
        for part in range(hg):

            @pl.when((group ^ k) == part)
            def _():
                cols = slice(part * cw, (part + 1) * cw)
                outs[k][0, :wr] = wq[:, cols]
                outs[k][1, :wr] = wk[:, cols]
                outs[k][2, :wr] = wv[:, cols]

        for i in range(3):
            outs[k][i, wr:] = jnp.broadcast_to(seg[...], (8, cw)).astype(jnp.bfloat16)


def dout_kernel(hg, tg, wr, count, cot, *refs):
    n = hg * tg
    pieces, outs, wout = refs[:n], refs[n : n + hg], refs[n + hg]
    own = lax.axis_index("seq")
    member = own % tg
    rows = cot.shape[0]
    position = own * rows + lax.broadcasted_iota(jnp.int32, cot.shape, 0)
    masked = jnp.where(position < count[0], cot[...].astype(jnp.float32), 0.0).astype(jnp.bfloat16)
    for k in range(hg):
        for tau in range(tg):
            to = pl.multiple_of((member ^ tau) * wr, wr)
            wout[k, pl.ds(to, wr), :] = pieces[tau * hg + k][...].astype(wout.dtype)
        block = wout[k].astype(jnp.bfloat16)
        outs[k][...] = dot_last(masked, block).astype(jnp.bfloat16)


def proj_kernel(hg, wout, *refs):
    out = refs[hg]
    total = None
    for k in range(hg):
        term = dot(refs[k][...], wout[k].astype(jnp.bfloat16))
        total = term if total is None else total + term
    out[0] = total.astype(jnp.bfloat16)


def main_kernel(hg, tg, parts, rows, wr, head_dim, by_dp, count, *refs):
    n = hg * tg
    refs = list(refs)
    tiles = [[refs.pop(0) for _ in range(parts)] for _ in range(n)]
    packed = [refs.pop(0) for _ in range(n)]
    douts = [refs.pop(0) for _ in range(hg)]
    o_out = [refs.pop(0) for _ in range(hg)]
    g_out = [refs.pop(0) for _ in range(tg)]
    wp_s, w_s, seg_s, col_s, q_s, k_s, v_s, t_s, bias_s, p_s, d_s, o_s, gt_s, grad_s, sems = refs
    cw = q_s.shape[1]
    own = lax.axis_index("seq")
    group = own // tg
    member = own % tg
    keys = n * rows
    heads = cw // head_dim
    packed_copies = [
        pltpu.make_async_copy(packed[r], wp_s.at[r], sems.at[n * parts + r]) for r in range(n)
    ]
    size = rows // parts
    tile_copies = [
        pltpu.make_async_copy(
            tiles[r][i], t_s.at[pl.ds(r * rows + i * size, size), :], sems.at[r * parts + i]
        )
        for r in range(n)
        for i in range(parts)
    ]
    dout_copies = [
        pltpu.make_async_copy(
            douts[k], d_s.at[pl.ds(k * rows, rows), :], sems.at[n * parts + n + k]
        )
        for k in range(hg)
    ]
    for copy in packed_copies + tile_copies + dout_copies:
        copy.start()
    for tau in range(tg):
        for k in range(hg):
            r = tau * hg + k
            packed_copies[r].wait()
            source = (group ^ k) * tg + (member ^ tau)
            to = pl.multiple_of(source * wr, wr)
            for i in range(3):
                w_s[i, pl.ds(to, wr), :] = wp_s[r, i, :wr].astype(w_s.dtype)
            line = wp_s[r, 0, wr : wr + 8, :].astype(jnp.float32)[:1]
            at = source * rows + lax.broadcasted_iota(jnp.int32, (1, rows), 1)
            columns = slice(r * rows, (r + 1) * rows)
            seg_s[0:1, columns] = line
            seg_s[1:2, columns] = jnp.where(at < count[0], line, -1.0)
    for copy in tile_copies:
        copy.wait()
    for tau in range(tg):
        at = slice(tau * hg * rows, (tau + 1) * hg * rows)
        block = t_s[at, :]
        if tau == 0:
            q_s[at, :] = dot(block, w_s[0].astype(jnp.bfloat16)).astype(jnp.bfloat16)
        k_s[at, :] = dot(block, w_s[1].astype(jnp.bfloat16)).astype(jnp.bfloat16)
        v_s[at, :] = dot(block, w_s[2].astype(jnp.bfloat16)).astype(jnp.bfloat16)
    for copy in dout_copies:
        copy.wait()
    gt_s[...] = jnp.zeros_like(gt_s)
    scale = head_dim ** (-0.5) * LOG2E
    lane_head = lax.broadcasted_iota(jnp.int32, (rows, cw), 1) // head_dim
    label = seg_s[1:2, :]
    square_row = lax.broadcasted_iota(jnp.int32, (rows, rows), 0)
    square_col = lax.broadcasted_iota(jnp.int32, (rows, rows), 1)

    for k in range(hg):
        at = slice(k * rows, (k + 1) * rows)
        line = jnp.where(square_row == square_col, seg_s[0:1, at], 0.0)
        col_s[:, k : k + 1] = jnp.sum(line, axis=1, keepdims=True)

    def chunk(k, carry):
        start = pl.multiple_of(k * rows, rows)
        column = lax.broadcasted_iota(jnp.int32, (1, keys), 1)
        in_block = (column >= start) & (column < start + rows) & (label >= 0.0)
        same_value = jnp.where(in_block, 1.0, 0.0)
        other_value = jnp.where(in_block, 0.0, NEG_BIG)
        chosen = lax.broadcasted_iota(jnp.int32, (rows, 128), 1) == k
        segment = jnp.sum(
            jnp.where(chosen, col_s[...], 0.0), axis=1, keepdims=True
        )
        bias = jnp.where(segment == label, same_value, other_value)
        row_at = start + lax.broadcasted_iota(jnp.int32, (rows, keys), 0)
        col_at = lax.broadcasted_iota(jnp.int32, (rows, keys), 1)
        bias_s[...] = jnp.where(row_at == col_at, 1.0, bias)
        q = q_s[pl.ds(start, rows), :]
        scaled = jnp.zeros((rows, cw), jnp.float32)
        for h in range(heads):
            qh = jnp.where(lane_head == h, q, jnp.zeros_like(q))
            s = dot_last(qh, k_s[...]) * scale + bias_s[...]
            top = jnp.max(s, axis=1, keepdims=True)
            p = jnp.exp2(s - top)
            total = jnp.sum(p, axis=1, keepdims=True)
            p_s[h] = p.astype(jnp.bfloat16)
            inverse = 1.0 / total
            scaled = jnp.where(lane_head == h, inverse, scaled)
        acc = jnp.zeros((rows, cw), jnp.float32)
        for h in range(heads):
            acc = jnp.where(lane_head == h, dot(p_s[h], v_s[...]), acc)
        o_s[pl.ds(start, rows), :] = (acc * scaled).astype(jnp.bfloat16)
        d = (d_s[pl.ds(start, rows), :].astype(jnp.float32) * scaled).T.astype(jnp.bfloat16)
        for h in range(heads):
            at = slice(h * head_dim, (h + 1) * head_dim)
            gt_s[at, :] += dot(d[at, :], p_s[h])
        return carry

    lax.fori_loop(0, hg, chunk, 0, unroll=True)
    for k in range(hg):
        o_out[k][...] = o_s[k * rows : (k + 1) * rows, :]
    grad_s[...] = dot(gt_s[...].astype(jnp.bfloat16), t_s[...]).T
    first = lax.axis_index("dp") if by_dp else 0
    for tau in range(tg):
        for m in range(hg):
            to = ((group ^ m ^ first) * tg + (member ^ tau)) * wr
            to = pl.multiple_of(to, wr)
            g_out[tau][m] = grad_s[pl.ds(to, wr), :].astype(jnp.bfloat16)


def main_call(hg, tg, parts, rows, width, wr, cw, head_dim, by_dp):
    n = hg * tg
    keys = n * rows
    bf16 = jnp.bfloat16
    wide = bf16 if wr % 16 == 0 else jnp.float32
    return pl.pallas_call(
        functools.partial(main_kernel, hg, tg, parts, rows, wr, head_dim, by_dp),
        out_shape=[jax.ShapeDtypeStruct((rows, cw), bf16)] * hg
        + [jax.ShapeDtypeStruct((hg, wr, cw), bf16)] * tg,
        in_specs=[SM] + [ANY] * (n * parts + n + hg),
        out_specs=[VM] * (hg + tg),
        scratch_shapes=[
            pltpu.VMEM((n, 3, wr + 8, cw), bf16),
            pltpu.VMEM((3, width, cw), wide),
            pltpu.VMEM((8, keys), jnp.float32),
            pltpu.VMEM((rows, 128), jnp.float32),
            pltpu.VMEM((hg * rows, cw), bf16),
            pltpu.VMEM((keys, cw), bf16),
            pltpu.VMEM((keys, cw), bf16),
            pltpu.VMEM((keys, width), bf16),
            pltpu.VMEM((rows, keys), jnp.float32),
            pltpu.VMEM((cw // head_dim, rows, keys), bf16),
            pltpu.VMEM((hg * rows, cw), bf16),
            pltpu.VMEM((hg * rows, cw), bf16),
            pltpu.VMEM((cw, keys), jnp.float32),
            pltpu.VMEM((width, cw), jnp.float32),
            pltpu.SemaphoreType.DMA((n * parts + n + hg,)),
        ],
        compiler_params=pltpu.CompilerParams(vmem_limit_bytes=60 * 1024 * 1024),
    )


def local(tiles, cotangent, segment_of, tissue_count, w_query, w_key, w_value, w_out):
    rows, width = tiles.shape[1:]
    wr = w_query.shape[0]
    n = lax.axis_size("seq")
    dp = lax.axis_size("dp")
    hg = math.gcd(HEADS, n)
    tg = n // hg
    cw = width // hg
    head_dim = width // HEADS
    by_dp = dp == hg
    own = lax.axis_index("seq")
    group = own // tg
    bf16 = jnp.bfloat16

    def hop(x, step):
        return lax.ppermute(x, "seq", [(s, s ^ step) for s in range(n)])

    def over_groups(pieces):
        return [pieces[0]] + [hop(pieces[k], k * tg) for k in range(1, hg)]

    def over_members(pieces):
        return [pieces] + [[hop(x, tau) for x in pieces] for tau in range(1, tg)]

    def flat(table):
        return [table[tau][k] for tau in range(tg) for k in range(hg)]

    wide = bf16 if wr % 16 == 0 else jnp.float32
    parts = 2 if hg == 4 and rows % 32 == 0 else 1
    segment_line = segment_of.reshape(1, rows)
    wout_table = over_members(over_groups([w_out] * hg))
    packed = pl.pallas_call(
        functools.partial(pack_kernel, hg, tg, wr, cw),
        out_shape=[jax.ShapeDtypeStruct((3, wr + 8, cw), bf16)] * hg,
        in_specs=[VM] * 4,
        out_specs=[VM] * hg,
    )(w_query, w_key, w_value, segment_line)
    weight_table = over_members(over_groups(packed))
    if parts == 2:
        half = rows // 2
        upper, lower = tiles[0, :half], tiles[0, half:]
        first = [hop(upper, tg), hop(lower, tg)]
        second = [hop(upper, 2 * tg), hop(lower, 2 * tg)]
        third = [hop(first[0], 2 * tg), hop(second[1], tg)]
        tile_pieces = [[upper, lower], first, second, third]
    else:
        tile_pieces = [[x] for x in over_groups([tiles[0]] * hg)]
    tile_pieces = tile_pieces + [
        [hop(x, tau) for x in piece]
        for tau in range(1, tg)
        for piece in tile_pieces
    ]

    *douts, wout = pl.pallas_call(
        functools.partial(dout_kernel, hg, tg, wr),
        out_shape=[jax.ShapeDtypeStruct((rows, cw), bf16)] * hg
        + [jax.ShapeDtypeStruct((hg, cw, width), wide)],
        in_specs=[SM] + [VM] * (1 + n),
        out_specs=[VM] * (hg + 1),
    )(tissue_count, cotangent[0], *flat(wout_table))
    douts = over_groups(douts)

    results = main_call(hg, tg, parts, rows, width, wr, cw, head_dim, by_dp)(
        tissue_count,
        *[x for piece in tile_pieces for x in piece],
        *flat(weight_table),
        *douts,
    )
    attention = over_groups(results[:hg])
    grads = results[hg:]
    summed = grads[0].astype(jnp.float32)
    for tau in range(1, tg):
        summed = summed + hop(grads[tau], tau).astype(jnp.float32)
    summed = summed.astype(bf16)

    layer_rows = pl.pallas_call(
        functools.partial(proj_kernel, hg),
        out_shape=jax.ShapeDtypeStruct((1, rows, width), bf16),
        in_specs=[VM] * (1 + hg),
        out_specs=VM,
    )(wout, *attention)

    if by_dp:
        own_dp = lax.axis_index("dp")
        mine = summed[0].astype(jnp.float32)
        for m in range(1, hg):
            got = lax.ppermute(summed[m], "dp", [(z, z ^ m) for z in range(dp)])
            mine = mine + got.astype(jnp.float32)
        mine = mine.astype(bf16)
        parts = []
        for m in range(dp):
            pairs = [
                (z * n + s, (z ^ m) * n + (s ^ (z * tg))) for z in range(dp) for s in range(n)
            ]
            parts.append(lax.ppermute(mine, ("dp", "seq"), pairs))
        index = group ^ own_dp
    else:
        total = lax.psum(summed, "dp")
        parts = over_groups([total[k] for k in range(hg)])
        index = group
    columns = []
    for p in range(hg):
        piece = parts[0]
        for m in range(1, hg):
            piece = jnp.where((index ^ p) == m, parts[m], piece)
        columns.append(piece)
    return (layer_rows, jnp.concatenate(columns, axis=1).astype(jnp.float32))


def solution(mesh):
    placed = (
        P("dp", "seq", None),
        P("dp", "seq", None),
        P("dp", "seq", None),
        P("dp"),
        P("seq", None),
        P("seq", None),
        P("seq", None),
        P("seq", None),
    )
    return jax.shard_map(
        local,
        mesh=mesh,
        in_specs=placed,
        out_specs=(P("dp", "seq", None), P("seq", None)),
        check_vma=False,
    )
```

```python
import functools
import math

import jax
import jax.numpy as jnp
from jax import lax
from jax.experimental import pallas as pl
from jax.experimental.pallas import tpu as pltpu
from jax.sharding import PartitionSpec as P


HEADS = 12
NEG_BIG = -1e30
LOG2E = 1.4426950408889634


VM = pl.BlockSpec(memory_space=pltpu.VMEM)
ANY = pl.BlockSpec(memory_space=pl.ANY)
SM = pl.BlockSpec(memory_space=pltpu.SMEM)


def dot_last(a, b):
    return lax.dot_general(a, b, (((1,), (1,)), ((), ())), preferred_element_type=jnp.float32)


def dot(a, b):
    return lax.dot_general(a, b, (((1,), (0,)), ((), ())), preferred_element_type=jnp.float32)


def pack_kernel(hg, tg, wr, cw, wq, wk, wv, seg, *outs):
    group = lax.axis_index("seq") // tg
    for k in range(hg):
        for part in range(hg):

            @pl.when((group ^ k) == part)
            def _():
                cols = slice(part * cw, (part + 1) * cw)
                outs[k][0, :wr] = wq[:, cols]
                outs[k][1, :wr] = wk[:, cols]
                outs[k][2, :wr] = wv[:, cols]

        for i in range(3):
            outs[k][i, wr:] = jnp.broadcast_to(seg[...], (8, cw)).astype(jnp.bfloat16)


def place_rows(scratch, pieces, member, wr):
    for tau, piece in enumerate(pieces):
        to = pl.multiple_of((member ^ tau) * wr, wr)
        scratch[pl.ds(to, wr), :] = piece[...].astype(scratch.dtype)
    return scratch[...].astype(jnp.bfloat16)


def proj_kernel(hg, tg, wr, *refs):
    n = hg * tg
    attention, pieces, out, wout = refs[:hg], refs[hg : hg + n], refs[hg + n], refs[hg + n + 1]
    member = lax.axis_index("seq") % tg
    total = None
    for k in range(hg):
        block = place_rows(wout.at[k], pieces[k::hg], member, wr)
        term = dot(attention[k][...], block)
        total = term if total is None else total + term
    out[0] = total.astype(jnp.bfloat16)


def attention_kernel(hg, tg, parts, rows, wr, head_dim, count, *refs):
    n = hg * tg
    refs = list(refs)
    tiles = [[refs.pop(0) for _ in range(parts)] for _ in range(n)]
    packed = [refs.pop(0) for _ in range(n)]
    o_out = [refs.pop(0) for _ in range(hg)]
    scaled_out, p_out = refs.pop(0), refs.pop(0)
    wp_s, w_s, seg_s, col_s, q_s, k_s, v_s, t_s, bias_s, p_s, o_s, sems = refs
    cw = q_s.shape[1]
    own = lax.axis_index("seq")
    group = own // tg
    member = own % tg
    keys = n * rows
    heads = cw // head_dim
    packed_copies = [
        pltpu.make_async_copy(packed[r], wp_s.at[r], sems.at[n * parts + r]) for r in range(n)
    ]
    size = rows // parts
    tile_copies = [
        pltpu.make_async_copy(
            tiles[r][i], t_s.at[pl.ds(r * rows + i * size, size), :], sems.at[r * parts + i]
        )
        for r in range(n)
        for i in range(parts)
    ]
    for copy in packed_copies + tile_copies:
        copy.start()
    for tau in range(tg):
        for k in range(hg):
            r = tau * hg + k
            packed_copies[r].wait()
            source = (group ^ k) * tg + (member ^ tau)
            to = pl.multiple_of(source * wr, wr)
            for i in range(3):
                w_s[i, pl.ds(to, wr), :] = wp_s[r, i, :wr].astype(w_s.dtype)
            line = wp_s[r, 0, wr : wr + 8, :].astype(jnp.float32)[:1]
            at = source * rows + lax.broadcasted_iota(jnp.int32, (1, rows), 1)
            columns = slice(r * rows, (r + 1) * rows)
            seg_s[0:1, columns] = line
            seg_s[1:2, columns] = jnp.where(at < count[0], line, -1.0)
    for copy in tile_copies:
        copy.wait()
    for tau in range(tg):
        at = slice(tau * hg * rows, (tau + 1) * hg * rows)
        block = t_s[at, :]
        if tau == 0:
            q_s[at, :] = dot(block, w_s[0].astype(jnp.bfloat16)).astype(jnp.bfloat16)
        k_s[at, :] = dot(block, w_s[1].astype(jnp.bfloat16)).astype(jnp.bfloat16)
        v_s[at, :] = dot(block, w_s[2].astype(jnp.bfloat16)).astype(jnp.bfloat16)
    scale = head_dim ** (-0.5) * LOG2E
    lane_head = lax.broadcasted_iota(jnp.int32, (rows, cw), 1) // head_dim
    label = seg_s[1:2, :]
    square_row = lax.broadcasted_iota(jnp.int32, (rows, rows), 0)
    square_col = lax.broadcasted_iota(jnp.int32, (rows, rows), 1)
    column = lax.broadcasted_iota(jnp.int32, (1, keys), 1)
    row_at = lax.broadcasted_iota(jnp.int32, (rows, keys), 0)
    col_at = lax.broadcasted_iota(jnp.int32, (rows, keys), 1)
    slots = p_s.shape[0]

    def p_copy(k):
        slot = k % slots
        return pltpu.make_async_copy(p_s.at[slot], p_out.at[k], sems.at[n * parts + n + slot])

    def chunk(k, carry):
        start = k * rows if isinstance(k, int) else pl.multiple_of(k * rows, rows)
        at = pl.ds(start, rows)
        slot = k % slots
        segment = col_s[k]
        in_block = (column >= start) & (column < start + rows) & (label >= 0.0)
        same_value = jnp.where(in_block, 1.0, 0.0)
        other_value = jnp.where(in_block, 0.0, NEG_BIG)
        bias = jnp.where(segment == label, same_value, other_value)
        bias_s[...] = jnp.where(row_at + start == col_at, 1.0, bias)
        q = q_s[at, :]
        scaled = jnp.zeros((rows, cw), jnp.float32)
        if slots < hg:

            @pl.when(k >= slots)
            def _():
                p_copy(k - slots).wait()

        for h in range(heads):
            qh = jnp.where(lane_head == h, q, jnp.zeros_like(q))
            s = dot_last(qh, k_s[...]) * scale + bias_s[...]
            top = jnp.max(s, axis=1, keepdims=True)
            p = jnp.exp2(s - top)
            total = jnp.sum(p, axis=1, keepdims=True)
            p_s[slot, h] = p.astype(jnp.bfloat16)
            scaled = jnp.where(lane_head == h, 1.0 / total, scaled)
        p_copy(k).start()
        acc = jnp.zeros((rows, cw), jnp.float32)
        for h in range(heads):
            acc = jnp.where(lane_head == h, dot(p_s[slot, h], v_s[...]), acc)
        scaled_out[at, :] = scaled
        o_s[at, :] = (acc * scaled).astype(jnp.bfloat16)
        return carry

    for k in range(hg):
        line = jnp.where(square_row == square_col, seg_s[0:1, k * rows : (k + 1) * rows], 0.0)
        col_s[k] = jnp.sum(line, axis=1, keepdims=True)
    if slots == hg:
        for k in range(hg):
            chunk(k, 0)
    else:
        lax.fori_loop(0, hg, chunk, 0)
    for k in range(hg):
        o_out[k][...] = o_s[k * rows : (k + 1) * rows, :]
    for k in range(hg - slots, hg):
        p_copy(k).wait()


def slot_count(hg, keys):
    return hg if keys <= 2048 else 1


def attention_call(hg, tg, parts, rows, width, wr, cw, head_dim):
    n = hg * tg
    keys = n * rows
    heads = cw // head_dim
    bf16 = jnp.bfloat16
    wide = bf16 if wr % 16 == 0 else jnp.float32
    return pl.pallas_call(
        functools.partial(attention_kernel, hg, tg, parts, rows, wr, head_dim),
        out_shape=[jax.ShapeDtypeStruct((rows, cw), bf16)] * hg
        + [
            jax.ShapeDtypeStruct((hg * rows, cw), jnp.float32),
            jax.ShapeDtypeStruct((hg, heads, rows, keys), bf16),
        ],
        in_specs=[SM] + [ANY] * (n * parts + n),
        out_specs=[VM] * (hg + 1) + [ANY],
        scratch_shapes=[
            pltpu.VMEM((n, 3, wr + 8, cw), bf16),
            pltpu.VMEM((3, width, cw), wide),
            pltpu.VMEM((8, keys), jnp.float32),
            pltpu.VMEM((hg, rows, 1), jnp.float32),
            pltpu.VMEM((hg * rows, cw), bf16),
            pltpu.VMEM((keys, cw), bf16),
            pltpu.VMEM((keys, cw), bf16),
            pltpu.VMEM((keys, width), bf16),
            pltpu.VMEM((rows, keys), jnp.float32),
            pltpu.VMEM((slot_count(hg, keys), heads, rows, keys), bf16),
            pltpu.VMEM((hg * rows, cw), bf16),
            pltpu.SemaphoreType.DMA((n * parts + n + hg,)),
        ],
        compiler_params=pltpu.CompilerParams(vmem_limit_bytes=60 * 1024 * 1024),
    )


def gradient_kernel(hg, tg, parts, rows, wr, head_dim, by_dp, count, *refs):
    n = hg * tg
    refs = list(refs)
    tiles = [[refs.pop(0) for _ in range(parts)] for _ in range(n)]
    p_in = refs.pop(0)
    cots = [refs.pop(0) for _ in range(hg)]
    wout_pieces = [refs.pop(0) for _ in range(tg)]
    scaled_in = refs.pop(0)
    g_out = [refs.pop(0) for _ in range(tg)]
    wout_s, t_s, p_s, gt_s, grad_s, sems = refs
    cw = wout_s.shape[0]
    own = lax.axis_index("seq")
    group = own // tg
    member = own % tg
    heads = cw // head_dim
    size = rows // parts
    slots = p_s.shape[0]
    p_copies = [
        pltpu.make_async_copy(
            p_in.at[k], p_s.at[k % slots], sems.at[n * parts + k % slots]
        )
        for k in range(hg)
    ]
    tile_copies = [
        pltpu.make_async_copy(
            tiles[r][i], t_s.at[pl.ds(r * rows + i * size, size), :], sems.at[r * parts + i]
        )
        for r in range(n)
        for i in range(parts)
    ]
    for copy in p_copies[:slots] + tile_copies:
        copy.start()
    wout = place_rows(wout_s, wout_pieces, member, wr)
    iota = lax.broadcasted_iota(jnp.int32, cots[0].shape, 0)
    for k in range(hg):
        position = ((group ^ k) * tg + member) * rows + iota
        masked = jnp.where(position < count[0], cots[k][...].astype(jnp.float32), 0.0)
        dout = dot_last(masked.astype(jnp.bfloat16), wout).astype(jnp.bfloat16)
        scaled = scaled_in[k * rows : (k + 1) * rows, :]
        d = (dout.astype(jnp.float32) * scaled).T.astype(jnp.bfloat16)
        p_copies[k].wait()
        for h in range(heads):
            at = slice(h * head_dim, (h + 1) * head_dim)
            term = dot(d[at, :], p_s[k % slots, h])
            gt_s[at, :] = term if k == 0 else gt_s[at, :] + term
        if k + slots < hg:
            p_copies[k + slots].start()
    for copy in tile_copies:
        copy.wait()
    grad_s[...] = dot(gt_s[...].astype(jnp.bfloat16), t_s[...]).T
    first = lax.axis_index("dp") if by_dp else 0
    for tau in range(tg):
        for m in range(hg):
            to = ((group ^ m ^ first) * tg + (member ^ tau)) * wr
            to = pl.multiple_of(to, wr)
            g_out[tau][m] = grad_s[pl.ds(to, wr), :].astype(jnp.bfloat16)


def gradient_call(hg, tg, parts, rows, width, wr, cw, head_dim, by_dp):
    n = hg * tg
    keys = n * rows
    heads = cw // head_dim
    bf16 = jnp.bfloat16
    wide = bf16 if wr % 16 == 0 else jnp.float32
    return pl.pallas_call(
        functools.partial(gradient_kernel, hg, tg, parts, rows, wr, head_dim, by_dp),
        out_shape=[jax.ShapeDtypeStruct((hg, wr, cw), bf16)] * tg,
        in_specs=[SM] + [ANY] * (n * parts + 1) + [VM] * (hg + tg + 1),
        out_specs=[VM] * tg,
        scratch_shapes=[
            pltpu.VMEM((cw, width), wide),
            pltpu.VMEM((keys, width), bf16),
            pltpu.VMEM((slot_count(hg, keys), heads, rows, keys), bf16),
            pltpu.VMEM((cw, keys), jnp.float32),
            pltpu.VMEM((width, cw), jnp.float32),
            pltpu.SemaphoreType.DMA((n * parts + hg,)),
        ],
        compiler_params=pltpu.CompilerParams(vmem_limit_bytes=60 * 1024 * 1024),
    )


def local(tiles, cotangent, segment_of, tissue_count, w_query, w_key, w_value, w_out):
    rows, width = tiles.shape[1:]
    wr = w_query.shape[0]
    n = lax.axis_size("seq")
    dp = lax.axis_size("dp")
    hg = math.gcd(HEADS, n)
    tg = n // hg
    cw = width // hg
    head_dim = width // HEADS
    by_dp = dp == hg
    own = lax.axis_index("seq")
    group = own // tg
    bf16 = jnp.bfloat16

    def hop(x, step):
        return lax.ppermute(x, "seq", [(s, s ^ step) for s in range(n)])

    def over_groups(pieces):
        return [pieces[0]] + [hop(pieces[k], k * tg) for k in range(1, hg)]

    def over_members(pieces):
        return [pieces] + [[hop(x, tau) for x in pieces] for tau in range(1, tg)]

    def flat(table):
        return [table[tau][k] for tau in range(tg) for k in range(hg)]

    wide = bf16 if wr % 16 == 0 else jnp.float32
    parts = 2 if hg == 4 and rows % 32 == 0 else 1
    segment_line = segment_of.reshape(1, rows)
    packed = pl.pallas_call(
        functools.partial(pack_kernel, hg, tg, wr, cw),
        out_shape=[jax.ShapeDtypeStruct((3, wr + 8, cw), bf16)] * hg,
        in_specs=[VM] * 4,
        out_specs=[VM] * hg,
    )(w_query, w_key, w_value, segment_line)
    weight_table = over_members(over_groups(packed))
    if parts == 2:
        half = rows // 2
        upper, lower = tiles[0, :half], tiles[0, half:]
        first = [hop(upper, tg), hop(lower, tg)]
        second = [hop(upper, 2 * tg), hop(lower, 2 * tg)]
        third = [hop(first[0], 2 * tg), hop(second[1], tg)]
        tile_pieces = [[upper, lower], first, second, third]
    else:
        tile_pieces = [[x] for x in over_groups([tiles[0]] * hg)]
    tile_pieces = tile_pieces + [
        [hop(x, tau) for x in piece]
        for tau in range(1, tg)
        for piece in tile_pieces
    ]
    flat_tiles = [x for piece in tile_pieces for x in piece]
    cots = over_groups([cotangent[0]] * hg)
    wout_table = over_members(over_groups([w_out] * hg))

    *attention, scaled, weights = attention_call(
        hg, tg, parts, rows, width, wr, cw, head_dim
    )(tissue_count, *flat_tiles, *flat(weight_table))
    attention = over_groups(attention)
    grads = gradient_call(hg, tg, parts, rows, width, wr, cw, head_dim, by_dp)(
        tissue_count,
        *flat_tiles,
        weights,
        *cots,
        *[line[0] for line in wout_table],
        scaled,
    )
    summed = grads[0].astype(jnp.float32)
    for tau in range(1, tg):
        summed = summed + hop(grads[tau], tau).astype(jnp.float32)
    summed = summed.astype(bf16)

    layer_rows = pl.pallas_call(
        functools.partial(proj_kernel, hg, tg, wr),
        out_shape=jax.ShapeDtypeStruct((1, rows, width), bf16),
        in_specs=[VM] * (hg + n),
        out_specs=VM,
        scratch_shapes=[pltpu.VMEM((hg, cw, width), wide)],
    )(*attention, *flat(wout_table))

    if by_dp:
        own_dp = lax.axis_index("dp")
        mine = summed[0].astype(jnp.float32)
        for m in range(1, hg):
            got = lax.ppermute(summed[m], "dp", [(z, z ^ m) for z in range(dp)])
            mine = mine + got.astype(jnp.float32)
        mine = mine.astype(bf16)
        pieces = []
        for m in range(dp):
            pairs = [
                (z * n + s, (z ^ m) * n + (s ^ (z * tg))) for z in range(dp) for s in range(n)
            ]
            pieces.append(lax.ppermute(mine, ("dp", "seq"), pairs))
        index = group ^ own_dp
    else:
        total = lax.psum(summed, "dp")
        pieces = over_groups([total[k] for k in range(hg)])
        index = group
    columns = []
    for p in range(hg):
        piece = pieces[0]
        for m in range(1, hg):
            piece = jnp.where((index ^ p) == m, pieces[m], piece)
        columns.append(piece)
    return (layer_rows, jnp.concatenate(columns, axis=1).astype(jnp.float32))


def solution(mesh):
    placed = (
        P("dp", "seq", None),
        P("dp", "seq", None),
        P("dp", "seq", None),
        P("dp"),
        P("seq", None),
        P("seq", None),
        P("seq", None),
        P("seq", None),
    )
    return jax.shard_map(
        local,
        mesh=mesh,
        in_specs=placed,
        out_specs=(P("dp", "seq", None), P("seq", None)),
        check_vma=False,
    )
```

```python
import functools
import math

import jax
import jax.numpy as jnp
from jax import lax
from jax.experimental import pallas as pl
from jax.experimental.pallas import tpu as pltpu
from jax.sharding import PartitionSpec as P


HEADS = 12
NEG_BIG = -1e30
LOG2E = 1.4426950408889634


VM = pl.BlockSpec(memory_space=pltpu.VMEM)
ANY = pl.BlockSpec(memory_space=pl.ANY)
SM = pl.BlockSpec(memory_space=pltpu.SMEM)


def dot_last(a, b):
    return lax.dot_general(a, b, (((1,), (1,)), ((), ())), preferred_element_type=jnp.float32)


def dot(a, b):
    return lax.dot_general(a, b, (((1,), (0,)), ((), ())), preferred_element_type=jnp.float32)


def pack_kernel(hg, tg, wr, cw, wq, wk, wv, seg, *outs):
    group = lax.axis_index("seq") // tg
    for k in range(hg):
        for part in range(hg):

            @pl.when((group ^ k) == part)
            def _():
                cols = slice(part * cw, (part + 1) * cw)
                outs[k][0, :wr] = wq[:, cols]
                outs[k][1, :wr] = wk[:, cols]
                outs[k][2, :wr] = wv[:, cols]

        for i in range(3):
            outs[k][i, wr:] = jnp.broadcast_to(seg[...], (8, cw)).astype(jnp.bfloat16)


def place_rows(scratch, pieces, member, wr):
    for tau, piece in enumerate(pieces):
        to = pl.multiple_of((member ^ tau) * wr, wr)
        scratch[pl.ds(to, wr), :] = piece[...].astype(scratch.dtype)
    return scratch[...].astype(jnp.bfloat16)


def proj_kernel(hg, tg, wr, *refs):
    n = hg * tg
    attention, pieces, out, wout = refs[:hg], refs[hg : hg + n], refs[hg + n], refs[hg + n + 1]
    member = lax.axis_index("seq") % tg
    total = None
    for k in range(hg):
        block = place_rows(wout.at[k], pieces[k::hg], member, wr)
        term = dot(attention[k][...], block)
        total = term if total is None else total + term
    out[0] = total.astype(jnp.bfloat16)


def attention_kernel(hg, tg, parts, rows, wr, head_dim, resident, count, *refs):
    n = hg * tg
    refs = list(refs)
    tiles = [[refs.pop(0) for _ in range(parts)] for _ in range(n)]
    packed = [refs.pop(0) for _ in range(n)]
    o_out = [refs.pop(0) for _ in range(hg)]
    scaled_out, p_out = refs.pop(0), refs.pop(0)
    if resident:
        p_s, t_s = p_out, refs.pop(0)
    else:
        p_s, t_s = refs.pop(0), refs.pop(0)
    wp_s, w_s, seg_s, col_s, q_s, k_s, v_s, bias_s, o_s, sems = refs
    cw = q_s.shape[1]
    own = lax.axis_index("seq")
    group = own // tg
    member = own % tg
    keys = n * rows
    heads = cw // head_dim
    packed_copies = [
        pltpu.make_async_copy(packed[r], wp_s.at[r], sems.at[n * parts + r]) for r in range(n)
    ]
    size = rows // parts
    tile_copies = [
        pltpu.make_async_copy(
            tiles[r][i], t_s.at[pl.ds(r * rows + i * size, size), :], sems.at[r * parts + i]
        )
        for r in range(n)
        for i in range(parts)
    ]
    for copy in packed_copies + tile_copies:
        copy.start()
    for tau in range(tg):
        for k in range(hg):
            r = tau * hg + k
            packed_copies[r].wait()
            source = (group ^ k) * tg + (member ^ tau)
            to = pl.multiple_of(source * wr, wr)
            for i in range(3):
                w_s[i, pl.ds(to, wr), :] = wp_s[r, i, :wr].astype(w_s.dtype)
            line = wp_s[r, 0, wr : wr + 8, :].astype(jnp.float32)[:1]
            at = source * rows + lax.broadcasted_iota(jnp.int32, (1, rows), 1)
            columns = slice(r * rows, (r + 1) * rows)
            seg_s[0:1, columns] = line
            seg_s[1:2, columns] = jnp.where(at < count[0], line, -1.0)
    for copy in tile_copies:
        copy.wait()
    for tau in range(tg):
        at = slice(tau * hg * rows, (tau + 1) * hg * rows)
        block = t_s[at, :]
        if tau == 0:
            q_s[at, :] = dot(block, w_s[0].astype(jnp.bfloat16)).astype(jnp.bfloat16)
        k_s[at, :] = dot(block, w_s[1].astype(jnp.bfloat16)).astype(jnp.bfloat16)
        v_s[at, :] = dot(block, w_s[2].astype(jnp.bfloat16)).astype(jnp.bfloat16)
    scale = head_dim ** (-0.5) * LOG2E
    lane_head = lax.broadcasted_iota(jnp.int32, (rows, cw), 1) // head_dim
    label = seg_s[1:2, :]
    square_row = lax.broadcasted_iota(jnp.int32, (rows, rows), 0)
    square_col = lax.broadcasted_iota(jnp.int32, (rows, rows), 1)
    column = lax.broadcasted_iota(jnp.int32, (1, keys), 1)
    row_at = lax.broadcasted_iota(jnp.int32, (rows, keys), 0)
    col_at = lax.broadcasted_iota(jnp.int32, (rows, keys), 1)
    slots = p_s.shape[0]

    def p_copy(k):
        slot = k % slots
        return pltpu.make_async_copy(p_s.at[slot], p_out.at[k], sems.at[n * parts + n + slot])

    def chunk(k, carry):
        start = k * rows if isinstance(k, int) else pl.multiple_of(k * rows, rows)
        at = pl.ds(start, rows)
        slot = k % slots
        segment = col_s[k]
        in_block = (column >= start) & (column < start + rows) & (label >= 0.0)
        same_value = jnp.where(in_block, 1.0, 0.0)
        other_value = jnp.where(in_block, 0.0, NEG_BIG)
        bias = jnp.where(segment == label, same_value, other_value)
        bias_s[...] = jnp.where(row_at + start == col_at, 1.0, bias)
        q = q_s[at, :]
        scaled = jnp.zeros((rows, cw), jnp.float32)
        if slots < hg:

            @pl.when(k >= slots)
            def _():
                p_copy(k - slots).wait()

        for h in range(heads):
            qh = jnp.where(lane_head == h, q, jnp.zeros_like(q))
            s = dot_last(qh, k_s[...]) * scale + bias_s[...]
            top = jnp.max(s, axis=1, keepdims=True)
            p = jnp.exp2(s - top)
            total = jnp.sum(p, axis=1, keepdims=True)
            p_s[slot, h] = p.astype(jnp.bfloat16)
            scaled = jnp.where(lane_head == h, 1.0 / total, scaled)
        if not resident:
            p_copy(k).start()
        acc = jnp.zeros((rows, cw), jnp.float32)
        for h in range(heads):
            acc = jnp.where(lane_head == h, dot(p_s[slot, h], v_s[...]), acc)
        scaled_out[at, :] = scaled
        o_s[at, :] = (acc * scaled).astype(jnp.bfloat16)
        return carry

    for k in range(hg):
        line = jnp.where(square_row == square_col, seg_s[0:1, k * rows : (k + 1) * rows], 0.0)
        col_s[k] = jnp.sum(line, axis=1, keepdims=True)
    if slots == hg:
        for k in range(hg):
            chunk(k, 0)
    else:
        lax.fori_loop(0, hg, chunk, 0)
    for k in range(hg):
        o_out[k][...] = o_s[k * rows : (k + 1) * rows, :]
    for k in range(hg - slots, hg):
        if not resident:
            p_copy(k).wait()


def fits(keys):
    return keys <= 2048


def attention_call(hg, tg, parts, rows, width, wr, cw, head_dim):
    n = hg * tg
    keys = n * rows
    heads = cw // head_dim
    bf16 = jnp.bfloat16
    wide = bf16 if wr % 16 == 0 else jnp.float32
    resident = fits(keys)
    if resident:
        kept = [pltpu.VMEM((hg, heads, rows, keys), bf16), pltpu.VMEM((keys, width), bf16)]
        local = []
    else:
        kept = [jax.ShapeDtypeStruct((hg, heads, rows, keys), bf16)]
        local = [pltpu.VMEM((1, heads, rows, keys), bf16), pltpu.VMEM((keys, width), bf16)]
    return pl.pallas_call(
        functools.partial(attention_kernel, hg, tg, parts, rows, wr, head_dim, resident),
        out_shape=[jax.ShapeDtypeStruct((rows, cw), bf16)] * hg
        + [jax.ShapeDtypeStruct((hg * rows, cw), jnp.float32)]
        + kept,
        in_specs=[SM] + [ANY] * (n * parts + n),
        out_specs=[VM] * (hg + 1) + [VM if resident else ANY] * len(kept),
        scratch_shapes=local
        + [
            pltpu.VMEM((n, 3, wr + 8, cw), bf16),
            pltpu.VMEM((3, width, cw), wide),
            pltpu.VMEM((8, keys), jnp.float32),
            pltpu.VMEM((hg, rows, 1), jnp.float32),
            pltpu.VMEM((hg * rows, cw), bf16),
            pltpu.VMEM((keys, cw), bf16),
            pltpu.VMEM((keys, cw), bf16),
            pltpu.VMEM((rows, keys), jnp.float32),
            pltpu.VMEM((hg * rows, cw), bf16),
            pltpu.SemaphoreType.DMA((n * parts + n + hg,)),
        ],
        compiler_params=pltpu.CompilerParams(vmem_limit_bytes=(40 if resident else 60) * 1024 * 1024),
    )


def gradient_kernel(hg, tg, parts, rows, wr, head_dim, by_dp, resident, count, *refs):
    n = hg * tg
    refs = list(refs)
    if resident:
        p_s, t_s = refs.pop(0), refs.pop(0)
    else:
        tiles = [[refs.pop(0) for _ in range(parts)] for _ in range(n)]
        p_in = refs.pop(0)
    cots = [refs.pop(0) for _ in range(hg)]
    wout_pieces = [refs.pop(0) for _ in range(tg)]
    scaled_in = refs.pop(0)
    g_out = [refs.pop(0) for _ in range(tg)]
    if not resident:
        p_s, t_s = refs.pop(0), refs.pop(0)
    wout_s, gt_s, grad_s, sems = refs
    cw = wout_s.shape[0]
    own = lax.axis_index("seq")
    group = own // tg
    member = own % tg
    heads = cw // head_dim
    size = rows // parts
    slots = p_s.shape[0]
    p_copies, tile_copies = [], []
    if not resident:
        p_copies = [
            pltpu.make_async_copy(
                p_in.at[k], p_s.at[k % slots], sems.at[n * parts + k % slots]
            )
            for k in range(hg)
        ]
        tile_copies = [
            pltpu.make_async_copy(
                tiles[r][i], t_s.at[pl.ds(r * rows + i * size, size), :], sems.at[r * parts + i]
            )
            for r in range(n)
            for i in range(parts)
        ]
    for copy in p_copies[:slots] + tile_copies:
        copy.start()
    wout = place_rows(wout_s, wout_pieces, member, wr)
    iota = lax.broadcasted_iota(jnp.int32, cots[0].shape, 0)
    for k in range(hg):
        position = ((group ^ k) * tg + member) * rows + iota
        masked = jnp.where(position < count[0], cots[k][...].astype(jnp.float32), 0.0)
        dout = dot_last(masked.astype(jnp.bfloat16), wout).astype(jnp.bfloat16)
        scaled = scaled_in[k * rows : (k + 1) * rows, :]
        d = (dout.astype(jnp.float32) * scaled).T.astype(jnp.bfloat16)
        if not resident:
            p_copies[k].wait()
        for h in range(heads):
            at = slice(h * head_dim, (h + 1) * head_dim)
            term = dot(d[at, :], p_s[k % slots, h])
            gt_s[at, :] = term if k == 0 else gt_s[at, :] + term
        if k + slots < hg:
            p_copies[k + slots].start()
    for copy in tile_copies:
        copy.wait()
    grad_s[...] = dot(gt_s[...].astype(jnp.bfloat16), t_s[...]).T
    first = lax.axis_index("dp") if by_dp else 0
    for tau in range(tg):
        for m in range(hg):
            to = ((group ^ m ^ first) * tg + (member ^ tau)) * wr
            to = pl.multiple_of(to, wr)
            g_out[tau][m] = grad_s[pl.ds(to, wr), :].astype(jnp.bfloat16)


def gradient_call(hg, tg, parts, rows, width, wr, cw, head_dim, by_dp):
    n = hg * tg
    keys = n * rows
    heads = cw // head_dim
    bf16 = jnp.bfloat16
    wide = bf16 if wr % 16 == 0 else jnp.float32
    resident = fits(keys)
    local = []
    if not resident:
        local = [pltpu.VMEM((1, heads, rows, keys), bf16), pltpu.VMEM((keys, width), bf16)]
    return pl.pallas_call(
        functools.partial(gradient_kernel, hg, tg, parts, rows, wr, head_dim, by_dp, resident),
        out_shape=[jax.ShapeDtypeStruct((hg, wr, cw), bf16)] * tg,
        in_specs=[SM]
        + ([VM] * 2 if resident else [ANY] * (n * parts + 1))
        + [VM] * (hg + tg + 1),
        out_specs=[VM] * tg,
        scratch_shapes=local
        + [
            pltpu.VMEM((cw, width), wide),
            pltpu.VMEM((cw, keys), jnp.float32),
            pltpu.VMEM((width, cw), jnp.float32),
            pltpu.SemaphoreType.DMA((n * parts + hg,)),
        ],
        compiler_params=pltpu.CompilerParams(vmem_limit_bytes=(40 if resident else 60) * 1024 * 1024),
    )


def local(tiles, cotangent, segment_of, tissue_count, w_query, w_key, w_value, w_out):
    rows, width = tiles.shape[1:]
    wr = w_query.shape[0]
    n = lax.axis_size("seq")
    dp = lax.axis_size("dp")
    hg = math.gcd(HEADS, n)
    tg = n // hg
    cw = width // hg
    head_dim = width // HEADS
    by_dp = dp == hg
    own = lax.axis_index("seq")
    group = own // tg
    bf16 = jnp.bfloat16

    def hop(x, step):
        return lax.ppermute(x, "seq", [(s, s ^ step) for s in range(n)])

    def over_groups(pieces):
        return [pieces[0]] + [hop(pieces[k], k * tg) for k in range(1, hg)]

    def over_members(pieces):
        return [pieces] + [[hop(x, tau) for x in pieces] for tau in range(1, tg)]

    def flat(table):
        return [table[tau][k] for tau in range(tg) for k in range(hg)]

    wide = bf16 if wr % 16 == 0 else jnp.float32
    parts = 2 if hg == 4 and rows % 32 == 0 else 1
    segment_line = segment_of.reshape(1, rows)
    packed = pl.pallas_call(
        functools.partial(pack_kernel, hg, tg, wr, cw),
        out_shape=[jax.ShapeDtypeStruct((3, wr + 8, cw), bf16)] * hg,
        in_specs=[VM] * 4,
        out_specs=[VM] * hg,
    )(w_query, w_key, w_value, segment_line)
    weight_table = over_members(over_groups(packed))
    if parts == 2:
        half = rows // 2
        upper, lower = tiles[0, :half], tiles[0, half:]
        first = [hop(upper, tg), hop(lower, tg)]
        second = [hop(upper, 2 * tg), hop(lower, 2 * tg)]
        third = [hop(first[0], 2 * tg), hop(second[1], tg)]
        tile_pieces = [[upper, lower], first, second, third]
    else:
        tile_pieces = [[x] for x in over_groups([tiles[0]] * hg)]
    tile_pieces = tile_pieces + [
        [hop(x, tau) for x in piece]
        for tau in range(1, tg)
        for piece in tile_pieces
    ]
    flat_tiles = [x for piece in tile_pieces for x in piece]
    cots = over_groups([cotangent[0]] * hg)
    wout_table = over_members(over_groups([w_out] * hg))

    results = attention_call(hg, tg, parts, rows, width, wr, cw, head_dim)(
        tissue_count, *flat_tiles, *flat(weight_table)
    )
    attention, scaled, kept = results[:hg], results[hg], results[hg + 1 :]
    if fits(n * rows):
        kept = [pltpu.with_memory_space_constraint(x, pltpu.VMEM) for x in kept]
    else:
        kept = [*flat_tiles, *kept]
    attention = over_groups(attention)
    grads = gradient_call(hg, tg, parts, rows, width, wr, cw, head_dim, by_dp)(
        tissue_count,
        *kept,
        *cots,
        *[line[0] for line in wout_table],
        scaled,
    )
    summed = grads[0].astype(jnp.float32)
    for tau in range(1, tg):
        summed = summed + hop(grads[tau], tau).astype(jnp.float32)
    summed = summed.astype(bf16)

    layer_rows = pl.pallas_call(
        functools.partial(proj_kernel, hg, tg, wr),
        out_shape=jax.ShapeDtypeStruct((1, rows, width), bf16),
        in_specs=[VM] * (hg + n),
        out_specs=VM,
        scratch_shapes=[pltpu.VMEM((hg, cw, width), wide)],
    )(*attention, *flat(wout_table))

    if by_dp:
        own_dp = lax.axis_index("dp")
        mine = summed[0].astype(jnp.float32)
        for m in range(1, hg):
            got = lax.ppermute(summed[m], "dp", [(z, z ^ m) for z in range(dp)])
            mine = mine + got.astype(jnp.float32)
        mine = mine.astype(bf16)
        pieces = []
        for m in range(dp):
            pairs = [
                (z * n + s, (z ^ m) * n + (s ^ (z * tg))) for z in range(dp) for s in range(n)
            ]
            pieces.append(lax.ppermute(mine, ("dp", "seq"), pairs))
        index = group ^ own_dp
    else:
        total = lax.psum(summed, "dp")
        pieces = over_groups([total[k] for k in range(hg)])
        index = group
    columns = []
    for p in range(hg):
        piece = pieces[0]
        for m in range(1, hg):
            piece = jnp.where((index ^ p) == m, pieces[m], piece)
        columns.append(piece)
    return (layer_rows, jnp.concatenate(columns, axis=1).astype(jnp.float32))


def solution(mesh):
    placed = (
        P("dp", "seq", None),
        P("dp", "seq", None),
        P("dp", "seq", None),
        P("dp"),
        P("seq", None),
        P("seq", None),
        P("seq", None),
        P("seq", None),
    )
    return jax.shard_map(
        local,
        mesh=mesh,
        in_specs=placed,
        out_specs=(P("dp", "seq", None), P("seq", None)),
        check_vma=False,
    )
```

```python
import functools
import math

import jax
import jax.numpy as jnp
from jax import lax
from jax.experimental import pallas as pl
from jax.experimental.pallas import tpu as pltpu
from jax.sharding import PartitionSpec as P


HEADS = 12
NEG_BIG = -1e30
LOG2E = 1.4426950408889634


VM = pl.BlockSpec(memory_space=pltpu.VMEM)
ANY = pl.BlockSpec(memory_space=pl.ANY)
SM = pl.BlockSpec(memory_space=pltpu.SMEM)


def dot_last(a, b):
    return lax.dot_general(a, b, (((1,), (1,)), ((), ())), preferred_element_type=jnp.float32)


def dot(a, b):
    return lax.dot_general(a, b, (((1,), (0,)), ((), ())), preferred_element_type=jnp.float32)


def pack_kernel(hg, tg, wr, cw, wq, wk, wv, seg, *outs):
    group = lax.axis_index("seq") // tg
    for k in range(hg):
        for part in range(hg):

            @pl.when((group ^ k) == part)
            def _():
                cols = slice(part * cw, (part + 1) * cw)
                outs[k][0, :wr] = wq[:, cols]
                outs[k][1, :wr] = wk[:, cols]
                outs[k][2, :wr] = wv[:, cols]

        for i in range(3):
            outs[k][i, wr:] = jnp.broadcast_to(seg[...], (8, cw)).astype(jnp.bfloat16)


def place_rows(scratch, pieces, member, wr):
    for tau, piece in enumerate(pieces):
        to = pl.multiple_of((member ^ tau) * wr, wr)
        scratch[pl.ds(to, wr), :] = piece[...].astype(scratch.dtype)
    return scratch[...].astype(jnp.bfloat16)


def proj_kernel(hg, tg, wr, *refs):
    n = hg * tg
    attention, pieces, out, wout = refs[:hg], refs[hg : hg + n], refs[hg + n], refs[hg + n + 1]
    member = lax.axis_index("seq") % tg
    total = None
    for k in range(hg):
        block = place_rows(wout.at[k], pieces[k::hg], member, wr)
        term = dot(attention[k][...], block)
        total = term if total is None else total + term
    out[0] = total.astype(jnp.bfloat16)


def attention_kernel(hg, tg, parts, rows, wr, head_dim, resident, count, *refs):
    n = hg * tg
    refs = list(refs)
    tiles = [[refs.pop(0) for _ in range(parts)] for _ in range(n)]
    packed = [refs.pop(0) for _ in range(n)]
    o_out = [refs.pop(0) for _ in range(hg)]
    scaled_out, p_out = refs.pop(0), refs.pop(0)
    if resident:
        p_s, t_s = p_out, refs.pop(0)
    else:
        p_s, t_s = refs.pop(0), refs.pop(0)
    if not resident:
        wp_s = refs.pop(0)
    w_s, seg_s, col_s, q_s, k_s, v_s, bias_s, o_s, sems = refs
    cw = q_s.shape[1]
    own = lax.axis_index("seq")
    group = own // tg
    member = own % tg
    keys = n * rows
    heads = cw // head_dim
    size = rows // parts
    if not resident:
        packed_copies = [
            pltpu.make_async_copy(packed[r], wp_s.at[r], sems.at[n * parts + r]) for r in range(n)
        ]
        tile_copies = [
            pltpu.make_async_copy(
                tiles[r][i], t_s.at[pl.ds(r * rows + i * size, size), :], sems.at[r * parts + i]
            )
            for r in range(n)
            for i in range(parts)
        ]
        for copy in packed_copies + tile_copies:
            copy.start()
    for tau in range(tg):
        for k in range(hg):
            r = tau * hg + k
            piece = packed[r]
            if not resident:
                packed_copies[r].wait()
                piece = wp_s.at[r]
            source = (group ^ k) * tg + (member ^ tau)
            to = pl.multiple_of(source * wr, wr)
            for i in range(3):
                w_s[i, pl.ds(to, wr), :] = piece[i, :wr].astype(w_s.dtype)
            line = piece[0, wr : wr + 8, :].astype(jnp.float32)[:1]
            at = source * rows + lax.broadcasted_iota(jnp.int32, (1, rows), 1)
            columns = slice(r * rows, (r + 1) * rows)
            seg_s[0:1, columns] = line
            seg_s[1:2, columns] = jnp.where(at < count[0], line, -1.0)
    for r in range(n):
        for i in range(parts):
            if resident:
                t_s[r * rows + i * size : r * rows + (i + 1) * size, :] = tiles[r][i][...]
            else:
                tile_copies[r * parts + i].wait()
    for tau in range(tg):
        at = slice(tau * hg * rows, (tau + 1) * hg * rows)
        block = t_s[at, :]
        if tau == 0:
            q_s[at, :] = dot(block, w_s[0].astype(jnp.bfloat16)).astype(jnp.bfloat16)
        k_s[at, :] = dot(block, w_s[1].astype(jnp.bfloat16)).astype(jnp.bfloat16)
        v_s[at, :] = dot(block, w_s[2].astype(jnp.bfloat16)).astype(jnp.bfloat16)
    scale = head_dim ** (-0.5) * LOG2E
    lane_head = lax.broadcasted_iota(jnp.int32, (rows, cw), 1) // head_dim
    label = seg_s[1:2, :]
    square_row = lax.broadcasted_iota(jnp.int32, (rows, rows), 0)
    square_col = lax.broadcasted_iota(jnp.int32, (rows, rows), 1)
    column = lax.broadcasted_iota(jnp.int32, (1, keys), 1)
    row_at = lax.broadcasted_iota(jnp.int32, (rows, keys), 0)
    col_at = lax.broadcasted_iota(jnp.int32, (rows, keys), 1)
    slots = p_s.shape[0]

    def p_copy(k):
        slot = k % slots
        return pltpu.make_async_copy(p_s.at[slot], p_out.at[k], sems.at[n * parts + n + slot])

    def chunk(k, carry):
        start = k * rows if isinstance(k, int) else pl.multiple_of(k * rows, rows)
        at = pl.ds(start, rows)
        slot = k % slots
        segment = col_s[k]
        in_block = (column >= start) & (column < start + rows) & (label >= 0.0)
        same_value = jnp.where(in_block, 1.0, 0.0)
        other_value = jnp.where(in_block, 0.0, NEG_BIG)
        bias = jnp.where(segment == label, same_value, other_value)
        bias_s[...] = jnp.where(row_at + start == col_at, 1.0, bias)
        q = q_s[at, :]
        scaled = jnp.zeros((rows, cw), jnp.float32)
        if slots < hg:

            @pl.when(k >= slots)
            def _():
                p_copy(k - slots).wait()

        for h in range(heads):
            qh = jnp.where(lane_head == h, q, jnp.zeros_like(q))
            s = dot_last(qh, k_s[...]) * scale + bias_s[...]
            top = jnp.max(s, axis=1, keepdims=True)
            p = jnp.exp2(s - top)
            total = jnp.sum(p, axis=1, keepdims=True)
            p_s[slot, h] = p.astype(jnp.bfloat16)
            scaled = jnp.where(lane_head == h, 1.0 / total, scaled)
        if not resident:
            p_copy(k).start()
        acc = jnp.zeros((rows, cw), jnp.float32)
        for h in range(heads):
            acc = jnp.where(lane_head == h, dot(p_s[slot, h], v_s[...]), acc)
        scaled_out[at, :] = scaled
        o_s[at, :] = (acc * scaled).astype(jnp.bfloat16)
        return carry

    for k in range(hg):
        line = jnp.where(square_row == square_col, seg_s[0:1, k * rows : (k + 1) * rows], 0.0)
        col_s[k] = jnp.sum(line, axis=1, keepdims=True)
    if slots == hg:
        for k in range(hg):
            chunk(k, 0)
    else:
        lax.fori_loop(0, hg, chunk, 0)
    for k in range(hg):
        o_out[k][...] = o_s[k * rows : (k + 1) * rows, :]
    for k in range(hg - slots, hg):
        if not resident:
            p_copy(k).wait()


def fits(keys):
    return keys <= 2048


def attention_call(hg, tg, parts, rows, width, wr, cw, head_dim):
    n = hg * tg
    keys = n * rows
    heads = cw // head_dim
    bf16 = jnp.bfloat16
    wide = bf16 if wr % 16 == 0 else jnp.float32
    resident = fits(keys)
    if resident:
        kept = [pltpu.VMEM((hg, heads, rows, keys), bf16), pltpu.VMEM((keys, width), bf16)]
        local = []
    else:
        kept = [jax.ShapeDtypeStruct((hg, heads, rows, keys), bf16)]
        local = [
            pltpu.VMEM((1, heads, rows, keys), bf16),
            pltpu.VMEM((keys, width), bf16),
            pltpu.VMEM((n, 3, wr + 8, cw), bf16),
        ]
    return pl.pallas_call(
        functools.partial(attention_kernel, hg, tg, parts, rows, wr, head_dim, resident),
        out_shape=[jax.ShapeDtypeStruct((rows, cw), bf16)] * hg
        + [jax.ShapeDtypeStruct((hg * rows, cw), jnp.float32)]
        + kept,
        in_specs=[SM] + [VM if resident else ANY] * (n * parts + n),
        out_specs=[VM] * (hg + 1) + [VM if resident else ANY] * len(kept),
        scratch_shapes=local
        + [
            pltpu.VMEM((3, width, cw), wide),
            pltpu.VMEM((8, keys), jnp.float32),
            pltpu.VMEM((hg, rows, 1), jnp.float32),
            pltpu.VMEM((hg * rows, cw), bf16),
            pltpu.VMEM((keys, cw), bf16),
            pltpu.VMEM((keys, cw), bf16),
            pltpu.VMEM((rows, keys), jnp.float32),
            pltpu.VMEM((hg * rows, cw), bf16),
            pltpu.SemaphoreType.DMA((n * parts + n + hg,)),
        ],
        compiler_params=pltpu.CompilerParams(vmem_limit_bytes=(40 if resident else 60) * 1024 * 1024),
    )


def gradient_kernel(hg, tg, parts, rows, wr, head_dim, by_dp, resident, count, *refs):
    n = hg * tg
    refs = list(refs)
    if resident:
        p_s, t_s = refs.pop(0), refs.pop(0)
    else:
        tiles = [[refs.pop(0) for _ in range(parts)] for _ in range(n)]
        p_in = refs.pop(0)
    cots = [refs.pop(0) for _ in range(hg)]
    wout_pieces = [refs.pop(0) for _ in range(tg)]
    scaled_in = refs.pop(0)
    g_out = [refs.pop(0) for _ in range(tg)]
    if not resident:
        p_s, t_s = refs.pop(0), refs.pop(0)
    wout_s, gt_s, grad_s, sems = refs
    cw = wout_s.shape[0]
    own = lax.axis_index("seq")
    group = own // tg
    member = own % tg
    heads = cw // head_dim
    size = rows // parts
    slots = p_s.shape[0]
    p_copies, tile_copies = [], []
    if not resident:
        p_copies = [
            pltpu.make_async_copy(
                p_in.at[k], p_s.at[k % slots], sems.at[n * parts + k % slots]
            )
            for k in range(hg)
        ]
        tile_copies = [
            pltpu.make_async_copy(
                tiles[r][i], t_s.at[pl.ds(r * rows + i * size, size), :], sems.at[r * parts + i]
            )
            for r in range(n)
            for i in range(parts)
        ]
    for copy in p_copies[:slots] + tile_copies:
        copy.start()
    wout = place_rows(wout_s, wout_pieces, member, wr)
    iota = lax.broadcasted_iota(jnp.int32, cots[0].shape, 0)
    for k in range(hg):
        position = ((group ^ k) * tg + member) * rows + iota
        masked = jnp.where(position < count[0], cots[k][...].astype(jnp.float32), 0.0)
        dout = dot_last(masked.astype(jnp.bfloat16), wout).astype(jnp.bfloat16)
        scaled = scaled_in[k * rows : (k + 1) * rows, :]
        d = (dout.astype(jnp.float32) * scaled).T.astype(jnp.bfloat16)
        if not resident:
            p_copies[k].wait()
        for h in range(heads):
            at = slice(h * head_dim, (h + 1) * head_dim)
            term = dot(d[at, :], p_s[k % slots, h])
            gt_s[at, :] = term if k == 0 else gt_s[at, :] + term
        if k + slots < hg:
            p_copies[k + slots].start()
    for copy in tile_copies:
        copy.wait()
    grad_s[...] = dot(gt_s[...].astype(jnp.bfloat16), t_s[...]).T
    first = lax.axis_index("dp") if by_dp else 0
    for tau in range(tg):
        for m in range(hg):
            to = ((group ^ m ^ first) * tg + (member ^ tau)) * wr
            to = pl.multiple_of(to, wr)
            g_out[tau][m] = grad_s[pl.ds(to, wr), :].astype(jnp.bfloat16)


def gradient_call(hg, tg, parts, rows, width, wr, cw, head_dim, by_dp):
    n = hg * tg
    keys = n * rows
    heads = cw // head_dim
    bf16 = jnp.bfloat16
    wide = bf16 if wr % 16 == 0 else jnp.float32
    resident = fits(keys)
    local = []
    if not resident:
        local = [pltpu.VMEM((1, heads, rows, keys), bf16), pltpu.VMEM((keys, width), bf16)]
    return pl.pallas_call(
        functools.partial(gradient_kernel, hg, tg, parts, rows, wr, head_dim, by_dp, resident),
        out_shape=[jax.ShapeDtypeStruct((hg, wr, cw), bf16)] * tg,
        in_specs=[SM]
        + ([VM] * 2 if resident else [ANY] * (n * parts + 1))
        + [VM] * (hg + tg + 1),
        out_specs=[VM] * tg,
        scratch_shapes=local
        + [
            pltpu.VMEM((cw, width), wide),
            pltpu.VMEM((cw, keys), jnp.float32),
            pltpu.VMEM((width, cw), jnp.float32),
            pltpu.SemaphoreType.DMA((n * parts + hg,)),
        ],
        compiler_params=pltpu.CompilerParams(vmem_limit_bytes=(40 if resident else 60) * 1024 * 1024),
    )


def local(tiles, cotangent, segment_of, tissue_count, w_query, w_key, w_value, w_out):
    rows, width = tiles.shape[1:]
    wr = w_query.shape[0]
    n = lax.axis_size("seq")
    dp = lax.axis_size("dp")
    hg = math.gcd(HEADS, n)
    tg = n // hg
    cw = width // hg
    head_dim = width // HEADS
    by_dp = dp == hg
    own = lax.axis_index("seq")
    group = own // tg
    bf16 = jnp.bfloat16

    def hop(x, step):
        return lax.ppermute(x, "seq", [(s, s ^ step) for s in range(n)])

    def over_groups(pieces):
        return [pieces[0]] + [hop(pieces[k], k * tg) for k in range(1, hg)]

    def over_members(pieces):
        return [pieces] + [[hop(x, tau) for x in pieces] for tau in range(1, tg)]

    def flat(table):
        return [table[tau][k] for tau in range(tg) for k in range(hg)]

    wide = bf16 if wr % 16 == 0 else jnp.float32
    parts = 2 if hg == 4 and rows % 32 == 0 else 1
    segment_line = segment_of.reshape(1, rows)
    packed = pl.pallas_call(
        functools.partial(pack_kernel, hg, tg, wr, cw),
        out_shape=[jax.ShapeDtypeStruct((3, wr + 8, cw), bf16)] * hg,
        in_specs=[VM] * 4,
        out_specs=[VM] * hg,
    )(w_query, w_key, w_value, segment_line)
    weight_table = over_members(over_groups(packed))
    if parts == 2:
        half = rows // 2
        upper, lower = tiles[0, :half], tiles[0, half:]
        first = [hop(upper, tg), hop(lower, tg)]
        second = [hop(upper, 2 * tg), hop(lower, 2 * tg)]
        third = [hop(first[0], 2 * tg), hop(second[1], tg)]
        tile_pieces = [[upper, lower], first, second, third]
    else:
        tile_pieces = [[x] for x in over_groups([tiles[0]] * hg)]
    tile_pieces = tile_pieces + [
        [hop(x, tau) for x in piece]
        for tau in range(1, tg)
        for piece in tile_pieces
    ]
    flat_tiles = [x for piece in tile_pieces for x in piece]
    cots = over_groups([cotangent[0]] * hg)
    wout_table = over_members(over_groups([w_out] * hg))

    def near_core(arrays):
        if not fits(n * rows):
            return arrays
        return [pltpu.with_memory_space_constraint(x, pltpu.VMEM) for x in arrays]

    results = attention_call(hg, tg, parts, rows, width, wr, cw, head_dim)(
        tissue_count, *near_core(flat_tiles), *near_core(flat(weight_table))
    )
    attention, scaled, kept = results[:hg], results[hg], results[hg + 1 :]
    if not fits(n * rows):
        kept = [*flat_tiles, *kept]
    attention = over_groups(attention)
    grads = gradient_call(hg, tg, parts, rows, width, wr, cw, head_dim, by_dp)(
        tissue_count,
        *near_core(kept),
        *near_core(cots),
        *near_core([line[0] for line in wout_table]),
        *near_core([scaled]),
    )
    summed = grads[0].astype(jnp.float32)
    for tau in range(1, tg):
        summed = summed + hop(grads[tau], tau).astype(jnp.float32)
    summed = summed.astype(bf16)

    layer_rows = pl.pallas_call(
        functools.partial(proj_kernel, hg, tg, wr),
        out_shape=jax.ShapeDtypeStruct((1, rows, width), bf16),
        in_specs=[VM] * (hg + n),
        out_specs=VM,
        scratch_shapes=[pltpu.VMEM((hg, cw, width), wide)],
    )(*near_core(attention), *near_core(flat(wout_table)))

    if by_dp:
        own_dp = lax.axis_index("dp")
        mine = summed[0].astype(jnp.float32)
        for m in range(1, hg):
            got = lax.ppermute(summed[m], "dp", [(z, z ^ m) for z in range(dp)])
            mine = mine + got.astype(jnp.float32)
        mine = mine.astype(bf16)
        pieces = []
        for m in range(dp):
            pairs = [
                (z * n + s, (z ^ m) * n + (s ^ (z * tg))) for z in range(dp) for s in range(n)
            ]
            pieces.append(lax.ppermute(mine, ("dp", "seq"), pairs))
        index = group ^ own_dp
    else:
        total = lax.psum(summed, "dp")
        pieces = over_groups([total[k] for k in range(hg)])
        index = group
    columns = []
    for p in range(hg):
        piece = pieces[0]
        for m in range(1, hg):
            piece = jnp.where((index ^ p) == m, pieces[m], piece)
        columns.append(piece)
    return (layer_rows, jnp.concatenate(columns, axis=1).astype(jnp.float32))


def solution(mesh):
    placed = (
        P("dp", "seq", None),
        P("dp", "seq", None),
        P("dp", "seq", None),
        P("dp"),
        P("seq", None),
        P("seq", None),
        P("seq", None),
        P("seq", None),
    )
    return jax.shard_map(
        local,
        mesh=mesh,
        in_specs=placed,
        out_specs=(P("dp", "seq", None), P("seq", None)),
        check_vma=False,
    )
```

```python
import functools
import math

import jax
import jax.numpy as jnp
from jax import lax
from jax.experimental import pallas as pl
from jax.experimental.pallas import tpu as pltpu
from jax.sharding import PartitionSpec as P


HEADS = 12
NEG_BIG = -1e30
LOG2E = 1.4426950408889634


SMALL = pltpu.CompilerParams(vmem_limit_bytes=16 * 1024 * 1024)
VM = pl.BlockSpec(memory_space=pltpu.VMEM)
ANY = pl.BlockSpec(memory_space=pl.ANY)
SM = pl.BlockSpec(memory_space=pltpu.SMEM)


def dot_last(a, b):
    return lax.dot_general(a, b, (((1,), (1,)), ((), ())), preferred_element_type=jnp.float32)


def dot(a, b):
    return lax.dot_general(a, b, (((1,), (0,)), ((), ())), preferred_element_type=jnp.float32)


def pack_kernel(hg, tg, wr, cw, wq, wk, wv, seg, *outs):
    group = lax.axis_index("seq") // tg
    for k in range(hg):
        for part in range(hg):

            @pl.when((group ^ k) == part)
            def _():
                cols = slice(part * cw, (part + 1) * cw)
                outs[k][0, :wr] = wq[:, cols]
                outs[k][1, :wr] = wk[:, cols]
                outs[k][2, :wr] = wv[:, cols]

        for i in range(3):
            outs[k][i, wr:] = jnp.broadcast_to(seg[...], (8, cw)).astype(jnp.bfloat16)


def merge_kernel(rows, count, cot, *refs):
    merged = refs[-1]
    position = lax.axis_index("seq") * rows + lax.broadcasted_iota(jnp.int32, cot.shape, 0)
    masked = jnp.where(position < count[0], cot[...].astype(jnp.float32), 0.0)
    merged[:rows, :] = masked.astype(jnp.bfloat16)
    if len(refs) == 2:
        merged[rows:, :] = refs[0][...]


def place_rows(scratch, pieces, member, wr):
    for tau, piece in enumerate(pieces):
        to = pl.multiple_of((member ^ tau) * wr, wr)
        last = piece.shape[0]
        scratch[pl.ds(to, wr), :] = piece[last - wr : last, :].astype(scratch.dtype)
    return scratch[...].astype(jnp.bfloat16)


def proj_kernel(hg, tg, wr, *refs):
    n = hg * tg
    attention, pieces, out, wout = refs[:hg], refs[hg : hg + n], refs[hg + n], refs[hg + n + 1]
    member = lax.axis_index("seq") % tg
    total = None
    for k in range(hg):
        block = place_rows(wout.at[k], pieces[k::hg], member, wr)
        term = dot(attention[k][...], block)
        total = term if total is None else total + term
    out[0] = total.astype(jnp.bfloat16)


def attention_kernel(hg, tg, parts, rows, wr, head_dim, resident, count, *refs):
    n = hg * tg
    refs = list(refs)
    tiles = [[refs.pop(0) for _ in range(parts)] for _ in range(n)]
    packed = [refs.pop(0) for _ in range(n)]
    o_out = [refs.pop(0) for _ in range(hg)]
    scaled_out, p_out = refs.pop(0), refs.pop(0)
    if resident:
        p_s, t_s = p_out, refs.pop(0)
    else:
        p_s, t_s = refs.pop(0), refs.pop(0)
    if not resident:
        wp_s = refs.pop(0)
    w_s, seg_s, col_s, q_s, k_s, v_s, bias_s, o_s, sems = refs
    cw = q_s.shape[1]
    own = lax.axis_index("seq")
    group = own // tg
    member = own % tg
    keys = n * rows
    heads = cw // head_dim
    size = rows // parts
    if not resident:
        packed_copies = [
            pltpu.make_async_copy(packed[r], wp_s.at[r], sems.at[n * parts + r]) for r in range(n)
        ]
        tile_copies = [
            pltpu.make_async_copy(
                tiles[r][i], t_s.at[pl.ds(r * rows + i * size, size), :], sems.at[r * parts + i]
            )
            for r in range(n)
            for i in range(parts)
        ]
        for copy in packed_copies + tile_copies:
            copy.start()
    for tau in range(tg):
        for k in range(hg):
            r = tau * hg + k
            piece = packed[r]
            if not resident:
                packed_copies[r].wait()
                piece = wp_s.at[r]
            source = (group ^ k) * tg + (member ^ tau)
            to = pl.multiple_of(source * wr, wr)
            for i in range(3):
                w_s[i, pl.ds(to, wr), :] = piece[i, :wr].astype(w_s.dtype)
            line = piece[0, wr : wr + 8, :].astype(jnp.float32)[:1]
            at = source * rows + lax.broadcasted_iota(jnp.int32, (1, rows), 1)
            columns = slice(r * rows, (r + 1) * rows)
            seg_s[0:1, columns] = line
            seg_s[1:2, columns] = jnp.where(at < count[0], line, -1.0)
    for r in range(n):
        for i in range(parts):
            if resident:
                t_s[r * rows + i * size : r * rows + (i + 1) * size, :] = tiles[r][i][...]
            else:
                tile_copies[r * parts + i].wait()
    for tau in range(tg):
        at = slice(tau * hg * rows, (tau + 1) * hg * rows)
        block = t_s[at, :]
        if tau == 0:
            q_s[at, :] = dot(block, w_s[0].astype(jnp.bfloat16)).astype(jnp.bfloat16)
        k_s[at, :] = dot(block, w_s[1].astype(jnp.bfloat16)).astype(jnp.bfloat16)
        v_s[at, :] = dot(block, w_s[2].astype(jnp.bfloat16)).astype(jnp.bfloat16)
    scale = head_dim ** (-0.5) * LOG2E
    lane_head = lax.broadcasted_iota(jnp.int32, (rows, cw), 1) // head_dim
    label = seg_s[1:2, :]
    square_row = lax.broadcasted_iota(jnp.int32, (rows, rows), 0)
    square_col = lax.broadcasted_iota(jnp.int32, (rows, rows), 1)
    column = lax.broadcasted_iota(jnp.int32, (1, keys), 1)
    row_at = lax.broadcasted_iota(jnp.int32, (rows, keys), 0)
    col_at = lax.broadcasted_iota(jnp.int32, (rows, keys), 1)
    slots = p_s.shape[0]

    def p_copy(k):
        slot = k % slots
        return pltpu.make_async_copy(p_s.at[slot], p_out.at[k], sems.at[n * parts + n + slot])

    def chunk(k, carry):
        start = k * rows if isinstance(k, int) else pl.multiple_of(k * rows, rows)
        at = pl.ds(start, rows)
        slot = k % slots
        segment = col_s[k]
        in_block = (column >= start) & (column < start + rows) & (label >= 0.0)
        same_value = jnp.where(in_block, 1.0, 0.0)
        other_value = jnp.where(in_block, 0.0, NEG_BIG)
        bias = jnp.where(segment == label, same_value, other_value)
        bias_s[...] = jnp.where(row_at + start == col_at, 1.0, bias)
        q = q_s[at, :]
        scaled = jnp.zeros((rows, cw), jnp.float32)
        if slots < hg:

            @pl.when(k >= slots)
            def _():
                p_copy(k - slots).wait()

        for h in range(heads):
            qh = jnp.where(lane_head == h, q, jnp.zeros_like(q))
            s = dot_last(qh, k_s[...]) * scale + bias_s[...]
            top = jnp.max(s, axis=1, keepdims=True)
            p = jnp.exp2(s - top)
            total = jnp.sum(p, axis=1, keepdims=True)
            p_s[slot, h] = p.astype(jnp.bfloat16)
            scaled = jnp.where(lane_head == h, 1.0 / total, scaled)
        if not resident:
            p_copy(k).start()
        acc = jnp.zeros((rows, cw), jnp.float32)
        for h in range(heads):
            acc = jnp.where(lane_head == h, dot(p_s[slot, h], v_s[...]), acc)
        scaled_out[at, :] = scaled
        o_s[at, :] = (acc * scaled).astype(jnp.bfloat16)
        return carry

    for k in range(hg):
        line = jnp.where(square_row == square_col, seg_s[0:1, k * rows : (k + 1) * rows], 0.0)
        col_s[k] = jnp.sum(line, axis=1, keepdims=True)
    if slots == hg:
        for k in range(hg):
            chunk(k, 0)
    else:
        lax.fori_loop(0, hg, chunk, 0)
    for k in range(hg):
        o_out[k][...] = o_s[k * rows : (k + 1) * rows, :]
    for k in range(hg - slots, hg):
        if not resident:
            p_copy(k).wait()


def fits(keys):
    return keys <= 2048


def attention_call(hg, tg, parts, rows, width, wr, cw, head_dim):
    n = hg * tg
    keys = n * rows
    heads = cw // head_dim
    bf16 = jnp.bfloat16
    wide = bf16 if wr % 16 == 0 else jnp.float32
    resident = fits(keys)
    if resident:
        kept = [pltpu.VMEM((hg, heads, rows, keys), bf16), pltpu.VMEM((keys, width), bf16)]
        local = []
    else:
        kept = [jax.ShapeDtypeStruct((hg, heads, rows, keys), bf16)]
        local = [
            pltpu.VMEM((1, heads, rows, keys), bf16),
            pltpu.VMEM((keys, width), bf16),
            pltpu.VMEM((n, 3, wr + 8, cw), bf16),
        ]
    return pl.pallas_call(
        functools.partial(attention_kernel, hg, tg, parts, rows, wr, head_dim, resident),
        out_shape=[jax.ShapeDtypeStruct((rows, cw), bf16)] * hg
        + [jax.ShapeDtypeStruct((hg * rows, cw), jnp.float32)]
        + kept,
        in_specs=[SM] + [VM if resident else ANY] * (n * parts + n),
        out_specs=[VM] * (hg + 1) + [VM if resident else ANY] * len(kept),
        scratch_shapes=local
        + [
            pltpu.VMEM((3, width, cw), wide),
            pltpu.VMEM((8, keys), jnp.float32),
            pltpu.VMEM((hg, rows, 1), jnp.float32),
            pltpu.VMEM((hg * rows, cw), bf16),
            pltpu.VMEM((keys, cw), bf16),
            pltpu.VMEM((keys, cw), bf16),
            pltpu.VMEM((rows, keys), jnp.float32),
            pltpu.VMEM((hg * rows, cw), bf16),
            pltpu.SemaphoreType.DMA((n * parts + n + hg,)),
        ],
        compiler_params=pltpu.CompilerParams(vmem_limit_bytes=(30 if resident else 60) * 1024 * 1024),
    )


def gradient_kernel(hg, tg, parts, rows, wr, head_dim, by_dp, resident, *refs):
    n = hg * tg
    refs = list(refs)
    if resident:
        p_s, t_s = refs.pop(0), refs.pop(0)
    else:
        tiles = [[refs.pop(0) for _ in range(parts)] for _ in range(n)]
        p_in = refs.pop(0)
    cots = [refs.pop(0) for _ in range(hg)]
    wout_pieces = [refs.pop(0) for _ in range(tg)]
    scaled_in = refs.pop(0)
    g_out = [refs.pop(0) for _ in range(tg)]
    if not resident:
        p_s, t_s = refs.pop(0), refs.pop(0)
    wout_s, gt_s, grad_s, sems = refs
    cw = wout_s.shape[0]
    own = lax.axis_index("seq")
    group = own // tg
    member = own % tg
    heads = cw // head_dim
    size = rows // parts
    slots = p_s.shape[0]
    p_copies, tile_copies = [], []
    if not resident:
        p_copies = [
            pltpu.make_async_copy(
                p_in.at[k], p_s.at[k % slots], sems.at[n * parts + k % slots]
            )
            for k in range(hg)
        ]
        tile_copies = [
            pltpu.make_async_copy(
                tiles[r][i], t_s.at[pl.ds(r * rows + i * size, size), :], sems.at[r * parts + i]
            )
            for r in range(n)
            for i in range(parts)
        ]
    for copy in p_copies[:slots] + tile_copies:
        copy.start()
    wout = place_rows(wout_s, wout_pieces, member, wr)
    for k in range(hg):
        dout = dot_last(cots[k][:rows, :], wout).astype(jnp.bfloat16)
        scaled = scaled_in[k * rows : (k + 1) * rows, :]
        d = (dout.astype(jnp.float32) * scaled).T.astype(jnp.bfloat16)
        if not resident:
            p_copies[k].wait()
        for h in range(heads):
            at = slice(h * head_dim, (h + 1) * head_dim)
            term = dot(d[at, :], p_s[k % slots, h])
            gt_s[at, :] = term if k == 0 else gt_s[at, :] + term
        if k + slots < hg:
            p_copies[k + slots].start()
    for copy in tile_copies:
        copy.wait()
    grad_s[...] = dot(gt_s[...].astype(jnp.bfloat16), t_s[...]).T
    first = lax.axis_index("dp") if by_dp else 0
    for tau in range(tg):
        for m in range(hg):
            to = ((group ^ m ^ first) * tg + (member ^ tau)) * wr
            to = pl.multiple_of(to, wr)
            g_out[tau][m] = grad_s[pl.ds(to, wr), :].astype(jnp.bfloat16)


def gradient_call(hg, tg, parts, rows, width, wr, cw, head_dim, by_dp):
    n = hg * tg
    keys = n * rows
    heads = cw // head_dim
    bf16 = jnp.bfloat16
    wide = bf16 if wr % 16 == 0 else jnp.float32
    resident = fits(keys)
    local = []
    if not resident:
        local = [pltpu.VMEM((1, heads, rows, keys), bf16), pltpu.VMEM((keys, width), bf16)]
    return pl.pallas_call(
        functools.partial(gradient_kernel, hg, tg, parts, rows, wr, head_dim, by_dp, resident),
        out_shape=[jax.ShapeDtypeStruct((hg, wr, cw), bf16)] * tg,
        in_specs=([VM] * 2 if resident else [ANY] * (n * parts + 1))
        + [VM] * (hg + tg + 1),
        out_specs=[VM] * tg,
        scratch_shapes=local
        + [
            pltpu.VMEM((cw, width), wide),
            pltpu.VMEM((cw, keys), jnp.float32),
            pltpu.VMEM((width, cw), jnp.float32),
            pltpu.SemaphoreType.DMA((n * parts + hg,)),
        ],
        compiler_params=pltpu.CompilerParams(vmem_limit_bytes=(30 if resident else 60) * 1024 * 1024),
    )


def local(tiles, cotangent, segment_of, tissue_count, w_query, w_key, w_value, w_out):
    rows, width = tiles.shape[1:]
    wr = w_query.shape[0]
    n = lax.axis_size("seq")
    dp = lax.axis_size("dp")
    hg = math.gcd(HEADS, n)
    tg = n // hg
    cw = width // hg
    head_dim = width // HEADS
    by_dp = dp == hg
    own = lax.axis_index("seq")
    group = own // tg
    bf16 = jnp.bfloat16

    def hop(x, step):
        return lax.ppermute(x, "seq", [(s, s ^ step) for s in range(n)])

    def over_groups(pieces):
        return [pieces[0]] + [hop(pieces[k], k * tg) for k in range(1, hg)]

    def over_members(pieces):
        return [pieces] + [[hop(x, tau) for x in pieces] for tau in range(1, tg)]

    def flat(table):
        return [table[tau][k] for tau in range(tg) for k in range(hg)]

    wide = bf16 if wr % 16 == 0 else jnp.float32
    parts = 2 if hg == 4 and rows % 32 == 0 else 1
    segment_line = segment_of.reshape(1, rows)
    packed = pl.pallas_call(
        functools.partial(pack_kernel, hg, tg, wr, cw),
        out_shape=[jax.ShapeDtypeStruct((3, wr + 8, cw), bf16)] * hg,
        in_specs=[VM] * 4,
        out_specs=[VM] * hg,
    )(w_query, w_key, w_value, segment_line)
    weight_table = over_members(over_groups(packed))
    if parts == 2:
        half = rows // 2
        upper, lower = tiles[0, :half], tiles[0, half:]
        first = [hop(upper, tg), hop(lower, tg)]
        second = [hop(upper, 2 * tg), hop(lower, 2 * tg)]
        third = [hop(first[0], 2 * tg), hop(second[1], tg)]
        tile_pieces = [[upper, lower], first, second, third]
    else:
        tile_pieces = [[x] for x in over_groups([tiles[0]] * hg)]
    tile_pieces = tile_pieces + [
        [hop(x, tau) for x in piece]
        for tau in range(1, tg)
        for piece in tile_pieces
    ]
    flat_tiles = [x for piece in tile_pieces for x in piece]
    joined = fits(n * rows)
    merged = pl.pallas_call(
        functools.partial(merge_kernel, rows),
        out_shape=jax.ShapeDtypeStruct((rows + wr if joined else rows, width), bf16),
        in_specs=[SM] + [VM] * (2 if joined else 1),
        out_specs=VM,
    )(tissue_count, cotangent[0], *([w_out] if joined else []))
    cots = over_groups([merged] * hg)
    if joined:
        wout_table = over_members(cots)
    else:
        wout_table = over_members(over_groups([w_out] * hg))

    def near_core(arrays):
        if not fits(n * rows):
            return arrays
        return [pltpu.with_memory_space_constraint(x, pltpu.VMEM) for x in arrays]

    results = attention_call(hg, tg, parts, rows, width, wr, cw, head_dim)(
        tissue_count, *near_core(flat_tiles), *near_core(flat(weight_table))
    )
    attention, scaled, kept = results[:hg], results[hg], results[hg + 1 :]
    if not fits(n * rows):
        kept = [*flat_tiles, *kept]
    attention = over_groups(attention)
    grads = gradient_call(hg, tg, parts, rows, width, wr, cw, head_dim, by_dp)(
        *near_core(kept),
        *near_core(cots),
        *near_core([line[0] for line in wout_table]),
        *near_core([scaled]),
    )
    summed = grads[0].astype(jnp.float32)
    for tau in range(1, tg):
        summed = summed + hop(grads[tau], tau).astype(jnp.float32)
    summed = summed.astype(bf16)

    layer_rows = pl.pallas_call(
        functools.partial(proj_kernel, hg, tg, wr),
        out_shape=jax.ShapeDtypeStruct((1, rows, width), bf16),
        in_specs=[VM] * (hg + n),
        out_specs=VM,
        scratch_shapes=[pltpu.VMEM((hg, cw, width), wide)],
        compiler_params=SMALL,
    )(*near_core(attention), *near_core(flat(wout_table)))

    if by_dp:
        own_dp = lax.axis_index("dp")
        mine = summed[0].astype(jnp.float32)
        for m in range(1, hg):
            got = lax.ppermute(summed[m], "dp", [(z, z ^ m) for z in range(dp)])
            mine = mine + got.astype(jnp.float32)
        mine = mine.astype(bf16)
        pieces = []
        for m in range(dp):
            pairs = [
                (z * n + s, (z ^ m) * n + (s ^ (z * tg))) for z in range(dp) for s in range(n)
            ]
            pieces.append(lax.ppermute(mine, ("dp", "seq"), pairs))
        index = group ^ own_dp
    else:
        total = lax.psum(summed, "dp")
        pieces = over_groups([total[k] for k in range(hg)])
        index = group
    columns = []
    for p in range(hg):
        piece = pieces[0]
        for m in range(1, hg):
            piece = jnp.where((index ^ p) == m, pieces[m], piece)
        columns.append(piece)
    return (layer_rows, jnp.concatenate(columns, axis=1).astype(jnp.float32))


def solution(mesh):
    placed = (
        P("dp", "seq", None),
        P("dp", "seq", None),
        P("dp", "seq", None),
        P("dp"),
        P("seq", None),
        P("seq", None),
        P("seq", None),
        P("seq", None),
    )
    return jax.shard_map(
        local,
        mesh=mesh,
        in_specs=placed,
        out_specs=(P("dp", "seq", None), P("seq", None)),
        check_vma=False,
    )
```

```python
import functools
import math

import jax
import jax.numpy as jnp
from jax import lax
from jax.experimental import pallas as pl
from jax.experimental.pallas import tpu as pltpu
from jax.sharding import PartitionSpec as P


HEADS = 12
NEG_BIG = -1e30
LOG2E = 1.4426950408889634


SMALL = pltpu.CompilerParams(vmem_limit_bytes=16 * 1024 * 1024)
VM = pl.BlockSpec(memory_space=pltpu.VMEM)
ANY = pl.BlockSpec(memory_space=pl.ANY)
SM = pl.BlockSpec(memory_space=pltpu.SMEM)


def dot_last(a, b):
    return lax.dot_general(a, b, (((1,), (1,)), ((), ())), preferred_element_type=jnp.float32)


def dot(a, b):
    return lax.dot_general(a, b, (((1,), (0,)), ((), ())), preferred_element_type=jnp.float32)


def pack_kernel(hg, tg, wr, cw, count, wq, wk, wv, seg, cot, wout, *outs):
    group = lax.axis_index("seq") // tg
    rows = cot.shape[0]
    merged = outs[hg]
    for k in range(hg):
        for part in range(hg):

            @pl.when((group ^ k) == part)
            def _():
                cols = slice(part * cw, (part + 1) * cw)
                outs[k][0, :wr] = wq[:, cols]
                outs[k][1, :wr] = wk[:, cols]
                outs[k][2, :wr] = wv[:, cols]

        for i in range(3):
            outs[k][i, wr:] = jnp.broadcast_to(seg[...], (8, cw)).astype(jnp.bfloat16)
    position = lax.axis_index("seq") * rows + lax.broadcasted_iota(jnp.int32, cot.shape, 0)
    masked = jnp.where(position < count[0], cot[...].astype(jnp.float32), 0.0)
    merged[:rows, :] = masked.astype(jnp.bfloat16)
    if merged.shape[0] > rows:
        merged[rows:, :] = wout[...]


def place_rows(scratch, pieces, member, wr):
    for tau, piece in enumerate(pieces):
        to = pl.multiple_of((member ^ tau) * wr, wr)
        last = piece.shape[0]
        scratch[pl.ds(to, wr), :] = piece[last - wr : last, :].astype(scratch.dtype)
    return scratch[...].astype(jnp.bfloat16)


def proj_kernel(hg, tg, wr, *refs):
    n = hg * tg
    attention, pieces, out, wout = refs[:hg], refs[hg : hg + n], refs[hg + n], refs[hg + n + 1]
    member = lax.axis_index("seq") % tg
    total = None
    for k in range(hg):
        block = place_rows(wout.at[k], pieces[k::hg], member, wr)
        term = dot(attention[k][...], block)
        total = term if total is None else total + term
    out[0] = total.astype(jnp.bfloat16)


def attention_kernel(hg, tg, parts, rows, wr, head_dim, resident, count, *refs):
    n = hg * tg
    refs = list(refs)
    tiles = [[refs.pop(0) for _ in range(parts)] for _ in range(n)]
    packed = [refs.pop(0) for _ in range(n)]
    o_out = [refs.pop(0) for _ in range(hg)]
    scaled_out, p_out = refs.pop(0), refs.pop(0)
    if resident:
        p_s, t_s = p_out, refs.pop(0)
    else:
        p_s, t_s = refs.pop(0), refs.pop(0)
    if not resident:
        wp_s = refs.pop(0)
    w_s, seg_s, col_s, q_s, k_s, v_s, bias_s, o_s, sems = refs
    cw = q_s.shape[1]
    own = lax.axis_index("seq")
    group = own // tg
    member = own % tg
    keys = n * rows
    heads = cw // head_dim
    size = rows // parts
    if not resident:
        packed_copies = [
            pltpu.make_async_copy(packed[r], wp_s.at[r], sems.at[n * parts + r]) for r in range(n)
        ]
        tile_copies = [
            pltpu.make_async_copy(
                tiles[r][i], t_s.at[pl.ds(r * rows + i * size, size), :], sems.at[r * parts + i]
            )
            for r in range(n)
            for i in range(parts)
        ]
        for copy in packed_copies + tile_copies:
            copy.start()
    for tau in range(tg):
        for k in range(hg):
            r = tau * hg + k
            piece = packed[r]
            if not resident:
                packed_copies[r].wait()
                piece = wp_s.at[r]
            source = (group ^ k) * tg + (member ^ tau)
            to = pl.multiple_of(source * wr, wr)
            for i in range(3):
                w_s[i, pl.ds(to, wr), :] = piece[i, :wr].astype(w_s.dtype)
            line = piece[0, wr : wr + 8, :].astype(jnp.float32)[:1]
            at = source * rows + lax.broadcasted_iota(jnp.int32, (1, rows), 1)
            columns = slice(r * rows, (r + 1) * rows)
            seg_s[0:1, columns] = line
            seg_s[1:2, columns] = jnp.where(at < count[0], line, -1.0)
    for r in range(n):
        for i in range(parts):
            if resident:
                t_s[r * rows + i * size : r * rows + (i + 1) * size, :] = tiles[r][i][...]
            else:
                tile_copies[r * parts + i].wait()
    for tau in range(tg):
        at = slice(tau * hg * rows, (tau + 1) * hg * rows)
        block = t_s[at, :]
        if tau == 0:
            q_s[at, :] = dot(block, w_s[0].astype(jnp.bfloat16)).astype(jnp.bfloat16)
        k_s[at, :] = dot(block, w_s[1].astype(jnp.bfloat16)).astype(jnp.bfloat16)
        v_s[at, :] = dot(block, w_s[2].astype(jnp.bfloat16)).astype(jnp.bfloat16)
    scale = head_dim ** (-0.5) * LOG2E
    lane_head = lax.broadcasted_iota(jnp.int32, (rows, cw), 1) // head_dim
    label = seg_s[1:2, :]
    square_row = lax.broadcasted_iota(jnp.int32, (rows, rows), 0)
    square_col = lax.broadcasted_iota(jnp.int32, (rows, rows), 1)
    column = lax.broadcasted_iota(jnp.int32, (1, keys), 1)
    row_at = lax.broadcasted_iota(jnp.int32, (rows, keys), 0)
    col_at = lax.broadcasted_iota(jnp.int32, (rows, keys), 1)
    slots = p_s.shape[0]

    def p_copy(k):
        slot = k % slots
        return pltpu.make_async_copy(p_s.at[slot], p_out.at[k], sems.at[n * parts + n + slot])

    def chunk(k, carry):
        start = k * rows if isinstance(k, int) else pl.multiple_of(k * rows, rows)
        at = pl.ds(start, rows)
        slot = k % slots
        segment = col_s[k]
        in_block = (column >= start) & (column < start + rows) & (label >= 0.0)
        same_value = jnp.where(in_block, 1.0, 0.0)
        other_value = jnp.where(in_block, 0.0, NEG_BIG)
        bias = jnp.where(segment == label, same_value, other_value)
        bias_s[...] = jnp.where(row_at + start == col_at, 1.0, bias)
        q = q_s[at, :]
        scaled = jnp.zeros((rows, cw), jnp.float32)
        if slots < hg:

            @pl.when(k >= slots)
            def _():
                p_copy(k - slots).wait()

        for h in range(heads):
            qh = jnp.where(lane_head == h, q, jnp.zeros_like(q))
            s = dot_last(qh, k_s[...]) * scale + bias_s[...]
            top = jnp.max(s, axis=1, keepdims=True)
            p = jnp.exp2(s - top)
            total = jnp.sum(p, axis=1, keepdims=True)
            p_s[slot, h] = p.astype(jnp.bfloat16)
            scaled = jnp.where(lane_head == h, 1.0 / total, scaled)
        if not resident:
            p_copy(k).start()
        acc = jnp.zeros((rows, cw), jnp.float32)
        for h in range(heads):
            acc = jnp.where(lane_head == h, dot(p_s[slot, h], v_s[...]), acc)
        scaled_out[at, :] = scaled
        o_s[at, :] = (acc * scaled).astype(jnp.bfloat16)
        return carry

    for k in range(hg):
        line = jnp.where(square_row == square_col, seg_s[0:1, k * rows : (k + 1) * rows], 0.0)
        col_s[k] = jnp.sum(line, axis=1, keepdims=True)
    if slots == hg:
        for k in range(hg):
            chunk(k, 0)
    else:
        lax.fori_loop(0, hg, chunk, 0)
    for k in range(hg):
        o_out[k][...] = o_s[k * rows : (k + 1) * rows, :]
    for k in range(hg - slots, hg):
        if not resident:
            p_copy(k).wait()


def fits(keys):
    return keys <= 2048


def attention_call(hg, tg, parts, rows, width, wr, cw, head_dim):
    n = hg * tg
    keys = n * rows
    heads = cw // head_dim
    bf16 = jnp.bfloat16
    wide = bf16 if wr % 16 == 0 else jnp.float32
    resident = fits(keys)
    own = pltpu.VMEM if resident else jax.ShapeDtypeStruct
    if resident:
        kept = [pltpu.VMEM((hg, heads, rows, keys), bf16), pltpu.VMEM((keys, width), bf16)]
        local = []
    else:
        kept = [jax.ShapeDtypeStruct((hg, heads, rows, keys), bf16)]
        local = [
            pltpu.VMEM((1, heads, rows, keys), bf16),
            pltpu.VMEM((keys, width), bf16),
            pltpu.VMEM((n, 3, wr + 8, cw), bf16),
        ]
    return pl.pallas_call(
        functools.partial(attention_kernel, hg, tg, parts, rows, wr, head_dim, resident),
        out_shape=[own((rows, cw), bf16)] * hg + [own((hg * rows, cw), jnp.float32)] + kept,
        in_specs=[SM] + [VM if resident else ANY] * (n * parts + n),
        out_specs=[VM] * (hg + 1) + [VM if resident else ANY] * len(kept),
        scratch_shapes=local
        + [
            pltpu.VMEM((3, width, cw), wide),
            pltpu.VMEM((8, keys), jnp.float32),
            pltpu.VMEM((hg, rows, 1), jnp.float32),
            pltpu.VMEM((hg * rows, cw), bf16),
            pltpu.VMEM((keys, cw), bf16),
            pltpu.VMEM((keys, cw), bf16),
            pltpu.VMEM((rows, keys), jnp.float32),
            pltpu.VMEM((hg * rows, cw), bf16),
            pltpu.SemaphoreType.DMA((n * parts + n + hg,)),
        ],
        compiler_params=pltpu.CompilerParams(vmem_limit_bytes=(30 if resident else 60) * 1024 * 1024),
    )


def gradient_kernel(hg, tg, parts, rows, wr, head_dim, by_dp, resident, *refs):
    n = hg * tg
    refs = list(refs)
    if resident:
        p_s, t_s = refs.pop(0), refs.pop(0)
    else:
        tiles = [[refs.pop(0) for _ in range(parts)] for _ in range(n)]
        p_in = refs.pop(0)
    cots = [refs.pop(0) for _ in range(hg)]
    wout_pieces = [refs.pop(0) for _ in range(tg)]
    scaled_in = refs.pop(0)
    g_out = [refs.pop(0) for _ in range(tg)]
    if not resident:
        p_s, t_s = refs.pop(0), refs.pop(0)
    wout_s, gt_s, grad_s, sems = refs
    cw = wout_s.shape[0]
    own = lax.axis_index("seq")
    group = own // tg
    member = own % tg
    heads = cw // head_dim
    size = rows // parts
    slots = p_s.shape[0]
    p_copies, tile_copies = [], []
    if not resident:
        p_copies = [
            pltpu.make_async_copy(
                p_in.at[k], p_s.at[k % slots], sems.at[n * parts + k % slots]
            )
            for k in range(hg)
        ]
        tile_copies = [
            pltpu.make_async_copy(
                tiles[r][i], t_s.at[pl.ds(r * rows + i * size, size), :], sems.at[r * parts + i]
            )
            for r in range(n)
            for i in range(parts)
        ]
    for copy in p_copies[:slots] + tile_copies:
        copy.start()
    wout = place_rows(wout_s, wout_pieces, member, wr)
    for k in range(hg):
        dout = dot_last(cots[k][:rows, :], wout).astype(jnp.bfloat16)
        scaled = scaled_in[k * rows : (k + 1) * rows, :]
        d = (dout.astype(jnp.float32) * scaled).T.astype(jnp.bfloat16)
        if not resident:
            p_copies[k].wait()
        for h in range(heads):
            at = slice(h * head_dim, (h + 1) * head_dim)
            term = dot(d[at, :], p_s[k % slots, h])
            gt_s[at, :] = term if k == 0 else gt_s[at, :] + term
        if k + slots < hg:
            p_copies[k + slots].start()
    for copy in tile_copies:
        copy.wait()
    grad_s[...] = dot(gt_s[...].astype(jnp.bfloat16), t_s[...]).T
    first = lax.axis_index("dp") if by_dp else 0
    for tau in range(tg):
        for m in range(hg):
            to = ((group ^ m ^ first) * tg + (member ^ tau)) * wr
            to = pl.multiple_of(to, wr)
            g_out[tau][m] = grad_s[pl.ds(to, wr), :].astype(jnp.bfloat16)


def gradient_call(hg, tg, parts, rows, width, wr, cw, head_dim, by_dp):
    n = hg * tg
    keys = n * rows
    heads = cw // head_dim
    bf16 = jnp.bfloat16
    wide = bf16 if wr % 16 == 0 else jnp.float32
    resident = fits(keys)
    local = []
    if not resident:
        local = [pltpu.VMEM((1, heads, rows, keys), bf16), pltpu.VMEM((keys, width), bf16)]
    return pl.pallas_call(
        functools.partial(gradient_kernel, hg, tg, parts, rows, wr, head_dim, by_dp, resident),
        out_shape=[jax.ShapeDtypeStruct((hg, wr, cw), bf16)] * tg,
        in_specs=([VM] * 2 if resident else [ANY] * (n * parts + 1))
        + [VM] * (hg + tg + 1),
        out_specs=[VM] * tg,
        scratch_shapes=local
        + [
            pltpu.VMEM((cw, width), wide),
            pltpu.VMEM((cw, keys), jnp.float32),
            pltpu.VMEM((width, cw), jnp.float32),
            pltpu.SemaphoreType.DMA((n * parts + hg,)),
        ],
        compiler_params=pltpu.CompilerParams(vmem_limit_bytes=(30 if resident else 60) * 1024 * 1024),
    )


def local(tiles, cotangent, segment_of, tissue_count, w_query, w_key, w_value, w_out):
    rows, width = tiles.shape[1:]
    wr = w_query.shape[0]
    n = lax.axis_size("seq")
    dp = lax.axis_size("dp")
    hg = math.gcd(HEADS, n)
    tg = n // hg
    cw = width // hg
    head_dim = width // HEADS
    by_dp = dp == hg
    own = lax.axis_index("seq")
    group = own // tg
    bf16 = jnp.bfloat16

    def hop(x, step):
        return lax.ppermute(x, "seq", [(s, s ^ step) for s in range(n)])

    def over_groups(pieces):
        return [pieces[0]] + [hop(pieces[k], k * tg) for k in range(1, hg)]

    def over_members(pieces):
        return [pieces] + [[hop(x, tau) for x in pieces] for tau in range(1, tg)]

    def flat(table):
        return [table[tau][k] for tau in range(tg) for k in range(hg)]

    wide = bf16 if wr % 16 == 0 else jnp.float32
    parts = 2 if hg == 4 and rows % 32 == 0 else 1
    segment_line = segment_of.reshape(1, rows)
    joined = fits(n * rows)
    own_shape = pltpu.VMEM if joined else jax.ShapeDtypeStruct
    *packed, merged = pl.pallas_call(
        functools.partial(pack_kernel, hg, tg, wr, cw),
        out_shape=[own_shape((3, wr + 8, cw), bf16)]
        + [jax.ShapeDtypeStruct((3, wr + 8, cw), bf16)] * (hg - 1)
        + [own_shape((rows + wr if joined else rows, width), bf16)],
        in_specs=[SM] + [VM] * 6,
        out_specs=[VM] * (hg + 1),
    )(tissue_count, w_query, w_key, w_value, segment_line, cotangent[0], w_out)
    weight_table = over_members(over_groups(packed))
    if parts == 2:
        half = rows // 2
        upper, lower = tiles[0, :half], tiles[0, half:]
        first = [hop(upper, tg), hop(lower, tg)]
        second = [hop(upper, 2 * tg), hop(lower, 2 * tg)]
        third = [hop(first[0], 2 * tg), hop(second[1], tg)]
        tile_pieces = [[upper, lower], first, second, third]
    else:
        tile_pieces = [[x] for x in over_groups([tiles[0]] * hg)]
    tile_pieces = tile_pieces + [
        [hop(x, tau) for x in piece]
        for tau in range(1, tg)
        for piece in tile_pieces
    ]
    flat_tiles = [x for piece in tile_pieces for x in piece]
    cots = over_groups([merged] * hg)
    if joined:
        wout_table = over_members(cots)
    else:
        wout_table = over_members(over_groups([w_out] * hg))

    def near_core(arrays):
        if not fits(n * rows):
            return arrays
        return [pltpu.with_memory_space_constraint(x, pltpu.VMEM) for x in arrays]

    results = attention_call(hg, tg, parts, rows, width, wr, cw, head_dim)(
        tissue_count, *near_core(flat_tiles), *near_core(flat(weight_table))
    )
    attention, scaled, kept = results[:hg], results[hg], results[hg + 1 :]
    if not fits(n * rows):
        kept = [*flat_tiles, *kept]
    attention = over_groups(attention)
    grads = gradient_call(hg, tg, parts, rows, width, wr, cw, head_dim, by_dp)(
        *near_core(kept),
        *near_core(cots),
        *near_core([line[0] for line in wout_table]),
        *near_core([scaled]),
    )
    summed = grads[0].astype(jnp.float32)
    for tau in range(1, tg):
        summed = summed + hop(grads[tau], tau).astype(jnp.float32)
    summed = summed.astype(bf16)

    layer_rows = pl.pallas_call(
        functools.partial(proj_kernel, hg, tg, wr),
        out_shape=jax.ShapeDtypeStruct((1, rows, width), bf16),
        in_specs=[VM] * (hg + n),
        out_specs=VM,
        scratch_shapes=[pltpu.VMEM((hg, cw, width), wide)],
        compiler_params=SMALL,
    )(*near_core(attention), *near_core(flat(wout_table)))

    if by_dp:
        own_dp = lax.axis_index("dp")
        mine = summed[0].astype(jnp.float32)
        for m in range(1, hg):
            got = lax.ppermute(summed[m], "dp", [(z, z ^ m) for z in range(dp)])
            mine = mine + got.astype(jnp.float32)
        mine = mine.astype(bf16)
        pieces = []
        for m in range(dp):
            pairs = [
                (z * n + s, (z ^ m) * n + (s ^ (z * tg))) for z in range(dp) for s in range(n)
            ]
            pieces.append(lax.ppermute(mine, ("dp", "seq"), pairs))
        index = group ^ own_dp
    else:
        total = lax.psum(summed, "dp")
        pieces = over_groups([total[k] for k in range(hg)])
        index = group
    columns = []
    for p in range(hg):
        piece = pieces[0]
        for m in range(1, hg):
            piece = jnp.where((index ^ p) == m, pieces[m], piece)
        columns.append(piece)
    return (layer_rows, jnp.concatenate(columns, axis=1).astype(jnp.float32))


def solution(mesh):
    placed = (
        P("dp", "seq", None),
        P("dp", "seq", None),
        P("dp", "seq", None),
        P("dp"),
        P("seq", None),
        P("seq", None),
        P("seq", None),
        P("seq", None),
    )
    return jax.shard_map(
        local,
        mesh=mesh,
        in_specs=placed,
        out_specs=(P("dp", "seq", None), P("seq", None)),
        check_vma=False,
    )
```

```python
import functools
import math

import jax
import jax.numpy as jnp
from jax import lax
from jax.experimental import pallas as pl
from jax.experimental.pallas import tpu as pltpu
from jax.sharding import PartitionSpec as P


HEADS = 12
NEG_BIG = -1e30
LOG2E = 1.4426950408889634


SMALL = pltpu.CompilerParams(vmem_limit_bytes=16 * 1024 * 1024)
VM = pl.BlockSpec(memory_space=pltpu.VMEM)
ANY = pl.BlockSpec(memory_space=pl.ANY)
SM = pl.BlockSpec(memory_space=pltpu.SMEM)


def dot_last(a, b):
    return lax.dot_general(a, b, (((1,), (1,)), ((), ())), preferred_element_type=jnp.float32)


def dot(a, b):
    return lax.dot_general(a, b, (((1,), (0,)), ((), ())), preferred_element_type=jnp.float32)


def pack_kernel(hg, tg, wr, cw, count, wq, wk, wv, seg, cot, wout, *outs):
    group = lax.axis_index("seq") // tg
    rows = cot.shape[0]
    for k in range(hg):
        for part in range(hg):

            @pl.when((group ^ k) == part)
            def _():
                cols = slice(part * cw, (part + 1) * cw)
                outs[k][0, :wr] = wq[:, cols]
                outs[k][1, :wr] = wk[:, cols]
                outs[k][2, :wr] = wv[:, cols]

        for i in range(3):
            outs[k][i, wr:] = jnp.broadcast_to(seg[...], (8, cw)).astype(jnp.bfloat16)
    position = lax.axis_index("seq") * rows + lax.broadcasted_iota(jnp.int32, cot.shape, 0)
    masked = jnp.where(position < count[0], cot[...].astype(jnp.float32), 0.0)
    outs[hg][...] = masked.astype(jnp.bfloat16)
    outs[hg + 1][...] = wout[...]


def column_kernel(hg, tg, cw, by_dp, *refs):
    pieces, out = refs[:hg], refs[hg]
    index = lax.axis_index("seq") // tg
    if by_dp:
        index = index ^ lax.axis_index("dp")
    for part in range(hg):
        for m in range(hg):

            @pl.when((index ^ part) == m)
            def _():
                out[:, part * cw : (part + 1) * cw] = pieces[m][...].astype(jnp.float32)


def place_rows(scratch, pieces, member, wr):
    for tau, piece in enumerate(pieces):
        to = pl.multiple_of((member ^ tau) * wr, wr)
        last = piece.shape[0]
        scratch[pl.ds(to, wr), :] = piece[last - wr : last, :].astype(scratch.dtype)
    return scratch[...].astype(jnp.bfloat16)


def proj_kernel(hg, tg, wr, *refs):
    n = hg * tg
    attention, pieces, out, wout = refs[:hg], refs[hg : hg + n], refs[hg + n], refs[hg + n + 1]
    member = lax.axis_index("seq") % tg
    total = None
    for k in range(hg):
        block = place_rows(wout.at[k], pieces[k::hg], member, wr)
        term = dot(attention[k][...], block)
        total = term if total is None else total + term
    out[0] = total.astype(jnp.bfloat16)


def attention_kernel(hg, tg, parts, rows, wr, head_dim, resident, count, *refs):
    n = hg * tg
    refs = list(refs)
    tiles = [[refs.pop(0) for _ in range(parts)] for _ in range(n)]
    packed = [refs.pop(0) for _ in range(n)]
    o_out = [refs.pop(0) for _ in range(hg)]
    scaled_out, p_out = refs.pop(0), refs.pop(0)
    if resident:
        p_s, t_s = p_out, refs.pop(0)
    else:
        p_s, t_s = refs.pop(0), refs.pop(0)
    if not resident:
        wp_s = refs.pop(0)
    w_s, seg_s, col_s, q_s, k_s, v_s, bias_s, o_s, sems = refs
    cw = q_s.shape[1]
    own = lax.axis_index("seq")
    group = own // tg
    member = own % tg
    keys = n * rows
    heads = cw // head_dim
    size = rows // parts
    if not resident:
        packed_copies = [
            pltpu.make_async_copy(packed[r], wp_s.at[r], sems.at[n * parts + r]) for r in range(n)
        ]
        tile_copies = [
            pltpu.make_async_copy(
                tiles[r][i], t_s.at[pl.ds(r * rows + i * size, size), :], sems.at[r * parts + i]
            )
            for r in range(n)
            for i in range(parts)
        ]
        for copy in packed_copies + tile_copies:
            copy.start()
    for tau in range(tg):
        for k in range(hg):
            r = tau * hg + k
            piece = packed[r]
            if not resident:
                packed_copies[r].wait()
                piece = wp_s.at[r]
            source = (group ^ k) * tg + (member ^ tau)
            to = pl.multiple_of(source * wr, wr)
            for i in range(3):
                w_s[i, pl.ds(to, wr), :] = piece[i, :wr].astype(w_s.dtype)
            line = piece[0, wr : wr + 8, :].astype(jnp.float32)[:1]
            at = source * rows + lax.broadcasted_iota(jnp.int32, (1, rows), 1)
            columns = slice(r * rows, (r + 1) * rows)
            seg_s[0:1, columns] = line
            seg_s[1:2, columns] = jnp.where(at < count[0], line, -1.0)
    for r in range(n):
        for i in range(parts):
            if resident:
                t_s[r * rows + i * size : r * rows + (i + 1) * size, :] = tiles[r][i][...]
            else:
                tile_copies[r * parts + i].wait()
    for tau in range(tg):
        at = slice(tau * hg * rows, (tau + 1) * hg * rows)
        block = t_s[at, :]
        if tau == 0:
            q_s[at, :] = dot(block, w_s[0].astype(jnp.bfloat16)).astype(jnp.bfloat16)
        k_s[at, :] = dot(block, w_s[1].astype(jnp.bfloat16)).astype(jnp.bfloat16)
        v_s[at, :] = dot(block, w_s[2].astype(jnp.bfloat16)).astype(jnp.bfloat16)
    scale = head_dim ** (-0.5) * LOG2E
    lane_head = lax.broadcasted_iota(jnp.int32, (rows, cw), 1) // head_dim
    label = seg_s[1:2, :]
    square_row = lax.broadcasted_iota(jnp.int32, (rows, rows), 0)
    square_col = lax.broadcasted_iota(jnp.int32, (rows, rows), 1)
    column = lax.broadcasted_iota(jnp.int32, (1, keys), 1)
    row_at = lax.broadcasted_iota(jnp.int32, (rows, keys), 0)
    col_at = lax.broadcasted_iota(jnp.int32, (rows, keys), 1)
    slots = p_s.shape[0]

    def p_copy(k):
        slot = k % slots
        return pltpu.make_async_copy(p_s.at[slot], p_out.at[k], sems.at[n * parts + n + slot])

    def chunk(k, carry):
        start = k * rows if isinstance(k, int) else pl.multiple_of(k * rows, rows)
        at = pl.ds(start, rows)
        slot = k % slots
        segment = col_s[k]
        in_block = (column >= start) & (column < start + rows) & (label >= 0.0)
        same_value = jnp.where(in_block, 1.0, 0.0)
        other_value = jnp.where(in_block, 0.0, NEG_BIG)
        bias = jnp.where(segment == label, same_value, other_value)
        bias_s[...] = jnp.where(row_at + start == col_at, 1.0, bias)
        q = q_s[at, :]
        scaled = jnp.zeros((rows, cw), jnp.float32)
        if slots < hg:

            @pl.when(k >= slots)
            def _():
                p_copy(k - slots).wait()

        for h in range(heads):
            qh = jnp.where(lane_head == h, q, jnp.zeros_like(q))
            s = dot_last(qh, k_s[...]) * scale + bias_s[...]
            top = jnp.max(s, axis=1, keepdims=True)
            p = jnp.exp2(s - top)
            total = jnp.sum(p, axis=1, keepdims=True)
            p_s[slot, h] = p.astype(jnp.bfloat16)
            scaled = jnp.where(lane_head == h, 1.0 / total, scaled)
        if not resident:
            p_copy(k).start()
        acc = jnp.zeros((rows, cw), jnp.float32)
        for h in range(heads):
            acc = jnp.where(lane_head == h, dot(p_s[slot, h], v_s[...]), acc)
        scaled_out[at, :] = scaled
        o_s[at, :] = (acc * scaled).astype(jnp.bfloat16)
        return carry

    for k in range(hg):
        line = jnp.where(square_row == square_col, seg_s[0:1, k * rows : (k + 1) * rows], 0.0)
        col_s[k] = jnp.sum(line, axis=1, keepdims=True)
    if slots == hg:
        for k in range(hg):
            chunk(k, 0)
    else:
        lax.fori_loop(0, hg, chunk, 0)
    for k in range(hg):
        o_out[k][...] = o_s[k * rows : (k + 1) * rows, :]
    for k in range(hg - slots, hg):
        if not resident:
            p_copy(k).wait()


def fits(keys):
    return keys <= 2048


def attention_call(hg, tg, parts, rows, width, wr, cw, head_dim):
    n = hg * tg
    keys = n * rows
    heads = cw // head_dim
    bf16 = jnp.bfloat16
    wide = bf16 if wr % 16 == 0 else jnp.float32
    resident = fits(keys)
    own = pltpu.VMEM if resident else jax.ShapeDtypeStruct
    if resident:
        kept = [pltpu.VMEM((hg, heads, rows, keys), bf16), pltpu.VMEM((keys, width), bf16)]
        local = []
    else:
        kept = [jax.ShapeDtypeStruct((hg, heads, rows, keys), bf16)]
        local = [
            pltpu.VMEM((1, heads, rows, keys), bf16),
            pltpu.VMEM((keys, width), bf16),
            pltpu.VMEM((n, 3, wr + 8, cw), bf16),
        ]
    return pl.pallas_call(
        functools.partial(attention_kernel, hg, tg, parts, rows, wr, head_dim, resident),
        out_shape=[own((rows, cw), bf16)] * hg + [own((hg * rows, cw), jnp.float32)] + kept,
        in_specs=[SM] + [VM if resident else ANY] * (n * parts + n),
        out_specs=[VM] * (hg + 1) + [VM if resident else ANY] * len(kept),
        scratch_shapes=local
        + [
            pltpu.VMEM((3, width, cw), wide),
            pltpu.VMEM((8, keys), jnp.float32),
            pltpu.VMEM((hg, rows, 1), jnp.float32),
            pltpu.VMEM((hg * rows, cw), bf16),
            pltpu.VMEM((keys, cw), bf16),
            pltpu.VMEM((keys, cw), bf16),
            pltpu.VMEM((rows, keys), jnp.float32),
            pltpu.VMEM((hg * rows, cw), bf16),
            pltpu.SemaphoreType.DMA((n * parts + n + hg,)),
        ],
        compiler_params=pltpu.CompilerParams(vmem_limit_bytes=(30 if resident else 60) * 1024 * 1024),
    )


def gradient_kernel(hg, tg, parts, rows, wr, head_dim, by_dp, resident, *refs):
    n = hg * tg
    refs = list(refs)
    if resident:
        p_s, t_s = refs.pop(0), refs.pop(0)
    else:
        tiles = [[refs.pop(0) for _ in range(parts)] for _ in range(n)]
        p_in = refs.pop(0)
    cots = [refs.pop(0) for _ in range(hg)]
    wout_pieces = [refs.pop(0) for _ in range(tg)]
    scaled_in = refs.pop(0)
    g_out = [refs.pop(0) for _ in range(tg)]
    if not resident:
        p_s, t_s = refs.pop(0), refs.pop(0)
    wout_s, gt_s, grad_s, sems = refs
    cw = wout_s.shape[0]
    own = lax.axis_index("seq")
    group = own // tg
    member = own % tg
    heads = cw // head_dim
    size = rows // parts
    slots = p_s.shape[0]
    p_copies, tile_copies = [], []
    if not resident:
        p_copies = [
            pltpu.make_async_copy(
                p_in.at[k], p_s.at[k % slots], sems.at[n * parts + k % slots]
            )
            for k in range(hg)
        ]
        tile_copies = [
            pltpu.make_async_copy(
                tiles[r][i], t_s.at[pl.ds(r * rows + i * size, size), :], sems.at[r * parts + i]
            )
            for r in range(n)
            for i in range(parts)
        ]
    for copy in p_copies[:slots] + tile_copies:
        copy.start()
    wout = place_rows(wout_s, wout_pieces, member, wr)
    for k in range(hg):
        dout = dot_last(cots[k][:rows, :], wout).astype(jnp.bfloat16)
        scaled = scaled_in[k * rows : (k + 1) * rows, :]
        d = (dout.astype(jnp.float32) * scaled).T.astype(jnp.bfloat16)
        if not resident:
            p_copies[k].wait()
        for h in range(heads):
            at = slice(h * head_dim, (h + 1) * head_dim)
            term = dot(d[at, :], p_s[k % slots, h])
            gt_s[at, :] = term if k == 0 else gt_s[at, :] + term
        if k + slots < hg:
            p_copies[k + slots].start()
    for copy in tile_copies:
        copy.wait()
    grad_s[...] = dot(gt_s[...].astype(jnp.bfloat16), t_s[...]).T
    first = lax.axis_index("dp") if by_dp else 0
    for tau in range(tg):
        for m in range(hg):
            to = ((group ^ m ^ first) * tg + (member ^ tau)) * wr
            to = pl.multiple_of(to, wr)
            g_out[tau][m] = grad_s[pl.ds(to, wr), :].astype(jnp.bfloat16)


def gradient_call(hg, tg, parts, rows, width, wr, cw, head_dim, by_dp):
    n = hg * tg
    keys = n * rows
    heads = cw // head_dim
    bf16 = jnp.bfloat16
    wide = bf16 if wr % 16 == 0 else jnp.float32
    resident = fits(keys)
    local = []
    if not resident:
        local = [pltpu.VMEM((1, heads, rows, keys), bf16), pltpu.VMEM((keys, width), bf16)]
    return pl.pallas_call(
        functools.partial(gradient_kernel, hg, tg, parts, rows, wr, head_dim, by_dp, resident),
        out_shape=[jax.ShapeDtypeStruct((hg, wr, cw), bf16)] * tg,
        in_specs=([VM] * 2 if resident else [ANY] * (n * parts + 1))
        + [VM] * (hg + tg + 1),
        out_specs=[VM] * tg,
        scratch_shapes=local
        + [
            pltpu.VMEM((cw, width), wide),
            pltpu.VMEM((cw, keys), jnp.float32),
            pltpu.VMEM((width, cw), jnp.float32),
            pltpu.SemaphoreType.DMA((n * parts + hg,)),
        ],
        compiler_params=pltpu.CompilerParams(vmem_limit_bytes=(30 if resident else 60) * 1024 * 1024),
    )


def local(tiles, cotangent, segment_of, tissue_count, w_query, w_key, w_value, w_out):
    rows, width = tiles.shape[1:]
    wr = w_query.shape[0]
    n = lax.axis_size("seq")
    dp = lax.axis_size("dp")
    hg = math.gcd(HEADS, n)
    tg = n // hg
    cw = width // hg
    head_dim = width // HEADS
    by_dp = dp == hg
    bf16 = jnp.bfloat16

    def hop(x, step):
        return lax.ppermute(x, "seq", [(s, s ^ step) for s in range(n)])

    def over_groups(pieces):
        return [pieces[0]] + [hop(pieces[k], k * tg) for k in range(1, hg)]

    def over_members(pieces):
        return [pieces] + [[hop(x, tau) for x in pieces] for tau in range(1, tg)]

    def flat(table):
        return [table[tau][k] for tau in range(tg) for k in range(hg)]

    wide = bf16 if wr % 16 == 0 else jnp.float32
    parts = 2 if hg == 4 and rows % 32 == 0 else 1
    segment_line = segment_of.reshape(1, rows)
    own_shape = pltpu.VMEM if fits(n * rows) else jax.ShapeDtypeStruct
    *packed, own_cot, own_wout = pl.pallas_call(
        functools.partial(pack_kernel, hg, tg, wr, cw),
        out_shape=[own_shape((3, wr + 8, cw), bf16)]
        + [jax.ShapeDtypeStruct((3, wr + 8, cw), bf16)] * (hg - 1)
        + [own_shape((rows, width), bf16), own_shape((wr, width), bf16)],
        in_specs=[SM] + [VM] * 6,
        out_specs=[VM] * (hg + 2),
    )(tissue_count, w_query, w_key, w_value, segment_line, cotangent[0], w_out)
    weight_table = over_members(over_groups(packed))
    if parts == 2:
        half = rows // 2
        upper, lower = tiles[0, :half], tiles[0, half:]
        first = [hop(upper, tg), hop(lower, tg)]
        second = [hop(upper, 2 * tg), hop(lower, 2 * tg)]
        third = [hop(first[0], 2 * tg), hop(second[1], tg)]
        tile_pieces = [[upper, lower], first, second, third]
    else:
        tile_pieces = [[x] for x in over_groups([tiles[0]] * hg)]
    tile_pieces = tile_pieces + [
        [hop(x, tau) for x in piece]
        for tau in range(1, tg)
        for piece in tile_pieces
    ]
    flat_tiles = [x for piece in tile_pieces for x in piece]
    cots = over_groups([own_cot] * hg)
    wout_table = over_members(over_groups([own_wout] + [w_out] * (hg - 1)))

    def near_core(arrays):
        if not fits(n * rows):
            return arrays
        return [pltpu.with_memory_space_constraint(x, pltpu.VMEM) for x in arrays]

    results = attention_call(hg, tg, parts, rows, width, wr, cw, head_dim)(
        tissue_count, *near_core(flat_tiles), *near_core(flat(weight_table))
    )
    attention, scaled, kept = results[:hg], results[hg], results[hg + 1 :]
    if not fits(n * rows):
        kept = [*flat_tiles, *kept]
    attention = over_groups(attention)
    grads = gradient_call(hg, tg, parts, rows, width, wr, cw, head_dim, by_dp)(
        *near_core(kept),
        *near_core(cots),
        *near_core([line[0] for line in wout_table]),
        *near_core([scaled]),
    )
    summed = grads[0].astype(jnp.float32)
    for tau in range(1, tg):
        summed = summed + hop(grads[tau], tau).astype(jnp.float32)
    summed = summed.astype(bf16)

    layer_rows = pl.pallas_call(
        functools.partial(proj_kernel, hg, tg, wr),
        out_shape=jax.ShapeDtypeStruct((1, rows, width), bf16),
        in_specs=[VM] * (hg + n),
        out_specs=VM,
        scratch_shapes=[pltpu.VMEM((hg, cw, width), wide)],
        compiler_params=SMALL,
    )(*near_core(attention), *near_core(flat(wout_table)))

    if by_dp:
        mine = summed[0].astype(jnp.float32)
        for m in range(1, hg):
            got = lax.ppermute(summed[m], "dp", [(z, z ^ m) for z in range(dp)])
            mine = mine + got.astype(jnp.float32)
        mine = mine.astype(bf16)
        pieces = []
        for m in range(dp):
            pairs = [
                (z * n + s, (z ^ m) * n + (s ^ (z * tg))) for z in range(dp) for s in range(n)
            ]
            pieces.append(lax.ppermute(mine, ("dp", "seq"), pairs))
    else:
        total = lax.psum(summed, "dp")
        pieces = over_groups([total[k] for k in range(hg)])
    grad = pl.pallas_call(
        functools.partial(column_kernel, hg, tg, cw, by_dp),
        out_shape=jax.ShapeDtypeStruct((wr, width), jnp.float32),
        in_specs=[VM] * hg,
        out_specs=VM,
        compiler_params=SMALL,
    )(*near_core(pieces))
    return (layer_rows, grad)


def solution(mesh):
    placed = (
        P("dp", "seq", None),
        P("dp", "seq", None),
        P("dp", "seq", None),
        P("dp"),
        P("seq", None),
        P("seq", None),
        P("seq", None),
        P("seq", None),
    )
    return jax.shard_map(
        local,
        mesh=mesh,
        in_specs=placed,
        out_specs=(P("dp", "seq", None), P("seq", None)),
        check_vma=False,
    )
```

```python
import functools
import math

import jax
import jax.numpy as jnp
from jax import lax
from jax.experimental import pallas as pl
from jax.experimental.pallas import tpu as pltpu
from jax.sharding import PartitionSpec as P


HEADS = 12
NEG_BIG = -1e30
LOG2E = 1.4426950408889634


SMALL = pltpu.CompilerParams(vmem_limit_bytes=16 * 1024 * 1024)
VM = pl.BlockSpec(memory_space=pltpu.VMEM)
ANY = pl.BlockSpec(memory_space=pl.ANY)
SM = pl.BlockSpec(memory_space=pltpu.SMEM)


def dot_last(a, b):
    return lax.dot_general(a, b, (((1,), (1,)), ((), ())), preferred_element_type=jnp.float32)


def dot(a, b):
    return lax.dot_general(a, b, (((1,), (0,)), ((), ())), preferred_element_type=jnp.float32)


def pack_kernel(hg, tg, wr, cw, count, wq, wk, wv, seg, cot, wout, *outs):
    group = lax.axis_index("seq") // tg
    rows = cot.shape[0]
    for k in range(hg):
        for part in range(hg):

            @pl.when((group ^ k) == part)
            def _():
                cols = slice(part * cw, (part + 1) * cw)
                outs[k][0, :wr] = wq[:, cols]
                outs[k][1, :wr] = wk[:, cols]
                outs[k][2, :wr] = wv[:, cols]

        for i in range(3):
            outs[k][i, wr:] = jnp.broadcast_to(seg[...], (8, cw)).astype(jnp.bfloat16)
    position = lax.axis_index("seq") * rows + lax.broadcasted_iota(jnp.int32, cot.shape, 0)
    masked = jnp.where(position < count[0], cot[...].astype(jnp.float32), 0.0)
    outs[hg][...] = masked.astype(jnp.bfloat16)
    outs[hg + 1][...] = wout[...]


def column_kernel(hg, tg, cw, by_dp, *refs):
    pieces, out = refs[:hg], refs[hg]
    index = lax.axis_index("seq") // tg
    if by_dp:
        index = index ^ lax.axis_index("dp")
    for part in range(hg):
        for m in range(hg):

            @pl.when((index ^ part) == m)
            def _():
                out[:, part * cw : (part + 1) * cw] = pieces[m][...].astype(jnp.float32)


def place_rows(scratch, pieces, member, wr):
    for tau, piece in enumerate(pieces):
        to = pl.multiple_of((member ^ tau) * wr, wr)
        last = piece.shape[0]
        scratch[pl.ds(to, wr), :] = piece[last - wr : last, :].astype(scratch.dtype)
    return scratch[...].astype(jnp.bfloat16)


def proj_kernel(hg, tg, wr, *refs):
    n = hg * tg
    attention, pieces, out, wout = refs[:hg], refs[hg : hg + n], refs[hg + n], refs[hg + n + 1]
    member = lax.axis_index("seq") % tg
    total = None
    for k in range(hg):
        block = place_rows(wout.at[k], pieces[k::hg], member, wr)
        term = dot(attention[k][...], block)
        total = term if total is None else total + term
    out[0] = total.astype(jnp.bfloat16)


def attention_kernel(hg, tg, counts, rows, wr, head_dim, resident, count, *refs):
    n = hg * tg
    refs = list(refs)
    tiles = [[refs.pop(0) for _ in range(counts[r])] for r in range(n)]
    packed = [refs.pop(0) for _ in range(n)]
    o_out = [refs.pop(0) for _ in range(hg)]
    scaled_out, p_out = refs.pop(0), refs.pop(0)
    if resident:
        p_s, t_s = p_out, refs.pop(0)
    else:
        p_s, t_s = refs.pop(0), refs.pop(0)
    if not resident:
        wp_s = refs.pop(0)
    w_s, seg_s, col_s, q_s, k_s, v_s, bias_s, o_s, sems = refs
    cw = q_s.shape[1]
    own = lax.axis_index("seq")
    group = own // tg
    member = own % tg
    keys = n * rows
    heads = cw // head_dim
    if not resident:
        packed_copies = [
            pltpu.make_async_copy(packed[r], wp_s.at[r], sems.at[n + r]) for r in range(n)
        ]
        tile_copies = [
            pltpu.make_async_copy(tiles[r][0], t_s.at[pl.ds(r * rows, rows), :], sems.at[r])
            for r in range(n)
        ]
        for copy in packed_copies + tile_copies:
            copy.start()
    else:
        own_tile = pltpu.make_async_copy(tiles[0][0], t_s.at[pl.ds(0, rows), :], sems.at[0])
        own_tile.start()
    for tau in range(tg):
        for k in range(hg):
            r = tau * hg + k
            piece = packed[r]
            if not resident:
                packed_copies[r].wait()
                piece = wp_s.at[r]
            source = (group ^ k) * tg + (member ^ tau)
            to = pl.multiple_of(source * wr, wr)
            for i in range(3):
                w_s[i, pl.ds(to, wr), :] = piece[i, :wr].astype(w_s.dtype)
            line = piece[0, wr : wr + 8, :].astype(jnp.float32)[:1]
            at = source * rows + lax.broadcasted_iota(jnp.int32, (1, rows), 1)
            columns = slice(r * rows, (r + 1) * rows)
            seg_s[0:1, columns] = line
            seg_s[1:2, columns] = jnp.where(at < count[0], line, -1.0)
    for r in range(n):
        if not resident:
            tile_copies[r].wait()
        elif r == 0:
            own_tile.wait()
        elif len(tiles[r]) == 1:
            t_s[r * rows : (r + 1) * rows, :] = tiles[r][0][...]
        else:
            parity = (member ^ (r // hg)) % 2
            for i in range(2):

                @pl.when(parity == i)
                def _():
                    t_s[r * rows : (r + 1) * rows, :] = tiles[r][i][...]

    for tau in range(tg):
        at = slice(tau * hg * rows, (tau + 1) * hg * rows)
        block = t_s[at, :]
        if tau == 0:
            q_s[at, :] = dot(block, w_s[0].astype(jnp.bfloat16)).astype(jnp.bfloat16)
        k_s[at, :] = dot(block, w_s[1].astype(jnp.bfloat16)).astype(jnp.bfloat16)
        v_s[at, :] = dot(block, w_s[2].astype(jnp.bfloat16)).astype(jnp.bfloat16)
    scale = head_dim ** (-0.5) * LOG2E
    lane_head = lax.broadcasted_iota(jnp.int32, (rows, cw), 1) // head_dim
    label = seg_s[1:2, :]
    square_row = lax.broadcasted_iota(jnp.int32, (rows, rows), 0)
    square_col = lax.broadcasted_iota(jnp.int32, (rows, rows), 1)
    column = lax.broadcasted_iota(jnp.int32, (1, keys), 1)
    row_at = lax.broadcasted_iota(jnp.int32, (rows, keys), 0)
    col_at = lax.broadcasted_iota(jnp.int32, (rows, keys), 1)
    slots = p_s.shape[0]

    def p_copy(k):
        slot = k % slots
        return pltpu.make_async_copy(p_s.at[slot], p_out.at[k], sems.at[2 * n + slot])

    def chunk(k, carry):
        start = k * rows if isinstance(k, int) else pl.multiple_of(k * rows, rows)
        at = pl.ds(start, rows)
        slot = k % slots
        segment = col_s[k]
        in_block = (column >= start) & (column < start + rows) & (label >= 0.0)
        same_value = jnp.where(in_block, 1.0, 0.0)
        other_value = jnp.where(in_block, 0.0, NEG_BIG)
        bias = jnp.where(segment == label, same_value, other_value)
        bias_s[...] = jnp.where(row_at + start == col_at, 1.0, bias)
        q = q_s[at, :]
        scaled = jnp.zeros((rows, cw), jnp.float32)
        if slots < hg:

            @pl.when(k >= slots)
            def _():
                p_copy(k - slots).wait()

        for h in range(heads):
            qh = jnp.where(lane_head == h, q, jnp.zeros_like(q))
            s = dot_last(qh, k_s[...]) * scale + bias_s[...]
            top = jnp.max(s, axis=1, keepdims=True)
            p = jnp.exp2(s - top)
            total = jnp.sum(p, axis=1, keepdims=True)
            p_s[slot, h] = p.astype(jnp.bfloat16)
            scaled = jnp.where(lane_head == h, 1.0 / total, scaled)
        if not resident:
            p_copy(k).start()
        acc = jnp.zeros((rows, cw), jnp.float32)
        for h in range(heads):
            acc = jnp.where(lane_head == h, dot(p_s[slot, h], v_s[...]), acc)
        scaled_out[at, :] = scaled
        o_s[at, :] = (acc * scaled).astype(jnp.bfloat16)
        return carry

    for k in range(hg):
        line = jnp.where(square_row == square_col, seg_s[0:1, k * rows : (k + 1) * rows], 0.0)
        col_s[k] = jnp.sum(line, axis=1, keepdims=True)
    if slots == hg:
        for k in range(hg):
            chunk(k, 0)
    else:
        lax.fori_loop(0, hg, chunk, 0)
    for k in range(hg):
        o_out[k][...] = o_s[k * rows : (k + 1) * rows, :]
    for k in range(hg - slots, hg):
        if not resident:
            p_copy(k).wait()


def fits(keys):
    return keys <= 2048


def attention_call(hg, tg, counts, rows, width, wr, cw, head_dim):
    n = hg * tg
    keys = n * rows
    heads = cw // head_dim
    bf16 = jnp.bfloat16
    wide = bf16 if wr % 16 == 0 else jnp.float32
    resident = fits(keys)
    own = pltpu.VMEM if resident else jax.ShapeDtypeStruct
    if resident:
        kept = [pltpu.VMEM((hg, heads, rows, keys), bf16), pltpu.VMEM((keys, width), bf16)]
        local = []
    else:
        kept = [jax.ShapeDtypeStruct((hg, heads, rows, keys), bf16)]
        local = [
            pltpu.VMEM((1, heads, rows, keys), bf16),
            pltpu.VMEM((keys, width), bf16),
            pltpu.VMEM((n, 3, wr + 8, cw), bf16),
        ]
    return pl.pallas_call(
        functools.partial(attention_kernel, hg, tg, counts, rows, wr, head_dim, resident),
        out_shape=[own((rows, cw), bf16)] * hg + [own((hg * rows, cw), jnp.float32)] + kept,
        in_specs=[SM, ANY] + [VM if resident else ANY] * (sum(counts) + n - 1),
        out_specs=[VM] * (hg + 1) + [VM if resident else ANY] * len(kept),
        scratch_shapes=local
        + [
            pltpu.VMEM((3, width, cw), wide),
            pltpu.VMEM((8, keys), jnp.float32),
            pltpu.VMEM((hg, rows, 1), jnp.float32),
            pltpu.VMEM((hg * rows, cw), bf16),
            pltpu.VMEM((keys, cw), bf16),
            pltpu.VMEM((keys, cw), bf16),
            pltpu.VMEM((rows, keys), jnp.float32),
            pltpu.VMEM((hg * rows, cw), bf16),
            pltpu.SemaphoreType.DMA((2 * n + hg,)),
        ],
        compiler_params=pltpu.CompilerParams(vmem_limit_bytes=(30 if resident else 60) * 1024 * 1024),
    )


def gradient_kernel(hg, tg, rows, wr, head_dim, by_dp, resident, *refs):
    n = hg * tg
    refs = list(refs)
    if resident:
        p_s, t_s = refs.pop(0), refs.pop(0)
    else:
        tiles = [refs.pop(0) for _ in range(n)]
        p_in = refs.pop(0)
    cots = [refs.pop(0) for _ in range(hg)]
    wout_pieces = [refs.pop(0) for _ in range(tg)]
    scaled_in = refs.pop(0)
    g_out = [refs.pop(0) for _ in range(tg)]
    if not resident:
        p_s, t_s = refs.pop(0), refs.pop(0)
    wout_s, gt_s, grad_s, sems = refs
    cw = wout_s.shape[0]
    own = lax.axis_index("seq")
    group = own // tg
    member = own % tg
    heads = cw // head_dim
    slots = p_s.shape[0]
    p_copies, tile_copies = [], []
    if not resident:
        p_copies = [
            pltpu.make_async_copy(
                p_in.at[k], p_s.at[k % slots], sems.at[n + k % slots]
            )
            for k in range(hg)
        ]
        tile_copies = [
            pltpu.make_async_copy(tiles[r], t_s.at[pl.ds(r * rows, rows), :], sems.at[r])
            for r in range(n)
        ]
    for copy in p_copies[:slots] + tile_copies:
        copy.start()
    wout = place_rows(wout_s, wout_pieces, member, wr)
    for k in range(hg):
        dout = dot_last(cots[k][:rows, :], wout).astype(jnp.bfloat16)
        scaled = scaled_in[k * rows : (k + 1) * rows, :]
        d = (dout.astype(jnp.float32) * scaled).T.astype(jnp.bfloat16)
        if not resident:
            p_copies[k].wait()
        for h in range(heads):
            at = slice(h * head_dim, (h + 1) * head_dim)
            term = dot(d[at, :], p_s[k % slots, h])
            gt_s[at, :] = term if k == 0 else gt_s[at, :] + term
        if k + slots < hg:
            p_copies[k + slots].start()
    for copy in tile_copies:
        copy.wait()
    grad_s[...] = dot(gt_s[...].astype(jnp.bfloat16), t_s[...]).T
    first = lax.axis_index("dp") if by_dp else 0
    for tau in range(tg):
        for m in range(hg):
            to = ((group ^ m ^ first) * tg + (member ^ tau)) * wr
            to = pl.multiple_of(to, wr)
            g_out[tau][m] = grad_s[pl.ds(to, wr), :].astype(jnp.bfloat16)


def gradient_call(hg, tg, rows, width, wr, cw, head_dim, by_dp):
    n = hg * tg
    keys = n * rows
    heads = cw // head_dim
    bf16 = jnp.bfloat16
    wide = bf16 if wr % 16 == 0 else jnp.float32
    resident = fits(keys)
    local = []
    if not resident:
        local = [pltpu.VMEM((1, heads, rows, keys), bf16), pltpu.VMEM((keys, width), bf16)]
    return pl.pallas_call(
        functools.partial(gradient_kernel, hg, tg, rows, wr, head_dim, by_dp, resident),
        out_shape=[jax.ShapeDtypeStruct((hg, wr, cw), bf16)] * tg,
        in_specs=([VM] * 2 if resident else [ANY] * (n + 1))
        + [VM] * (hg + tg + 1),
        out_specs=[VM] * tg,
        scratch_shapes=local
        + [
            pltpu.VMEM((cw, width), wide),
            pltpu.VMEM((cw, keys), jnp.float32),
            pltpu.VMEM((width, cw), jnp.float32),
            pltpu.SemaphoreType.DMA((n + hg,)),
        ],
        compiler_params=pltpu.CompilerParams(vmem_limit_bytes=(30 if resident else 60) * 1024 * 1024),
    )


def local(tiles, cotangent, segment_of, tissue_count, w_query, w_key, w_value, w_out):
    rows, width = tiles.shape[1:]
    wr = w_query.shape[0]
    n = lax.axis_size("seq")
    dp = lax.axis_size("dp")
    hg = math.gcd(HEADS, n)
    tg = n // hg
    cw = width // hg
    head_dim = width // HEADS
    by_dp = dp == hg
    bf16 = jnp.bfloat16

    def hop(x, step, senders=(0, 1)):
        pairs = [(s, s ^ step) for s in range(n) if s % tg % 2 in senders]
        return lax.ppermute(x, "seq", pairs)

    def over_groups(pieces):
        return [pieces[0]] + [hop(pieces[k], k * tg) for k in range(1, hg)]

    def over_members(pieces):
        return [pieces] + [[hop(x, tau) for x in pieces] for tau in range(1, tg)]

    def flat(table):
        return [table[tau][k] for tau in range(tg) for k in range(hg)]

    wide = bf16 if wr % 16 == 0 else jnp.float32
    relayed = hg == 4 and tg % 2 == 0 and fits(n * rows)
    segment_line = segment_of.reshape(1, rows)
    own_shape = pltpu.VMEM if fits(n * rows) else jax.ShapeDtypeStruct
    *packed, own_cot, own_wout = pl.pallas_call(
        functools.partial(pack_kernel, hg, tg, wr, cw),
        out_shape=[own_shape((3, wr + 8, cw), bf16)]
        + [jax.ShapeDtypeStruct((3, wr + 8, cw), bf16)] * (hg - 1)
        + [own_shape((rows, width), bf16), own_shape((wr, width), bf16)],
        in_specs=[SM] + [VM] * 6,
        out_specs=[VM] * (hg + 2),
    )(tissue_count, w_query, w_key, w_value, segment_line, cotangent[0], w_out)
    weight_table = over_members(over_groups(packed))
    if relayed:
        first, second = hop(tiles[0], tg), hop(tiles[0], 2 * tg)
        third = [hop(first, 2 * tg, (0,)), hop(second, tg, (1,))]
        tile_pieces = [[tiles[0]], [first], [second], third]
    else:
        tile_pieces = [[x] for x in over_groups([tiles[0]] * hg)]
    tile_pieces = tile_pieces + [
        [hop(x, tau, (0, 1) if len(piece) == 1 else (i,)) for i, x in enumerate(piece)]
        for tau in range(1, tg)
        for piece in tile_pieces
    ]
    counts = [len(piece) for piece in tile_pieces]
    flat_tiles = [x for piece in tile_pieces for x in piece]
    cots = over_groups([own_cot] * hg)
    wout_table = over_members(over_groups([own_wout] + [w_out] * (hg - 1)))

    def near_core(arrays):
        if not fits(n * rows):
            return arrays
        return [pltpu.with_memory_space_constraint(x, pltpu.VMEM) for x in arrays]

    far_tile = pltpu.with_memory_space_constraint(flat_tiles[0], pltpu.HBM)
    results = attention_call(hg, tg, counts, rows, width, wr, cw, head_dim)(
        tissue_count, far_tile, *near_core(flat_tiles[1:]), *near_core(flat(weight_table))
    )
    attention, scaled, kept = results[:hg], results[hg], results[hg + 1 :]
    if not fits(n * rows):
        kept = [*flat_tiles, *kept]
    attention = over_groups(attention)
    grads = gradient_call(hg, tg, rows, width, wr, cw, head_dim, by_dp)(
        *near_core(kept),
        *near_core(cots),
        *near_core([line[0] for line in wout_table]),
        *near_core([scaled]),
    )
    summed = grads[0].astype(jnp.float32)
    for tau in range(1, tg):
        summed = summed + hop(grads[tau], tau).astype(jnp.float32)
    summed = summed.astype(bf16)

    layer_rows = pl.pallas_call(
        functools.partial(proj_kernel, hg, tg, wr),
        out_shape=jax.ShapeDtypeStruct((1, rows, width), bf16),
        in_specs=[VM] * (hg + n),
        out_specs=VM,
        scratch_shapes=[pltpu.VMEM((hg, cw, width), wide)],
        compiler_params=SMALL,
    )(*near_core(attention), *near_core(flat(wout_table)))

    if by_dp:
        mine = summed[0].astype(jnp.float32)
        for m in range(1, hg):
            got = lax.ppermute(summed[m], "dp", [(z, z ^ m) for z in range(dp)])
            mine = mine + got.astype(jnp.float32)
        mine = mine.astype(bf16)
        pieces = []
        for m in range(dp):
            pairs = [
                (z * n + s, (z ^ m) * n + (s ^ (z * tg))) for z in range(dp) for s in range(n)
            ]
            pieces.append(lax.ppermute(mine, ("dp", "seq"), pairs))
    else:
        total = lax.psum(summed, "dp")
        pieces = over_groups([total[k] for k in range(hg)])
    grad = pl.pallas_call(
        functools.partial(column_kernel, hg, tg, cw, by_dp),
        out_shape=jax.ShapeDtypeStruct((wr, width), jnp.float32),
        in_specs=[VM] * hg,
        out_specs=VM,
        compiler_params=SMALL,
    )(*near_core(pieces))
    return (layer_rows, grad)


def solution(mesh):
    placed = (
        P("dp", "seq", None),
        P("dp", "seq", None),
        P("dp", "seq", None),
        P("dp"),
        P("seq", None),
        P("seq", None),
        P("seq", None),
        P("seq", None),
    )
    return jax.shard_map(
        local,
        mesh=mesh,
        in_specs=placed,
        out_specs=(P("dp", "seq", None), P("seq", None)),
        check_vma=False,
    )
```

```python
import functools
import math

import jax
import jax.numpy as jnp
from jax import lax
from jax.experimental import pallas as pl
from jax.experimental.pallas import tpu as pltpu
from jax.sharding import PartitionSpec as P


HEADS = 12
NEG_BIG = -1e30
LOG2E = 1.4426950408889634


SMALL = pltpu.CompilerParams(vmem_limit_bytes=16 * 1024 * 1024)
VM = pl.BlockSpec(memory_space=pltpu.VMEM)
ANY = pl.BlockSpec(memory_space=pl.ANY)
SM = pl.BlockSpec(memory_space=pltpu.SMEM)


def dot_last(a, b):
    return lax.dot_general(a, b, (((1,), (1,)), ((), ())), preferred_element_type=jnp.float32)


def dot(a, b):
    return lax.dot_general(a, b, (((1,), (0,)), ((), ())), preferred_element_type=jnp.float32)


def pack_kernel(hg, tg, wr, cw, count, wq, wk, wv, seg, cot, wout, *outs):
    group = lax.axis_index("seq") // tg
    rows = cot.shape[0]
    for k in range(hg):
        for part in range(hg):

            @pl.when((group ^ k) == part)
            def _():
                cols = slice(part * cw, (part + 1) * cw)
                outs[k][0, :wr] = wq[:, cols]
                outs[k][1, :wr] = wk[:, cols]
                outs[k][2, :wr] = wv[:, cols]

        for i in range(3):
            outs[k][i, wr:] = jnp.broadcast_to(seg[...], (8, cw)).astype(jnp.bfloat16)
    position = lax.axis_index("seq") * rows + lax.broadcasted_iota(jnp.int32, cot.shape, 0)
    masked = jnp.where(position < count[0], cot[...].astype(jnp.float32), 0.0)
    outs[hg][...] = masked.astype(jnp.bfloat16)
    outs[hg + 1][...] = wout[...]


def column_kernel(hg, tg, cw, by_dp, *refs):
    pieces, out = refs[:hg], refs[hg]
    index = lax.axis_index("seq") // tg
    if by_dp:
        index = index ^ lax.axis_index("dp")
    for part in range(hg):
        for m in range(hg):

            @pl.when((index ^ part) == m)
            def _():
                out[:, part * cw : (part + 1) * cw] = pieces[m][...].astype(jnp.float32)


def place_rows(scratch, pieces, member, wr):
    for tau, piece in enumerate(pieces):
        to = pl.multiple_of((member ^ tau) * wr, wr)
        last = piece.shape[0]
        scratch[pl.ds(to, wr), :] = piece[last - wr : last, :].astype(scratch.dtype)
    return scratch[...].astype(jnp.bfloat16)


def proj_kernel(hg, tg, wr, *refs):
    n = hg * tg
    attention, pieces, out, wout = refs[:hg], refs[hg : hg + n], refs[hg + n], refs[hg + n + 1]
    member = lax.axis_index("seq") % tg
    total = None
    for k in range(hg):
        block = place_rows(wout.at[k], pieces[k::hg], member, wr)
        term = dot(attention[k][...], block)
        total = term if total is None else total + term
    out[0] = total.astype(jnp.bfloat16)


def attention_kernel(hg, tg, parts, rows, wr, head_dim, resident, count, *refs):
    n = hg * tg
    refs = list(refs)
    tiles = [[refs.pop(0) for _ in range(parts)] for _ in range(n)]
    packed = [refs.pop(0) for _ in range(n)]
    o_out = [refs.pop(0) for _ in range(hg)]
    scaled_out, p_out = refs.pop(0), refs.pop(0)
    if resident:
        p_s, t_s = p_out, refs.pop(0)
    else:
        p_s, t_s = refs.pop(0), refs.pop(0)
    if not resident:
        wp_s = refs.pop(0)
    w_s, seg_s, col_s, q_s, k_s, v_s, bias_s, o_s, sems = refs
    cw = q_s.shape[1]
    own = lax.axis_index("seq")
    group = own // tg
    member = own % tg
    keys = n * rows
    heads = cw // head_dim
    size = rows // parts
    if not resident:
        packed_copies = [
            pltpu.make_async_copy(packed[r], wp_s.at[r], sems.at[n * parts + r]) for r in range(n)
        ]
        tile_copies = [
            pltpu.make_async_copy(
                tiles[r][i], t_s.at[pl.ds(r * rows + i * size, size), :], sems.at[r * parts + i]
            )
            for r in range(n)
            for i in range(parts)
        ]
        for copy in packed_copies + tile_copies:
            copy.start()
    for tau in range(tg):
        for k in range(hg):
            r = tau * hg + k
            piece = packed[r]
            if not resident:
                packed_copies[r].wait()
                piece = wp_s.at[r]
            source = (group ^ k) * tg + (member ^ tau)
            to = pl.multiple_of(source * wr, wr)
            for i in range(3):
                w_s[i, pl.ds(to, wr), :] = piece[i, :wr].astype(w_s.dtype)
            line = piece[0, wr : wr + 8, :].astype(jnp.float32)[:1]
            at = source * rows + lax.broadcasted_iota(jnp.int32, (1, rows), 1)
            columns = slice(r * rows, (r + 1) * rows)
            seg_s[0:1, columns] = line
            seg_s[1:2, columns] = jnp.where(at < count[0], line, -1.0)
    for r in range(n):
        for i in range(parts):
            if resident:
                t_s[r * rows + i * size : r * rows + (i + 1) * size, :] = tiles[r][i][...]
            else:
                tile_copies[r * parts + i].wait()
    for tau in range(tg):
        at = slice(tau * hg * rows, (tau + 1) * hg * rows)
        block = t_s[at, :]
        if tau == 0:
            q_s[at, :] = dot(block, w_s[0].astype(jnp.bfloat16)).astype(jnp.bfloat16)
        k_s[at, :] = dot(block, w_s[1].astype(jnp.bfloat16)).astype(jnp.bfloat16)
        v_s[at, :] = dot(block, w_s[2].astype(jnp.bfloat16)).astype(jnp.bfloat16)
    scale = head_dim ** (-0.5) * LOG2E
    lane_head = lax.broadcasted_iota(jnp.int32, (rows, cw), 1) // head_dim
    label = seg_s[1:2, :]
    square_row = lax.broadcasted_iota(jnp.int32, (rows, rows), 0)
    square_col = lax.broadcasted_iota(jnp.int32, (rows, rows), 1)
    column = lax.broadcasted_iota(jnp.int32, (1, keys), 1)
    row_at = lax.broadcasted_iota(jnp.int32, (rows, keys), 0)
    col_at = lax.broadcasted_iota(jnp.int32, (rows, keys), 1)
    slots = p_s.shape[0]

    def p_copy(k):
        slot = k % slots
        return pltpu.make_async_copy(p_s.at[slot], p_out.at[k], sems.at[n * parts + n + slot])

    def chunk(k, carry):
        start = k * rows if isinstance(k, int) else pl.multiple_of(k * rows, rows)
        at = pl.ds(start, rows)
        slot = k % slots
        segment = col_s[k]
        in_block = (column >= start) & (column < start + rows) & (label >= 0.0)
        same_value = jnp.where(in_block, 1.0, 0.0)
        other_value = jnp.where(in_block, 0.0, NEG_BIG)
        bias = jnp.where(segment == label, same_value, other_value)
        bias_s[...] = jnp.where(row_at + start == col_at, 1.0, bias)
        q = q_s[at, :]
        scaled = jnp.zeros((rows, cw), jnp.float32)
        if slots < hg:

            @pl.when(k >= slots)
            def _():
                p_copy(k - slots).wait()

        for h in range(heads):
            qh = jnp.where(lane_head == h, q, jnp.zeros_like(q))
            s = dot_last(qh, k_s[...]) * scale + bias_s[...]
            top = jnp.max(s, axis=1, keepdims=True)
            p = jnp.exp2(s - top)
            total = jnp.sum(p, axis=1, keepdims=True)
            p_s[slot, h] = p.astype(jnp.bfloat16)
            scaled = jnp.where(lane_head == h, 1.0 / total, scaled)
        if not resident:
            p_copy(k).start()
        acc = jnp.zeros((rows, cw), jnp.float32)
        for h in range(heads):
            acc = jnp.where(lane_head == h, dot(p_s[slot, h], v_s[...]), acc)
        scaled_out[at, :] = scaled
        o_s[at, :] = (acc * scaled).astype(jnp.bfloat16)
        return carry

    for k in range(hg):
        line = jnp.where(square_row == square_col, seg_s[0:1, k * rows : (k + 1) * rows], 0.0)
        col_s[k] = jnp.sum(line, axis=1, keepdims=True)

    def pair(k):
        both = 2 * rows
        at = slice(k * rows, k * rows + both)
        for j in (0, 1):
            start = (k + j) * rows
            in_block = (column >= start) & (column < start + rows) & (label >= 0.0)
            same_value = jnp.where(in_block, 1.0, 0.0)
            other_value = jnp.where(in_block, 0.0, NEG_BIG)
            bias = jnp.where(col_s[k + j] == label, same_value, other_value)
            bias_s[j * rows : (j + 1) * rows, :] = jnp.where(row_at + start == col_at, 1.0, bias)
        head_of = lax.broadcasted_iota(jnp.int32, (both, cw), 1) // head_dim
        q = q_s[at, :]
        scaled = jnp.zeros((both, cw), jnp.float32)
        acc = jnp.zeros((both, cw), jnp.float32)
        for h in range(heads):
            qh = jnp.where(head_of == h, q, jnp.zeros_like(q))
            s = dot_last(qh, k_s[...]) * scale + bias_s[...]
            top = jnp.max(s, axis=1, keepdims=True)
            p = jnp.exp2(s - top)
            total = jnp.sum(p, axis=1, keepdims=True)
            weight = p.astype(jnp.bfloat16)
            p_s[k, h] = weight[:rows]
            p_s[k + 1, h] = weight[rows:]
            scaled = jnp.where(head_of == h, 1.0 / total, scaled)
            acc = jnp.where(head_of == h, dot(weight, v_s[...]), acc)
        scaled_out[at, :] = scaled
        o_s[at, :] = (acc * scaled).astype(jnp.bfloat16)

    if resident and hg % 2 == 0:
        for k in range(0, hg, 2):
            pair(k)
    elif slots == hg:
        for k in range(hg):
            chunk(k, 0)
    else:
        lax.fori_loop(0, hg, chunk, 0)
    for k in range(hg):
        o_out[k][...] = o_s[k * rows : (k + 1) * rows, :]
    for k in range(hg - slots, hg):
        if not resident:
            p_copy(k).wait()


def fits(keys):
    return keys <= 2048


def attention_call(hg, tg, parts, rows, width, wr, cw, head_dim):
    n = hg * tg
    keys = n * rows
    heads = cw // head_dim
    bf16 = jnp.bfloat16
    wide = bf16 if wr % 16 == 0 else jnp.float32
    resident = fits(keys)
    own = pltpu.VMEM if resident else jax.ShapeDtypeStruct
    if resident:
        kept = [pltpu.VMEM((hg, heads, rows, keys), bf16), pltpu.VMEM((keys, width), bf16)]
        local = []
    else:
        kept = [jax.ShapeDtypeStruct((hg, heads, rows, keys), bf16)]
        local = [
            pltpu.VMEM((1, heads, rows, keys), bf16),
            pltpu.VMEM((keys, width), bf16),
            pltpu.VMEM((n, 3, wr + 8, cw), bf16),
        ]
    return pl.pallas_call(
        functools.partial(attention_kernel, hg, tg, parts, rows, wr, head_dim, resident),
        out_shape=[own((rows, cw), bf16)] * hg + [own((hg * rows, cw), jnp.float32)] + kept,
        in_specs=[SM] + [VM if resident else ANY] * (n * parts + n),
        out_specs=[VM] * (hg + 1) + [VM if resident else ANY] * len(kept),
        scratch_shapes=local
        + [
            pltpu.VMEM((3, width, cw), wide),
            pltpu.VMEM((8, keys), jnp.float32),
            pltpu.VMEM((hg, rows, 1), jnp.float32),
            pltpu.VMEM((hg * rows, cw), bf16),
            pltpu.VMEM((keys, cw), bf16),
            pltpu.VMEM((keys, cw), bf16),
            pltpu.VMEM(((2 if resident else 1) * rows, keys), jnp.float32),
            pltpu.VMEM((hg * rows, cw), bf16),
            pltpu.SemaphoreType.DMA((n * parts + n + hg,)),
        ],
        compiler_params=pltpu.CompilerParams(vmem_limit_bytes=(30 if resident else 60) * 1024 * 1024),
    )


def gradient_kernel(hg, tg, parts, rows, wr, head_dim, by_dp, resident, *refs):
    n = hg * tg
    refs = list(refs)
    if resident:
        p_s, t_s = refs.pop(0), refs.pop(0)
    else:
        tiles = [[refs.pop(0) for _ in range(parts)] for _ in range(n)]
        p_in = refs.pop(0)
    cots = [refs.pop(0) for _ in range(hg)]
    wout_pieces = [refs.pop(0) for _ in range(tg)]
    scaled_in = refs.pop(0)
    g_out = [refs.pop(0) for _ in range(tg)]
    if not resident:
        p_s, t_s = refs.pop(0), refs.pop(0)
    wout_s, gt_s, grad_s, sems = refs
    cw = wout_s.shape[0]
    own = lax.axis_index("seq")
    group = own // tg
    member = own % tg
    heads = cw // head_dim
    size = rows // parts
    slots = p_s.shape[0]
    p_copies, tile_copies = [], []
    if not resident:
        p_copies = [
            pltpu.make_async_copy(
                p_in.at[k], p_s.at[k % slots], sems.at[n * parts + k % slots]
            )
            for k in range(hg)
        ]
        tile_copies = [
            pltpu.make_async_copy(
                tiles[r][i], t_s.at[pl.ds(r * rows + i * size, size), :], sems.at[r * parts + i]
            )
            for r in range(n)
            for i in range(parts)
        ]
    for copy in p_copies[:slots] + tile_copies:
        copy.start()
    wout = place_rows(wout_s, wout_pieces, member, wr)
    for k in range(hg):
        dout = dot_last(cots[k][:rows, :], wout).astype(jnp.bfloat16)
        scaled = scaled_in[k * rows : (k + 1) * rows, :]
        d = (dout.astype(jnp.float32) * scaled).T.astype(jnp.bfloat16)
        if not resident:
            p_copies[k].wait()
        for h in range(heads):
            at = slice(h * head_dim, (h + 1) * head_dim)
            term = dot(d[at, :], p_s[k % slots, h])
            gt_s[at, :] = term if k == 0 else gt_s[at, :] + term
        if k + slots < hg:
            p_copies[k + slots].start()
    for copy in tile_copies:
        copy.wait()
    grad_s[...] = dot(gt_s[...].astype(jnp.bfloat16), t_s[...]).T
    first = lax.axis_index("dp") if by_dp else 0
    for tau in range(tg):
        for m in range(hg):
            to = ((group ^ m ^ first) * tg + (member ^ tau)) * wr
            to = pl.multiple_of(to, wr)
            g_out[tau][m] = grad_s[pl.ds(to, wr), :].astype(jnp.bfloat16)


def gradient_call(hg, tg, parts, rows, width, wr, cw, head_dim, by_dp):
    n = hg * tg
    keys = n * rows
    heads = cw // head_dim
    bf16 = jnp.bfloat16
    wide = bf16 if wr % 16 == 0 else jnp.float32
    resident = fits(keys)
    local = []
    if not resident:
        local = [pltpu.VMEM((1, heads, rows, keys), bf16), pltpu.VMEM((keys, width), bf16)]
    return pl.pallas_call(
        functools.partial(gradient_kernel, hg, tg, parts, rows, wr, head_dim, by_dp, resident),
        out_shape=[jax.ShapeDtypeStruct((hg, wr, cw), bf16)] * tg,
        in_specs=([VM] * 2 if resident else [ANY] * (n * parts + 1))
        + [VM] * (hg + tg + 1),
        out_specs=[VM] * tg,
        scratch_shapes=local
        + [
            pltpu.VMEM((cw, width), wide),
            pltpu.VMEM((cw, keys), jnp.float32),
            pltpu.VMEM((width, cw), jnp.float32),
            pltpu.SemaphoreType.DMA((n * parts + hg,)),
        ],
        compiler_params=pltpu.CompilerParams(vmem_limit_bytes=(30 if resident else 60) * 1024 * 1024),
    )


def local(tiles, cotangent, segment_of, tissue_count, w_query, w_key, w_value, w_out):
    rows, width = tiles.shape[1:]
    wr = w_query.shape[0]
    n = lax.axis_size("seq")
    dp = lax.axis_size("dp")
    hg = math.gcd(HEADS, n)
    tg = n // hg
    cw = width // hg
    head_dim = width // HEADS
    by_dp = dp == hg
    bf16 = jnp.bfloat16

    def hop(x, step):
        return lax.ppermute(x, "seq", [(s, s ^ step) for s in range(n)])

    def over_groups(pieces):
        return [pieces[0]] + [hop(pieces[k], k * tg) for k in range(1, hg)]

    def over_members(pieces):
        return [pieces] + [[hop(x, tau) for x in pieces] for tau in range(1, tg)]

    def flat(table):
        return [table[tau][k] for tau in range(tg) for k in range(hg)]

    wide = bf16 if wr % 16 == 0 else jnp.float32
    parts = 2 if hg == 4 and rows % 32 == 0 else 1
    segment_line = segment_of.reshape(1, rows)
    own_shape = pltpu.VMEM if fits(n * rows) else jax.ShapeDtypeStruct
    *packed, own_cot, own_wout = pl.pallas_call(
        functools.partial(pack_kernel, hg, tg, wr, cw),
        out_shape=[own_shape((3, wr + 8, cw), bf16)]
        + [jax.ShapeDtypeStruct((3, wr + 8, cw), bf16)] * (hg - 1)
        + [own_shape((rows, width), bf16), own_shape((wr, width), bf16)],
        in_specs=[SM] + [VM] * 6,
        out_specs=[VM] * (hg + 2),
    )(tissue_count, w_query, w_key, w_value, segment_line, cotangent[0], w_out)
    weight_table = over_members(over_groups(packed))
    if parts == 2:
        half = rows // 2
        upper, lower = tiles[0, :half], tiles[0, half:]
        first = [hop(upper, tg), hop(lower, tg)]
        second = [hop(upper, 2 * tg), hop(lower, 2 * tg)]
        third = [hop(first[0], 2 * tg), hop(second[1], tg)]
        tile_pieces = [[upper, lower], first, second, third]
    else:
        tile_pieces = [[x] for x in over_groups([tiles[0]] * hg)]
    tile_pieces = tile_pieces + [
        [hop(x, tau) for x in piece]
        for tau in range(1, tg)
        for piece in tile_pieces
    ]
    flat_tiles = [x for piece in tile_pieces for x in piece]
    cots = over_groups([own_cot] * hg)
    wout_table = over_members(over_groups([own_wout] + [w_out] * (hg - 1)))

    def near_core(arrays):
        if not fits(n * rows):
            return arrays
        return [pltpu.with_memory_space_constraint(x, pltpu.VMEM) for x in arrays]

    results = attention_call(hg, tg, parts, rows, width, wr, cw, head_dim)(
        tissue_count, *near_core(flat_tiles), *near_core(flat(weight_table))
    )
    attention, scaled, kept = results[:hg], results[hg], results[hg + 1 :]
    if not fits(n * rows):
        kept = [*flat_tiles, *kept]
    attention = over_groups(attention)
    grads = gradient_call(hg, tg, parts, rows, width, wr, cw, head_dim, by_dp)(
        *near_core(kept),
        *near_core(cots),
        *near_core([line[0] for line in wout_table]),
        *near_core([scaled]),
    )
    summed = grads[0].astype(jnp.float32)
    for tau in range(1, tg):
        summed = summed + hop(grads[tau], tau).astype(jnp.float32)
    summed = summed.astype(bf16)

    layer_rows = pl.pallas_call(
        functools.partial(proj_kernel, hg, tg, wr),
        out_shape=jax.ShapeDtypeStruct((1, rows, width), bf16),
        in_specs=[VM] * (hg + n),
        out_specs=VM,
        scratch_shapes=[pltpu.VMEM((hg, cw, width), wide)],
        compiler_params=SMALL,
    )(*near_core(attention), *near_core(flat(wout_table)))

    if by_dp:
        mine = summed[0].astype(jnp.float32)
        for m in range(1, hg):
            got = lax.ppermute(summed[m], "dp", [(z, z ^ m) for z in range(dp)])
            mine = mine + got.astype(jnp.float32)
        mine = mine.astype(bf16)
        pieces = []
        for m in range(dp):
            pairs = [
                (z * n + s, (z ^ m) * n + (s ^ (z * tg))) for z in range(dp) for s in range(n)
            ]
            pieces.append(lax.ppermute(mine, ("dp", "seq"), pairs))
    else:
        total = lax.psum(summed, "dp")
        pieces = over_groups([total[k] for k in range(hg)])
    grad = pl.pallas_call(
        functools.partial(column_kernel, hg, tg, cw, by_dp),
        out_shape=jax.ShapeDtypeStruct((wr, width), jnp.float32),
        in_specs=[VM] * hg,
        out_specs=VM,
        compiler_params=SMALL,
    )(*near_core(pieces))
    return (layer_rows, grad)


def solution(mesh):
    placed = (
        P("dp", "seq", None),
        P("dp", "seq", None),
        P("dp", "seq", None),
        P("dp"),
        P("seq", None),
        P("seq", None),
        P("seq", None),
        P("seq", None),
    )
    return jax.shard_map(
        local,
        mesh=mesh,
        in_specs=placed,
        out_specs=(P("dp", "seq", None), P("seq", None)),
        check_vma=False,
    )
```
